32 devices in a mesh: wide: 8 (over y, x, core), eight: 4 (over z).
Axes of the slice: x: 2, y: 2, z: 4, core: 2. Of those that a mesh axis runs over, the one named last changes fastest.
Arguments:
- multipliers: float32 [64, 1024, 256], P(('wide', 'eight')), may hold values from -6 to 6
- gap: float32 [64, 1024, 256], P(('wide', 'eight'))
- flexibility: bfloat16 [64, 1024, 1024], P(('wide', 'eight'))
- dirichlet: bfloat16 [64, 1024, 1024], P(('wide', 'eight'))
- side: int32 [64, 8], P(('wide', 'eight')), may hold values from 0 to 3
- powers: int32 [64], P(('wide', 'eight')), may hold values from 1 to 3, as said below
- active: int32 [3, 64, 1024], P(None, ('wide', 'eight')), may hold values 0 or 1
Outputs:
- solution: float32 [64, 1024, 256], P(('wide', 'eight'))
- steps: float32 [3, 256], replicated
- centres: float32 [3, 1024, 256], replicated
The draws below stay inside these ranges and needn't reach their ends.
Inputs may be any that keep to these rules, and one draw needn't show every extreme that they name: `powers`: some subdomain has 3 applications in every draw.
All inputs are finite; a program needn't handle non-finite values. No bound on the sum of `active` on one device may be relied on, other than what follows from the above.
Results may differ from the reference program's by a relative error of at most 0.0075.
Values may be sent and summed in bfloat16 or wider, within the bound.
No kernel may reach another device: no remote copies, remote signals or barrier semaphores. Data moves between devices by JAX's collectives and lax.ppermute only.
A program may use at most 128 MiB of HBM per device.

```python
import jax
import jax.numpy as jnp
from jax import lax

M = 1024
BLOCKS = 8
K = 256
ITERS = 3
PMAX = 3
SUBS = 64
GROUP = 8


def draw_flexibility(key, part):
    noise = jax.random.normal(key, (SUBS, M, M), jnp.float32) * (0.3 / M ** 0.5)
    return (jnp.eye(M, dtype=jnp.float32)[None] + noise).astype(jnp.bfloat16)


def draw_dirichlet(key, part):
    key = jax.random.fold_in(key, 7)
    noise = jax.random.normal(key, (SUBS, M, M), jnp.float32) * (0.3 / M ** 0.5)
    return (0.6 * jnp.eye(M, dtype=jnp.float32)[None] + noise).astype(jnp.bfloat16)


def draw_powers(key, part):
    key = jax.random.fold_in(key, 11)
    first, second = jax.random.split(key)
    rolls = jax.random.randint(first, (SUBS,), 0, 16)
    counts = jnp.where(rolls == 0, PMAX, jnp.where(rolls == 1, 2, 1))
    spot = jax.random.randint(second, (), 0, SUBS)
    return jnp.where(jnp.arange(SUBS) == spot, PMAX, counts).astype(jnp.int32)


def draw_gap(key, part):
    key = jax.random.fold_in(key, 13)
    scale = 1.0 + 2.0 * jnp.arange(SUBS, dtype=jnp.float32) / max(SUBS - 1, 1)
    values = jax.random.normal(key, (SUBS, M, K), jnp.float32)
    return values * scale[:, None, None]


def with_ends(result, own_key, low, top_value):
    shape = result.shape
    spot = [jax.random.randint(jax.random.fold_in(own_key, axis), (), 0, shape[axis]) for axis in range(len(shape))]
    result = result.at[tuple(spot)].set(low)
    longest = shape.index(max(shape))
    spot[longest] = (spot[longest] + 1) % shape[longest]
    return result.at[tuple(spot)].set(top_value)


def steps_of(key, dims, pieces, smallest, largest):
    level = 1.0
    for dim, parts in pieces:
        steps = jax.random.uniform(jax.random.fold_in(jax.random.fold_in(key, 6), dim), (parts,), jnp.float32, smallest / len(pieces), largest / len(pieces))
        level = level * jnp.repeat(jnp.exp(steps), dims[dim] // parts).reshape((-1,) + (1,) * (len(dims) - 1 - dim))
    return level


def centred(own_key, extent, spread, bound, cuts=(), held_as=jnp.bfloat16):
    level = steps_of(own_key, extent, cuts, -0.22, 0.18) if cuts else 1.0
    drawn = jax.random.normal(own_key, extent, jnp.float32) * spread * level
    return jnp.minimum(jnp.maximum(drawn, -bound), bound).astype(held_as)


def setup_inputs(seed: int = 0) -> dict:
    key_list = jax.random.split(jax.random.key(seed), 8)
    return {
        "multipliers": centred(key_list[0], (SUBS, M, K), 1.0, 6.0, ((0, 32),), jnp.float32),
        "gap": draw_gap(jax.random.fold_in(key_list[7], 71), 0),
        "flexibility": draw_flexibility(jax.random.fold_in(key_list[7], 71), 0),
        "dirichlet": draw_dirichlet(jax.random.fold_in(key_list[7], 71), 0),
        "side": with_ends(jax.random.randint(key_list[4], (SUBS, BLOCKS), 0, 4), jax.random.fold_in(key_list[4], 1), 0, 3).astype(jnp.int32),
        "powers": draw_powers(jax.random.fold_in(key_list[7], 71), 0),
        "active": with_ends((jax.random.randint(key_list[6], (ITERS, SUBS, M), 0, 2) < 1).astype(jnp.int32), jax.random.fold_in(key_list[6], 1), 0, 1),
    }


def apply_each(operators, fields):
    def one(pair):
        return jnp.dot(pair[0], pair[1], preferred_element_type=jnp.float32).astype(jnp.bfloat16)
    return lax.map(one, (operators, fields))


def group_shift(field, offset):
    grouped = field.reshape((SUBS // GROUP, GROUP) + field.shape[1:])
    zeros = jnp.zeros_like(grouped[:, :1])
    if offset > 0:
        moved = jnp.concatenate([grouped[:, 1:], zeros], axis=1)
    else:
        moved = jnp.concatenate([zeros, grouped[:, :-1]], axis=1)
    return moved.reshape(field.shape)


def reference(multipliers, gap, flexibility, dirichlet, side, powers, active):
    lam = multipliers
    side_rows = jnp.repeat(side, M // BLOCKS, axis=1)[:, :, None]
    alphas = []
    centre_list = []
    for step in range(ITERS):
        disp = apply_each(flexibility, lam.astype(jnp.bfloat16))
        next_wide = jnp.roll(disp, -GROUP, axis=0)
        prev_wide = jnp.roll(disp, GROUP, axis=0)
        next_group = group_shift(disp, 1)
        prev_group = group_shift(disp, -1)
        facing = jnp.where(side_rows == 0, next_wide,
                           jnp.where(side_rows == 1, prev_wide,
                                     jnp.where(side_rows == 2, next_group, prev_group)))
        jump = gap - (disp.astype(jnp.float32) - facing.astype(jnp.float32))
        direct = jump.astype(jnp.bfloat16)
        for level in range(PMAX):
            applied = apply_each(dirichlet, direct)
            direct = jnp.where((level < powers)[:, None, None], applied, direct)
        dfloat = direct.astype(jnp.float32)
        inner = jnp.sum(jump * dfloat, axis=(0, 1))
        square = jnp.sum(dfloat * dfloat, axis=(0, 1))
        alpha = inner / (square + 1e-6)
        trial = lam + alpha * dfloat
        centre = jnp.sum(trial, axis=0) / SUBS
        alphas.append(alpha)
        centre_list.append(centre)
        lam = trial - centre
        lam = jnp.where(active[step][:, :, None] == 1, jnp.maximum(lam, 0.0), lam)
    return lam, jnp.stack(alphas), jnp.stack(centre_list)
```

```python
import functools

import jax
import jax.numpy as jnp
from jax import lax
from jax.experimental import pallas as pl
from jax.experimental.pallas import tpu as pltpu
from jax.sharding import PartitionSpec as P

ITERS = 3
PMAX = 3
EXTRA = 16
F32 = jnp.float32
BF16 = jnp.bfloat16
VMEM = pl.BlockSpec(memory_space=pltpu.VMEM)
SMEM = pl.BlockSpec(memory_space=pltpu.SMEM)


def call(kernel, outs, n_in, n_smem, flops, nbytes, scratch=(), vmem=40):
    return pl.pallas_call(
        kernel,
        out_shape=outs,
        in_specs=[SMEM] * n_smem + [VMEM] * (n_in - n_smem),
        out_specs=[VMEM] * len(outs),
        scratch_shapes=list(scratch),
        compiler_params=pltpu.CompilerParams(vmem_limit_bytes=vmem << 20),
        cost_estimate=pl.CostEstimate(flops=flops, bytes_accessed=nbytes, transcendentals=0),
    )


def sds(shape, dtype):
    return jax.ShapeDtypeStruct(shape, dtype)


def stage_bits(size):
    total = size.bit_length() - 1
    groups = [1]
    left = total - 1
    while left > 0:
        take = 2 if left >= 2 else 1
        groups.append(take)
        left -= take
    return groups


def pack_products(inner, square):
    shape = (EXTRA, inner.shape[1])
    row = lax.broadcasted_iota(jnp.int32, shape, 0)
    ih = inner.astype(BF16).astype(F32)
    sh = square.astype(BF16).astype(F32)
    tile = jnp.where(
        row == 0,
        jnp.broadcast_to(ih, shape),
        jnp.where(
            row == 1,
            jnp.broadcast_to(inner - ih, shape),
            jnp.where(
                row == 2,
                jnp.broadcast_to(sh, shape),
                jnp.where(row == 3, jnp.broadcast_to(square - sh, shape), 0.0),
            ),
        ),
    )
    return tile.astype(BF16)


def unpack_products(tiles):
    vals = []
    for tile in tiles:
        t = tile.astype(F32)
        vals.append((t[0:1] + t[1:2], t[2:3] + t[3:4]))
    return tree([v[0] for v in vals]), tree([v[1] for v in vals])


def tree(items):
    items = list(items)
    while len(items) > 1:
        items = [items[i] + items[i + 1] for i in range(0, len(items), 2)]
    return items[0]


def first_kernel(chunk, wide, info, lam_ref, flex_ref, disp_ref, keep_ref, send_ref):
    w = info[0]
    subs = lam_ref.shape[0]
    for k in range(wide):
        rows = pl.ds(pl.multiple_of(jnp.bitwise_xor(w, k) * chunk, chunk), chunk)
        total = lam_ref[0, rows, :]
        for s in range(1, subs):
            total = total + lam_ref[s, rows, :]
        out = send_ref if k % 2 else keep_ref
        out[pl.ds((k // 2) * chunk, chunk), :] = total.astype(BF16)
    for s in range(subs):
        disp_ref[s] = jnp.dot(
            flex_ref[s], lam_ref[s].astype(BF16), preferred_element_type=F32
        ).astype(BF16)


def update_kernel(chunk, wide, last, info, *refs):
    lam_ref, dir_ref, alpha_ref, floor_ref = refs[:4]
    centre_refs = refs[4 : 4 + wide]
    refs = refs[4 + wide :]
    w = info[0]
    subs, rows_all, cols = lam_ref.shape
    if last:
        lam_out, centre_out = refs
    else:
        flex_ref, lam_out, centre_out, disp_ref, keep_ref, send_ref, half = refs
    alpha = jnp.broadcast_to(alpha_ref[0:1, :], (chunk, cols))
    for k in range(wide):
        rows = pl.ds(pl.multiple_of(jnp.bitwise_xor(w, k) * chunk, chunk), chunk)
        centre = centre_refs[k][...].astype(F32)
        centre_out[rows, :] = centre
        total = None
        for s in range(subs):
            trial = lam_ref[s, rows, :] + alpha * dir_ref[s, rows, :].astype(F32)
            low = floor_ref[s, rows, :]
            low = jnp.concatenate([low] * (cols // low.shape[1]), axis=1)
            new = jnp.maximum(trial - centre, low)
            lam_out[s, rows, :] = new
            if not last:
                half[s, rows, :] = new.astype(BF16)
                total = new if total is None else total + new
        if not last:
            out = send_ref if k % 2 else keep_ref
            out[pl.ds((k // 2) * chunk, chunk), :] = total.astype(BF16)
    if not last:
        for s in range(subs):
            disp_ref[s] = jnp.dot(
                flex_ref[s], half[s], preferred_element_type=F32
            ).astype(BF16)


def direct_kernel(chunk, wide, info, side, powers, gap_ref, disp_ref, chip_ref, off_ref, up_ref, down_ref, diri_ref, dir_ref, keep_ref, send_ref, jump, work):
    w = info[0]
    odd = jnp.bitwise_and(w, 1)
    subs, rows_all, cols = gap_ref.shape
    blocks = side.shape[1]
    height = rows_all // blocks
    inner = jnp.zeros((8, cols), F32)
    square = jnp.zeros((8, cols), F32)
    for s in range(subs):

        def block(b, carry, s=s):
            face = side[s, b]
            rows = pl.ds(pl.multiple_of(b * height, height), height)

            def put(source):
                value = gap_ref[s, rows, :] - (
                    disp_ref[s, rows, :].astype(F32) - source.astype(F32)
                )
                jump[rows, :] = value
                work[s, rows, :] = value.astype(BF16)

            onchip = face == odd
            pl.when((face < 2) & onchip)(lambda: put(chip_ref[s, rows, :]))
            pl.when((face < 2) & jnp.logical_not(onchip))(lambda: put(off_ref[s, rows, :]))
            pl.when(face == 2)(
                lambda: put(disp_ref[s + 1, rows, :] if s + 1 < subs else up_ref[rows, :])
            )
            pl.when(face == 3)(
                lambda: put(disp_ref[s - 1, rows, :] if s > 0 else down_ref[rows, :])
            )
            return carry

        lax.fori_loop(0, blocks, block, 0)

        def level(i, carry, s=s):
            work[s] = jnp.dot(
                diri_ref[s], work[s], preferred_element_type=F32
            ).astype(BF16)
            return carry

        lax.fori_loop(0, powers[s], level, 0)
        direct = work[s]
        dir_ref[s] = direct
        dfloat = direct.astype(F32)
        inner = inner + jnp.sum((jump[...] * dfloat).reshape(rows_all // 8, 8, cols), axis=0)
        square = square + jnp.sum((dfloat * dfloat).reshape(rows_all // 8, 8, cols), axis=0)
    for k in range(wide):
        rows = pl.ds(pl.multiple_of(jnp.bitwise_xor(w, k) * chunk, chunk), chunk)
        total = tree([work[s, rows, :].astype(F32) for s in range(subs)])
        out = send_ref if k % 2 else keep_ref
        out[pl.ds((k // 2) * chunk, chunk), :] = total.astype(BF16)
    tile = pack_products(
        jnp.sum(inner, axis=0, keepdims=True), jnp.sum(square, axis=0, keepdims=True)
    )
    tail = pl.ds((wide // 2) * chunk, EXTRA)
    keep_ref[tail, :] = tile
    send_ref[tail, :] = tile


def add_kernel(chunk, chunks, ways_in, ways_out, extra, *refs):
    ins, outs = refs[:ways_in], refs[ways_in:]
    for c in range(chunks):
        rows = pl.ds(c * chunk, chunk)
        total = tree([r[rows, :].astype(F32) for r in ins]).astype(BF16)
        outs[c % ways_out][pl.ds((c // ways_out) * chunk, chunk), :] = total
    if extra:
        tail = pl.ds(chunks * chunk, EXTRA)
        tile = pack_products(*unpack_products([r[tail, :] for r in ins]))
        for o in outs:
            o[pl.ds((chunks // ways_out) * chunk, EXTRA), :] = tile


def centre_kernel(chunk, ways, count, *refs):
    dirs, lams = refs[:ways], refs[ways : 2 * ways]
    centre_ref, alpha_ref = refs[2 * ways :]
    rows = pl.ds(0, chunk)
    tail = pl.ds(chunk, EXTRA)
    inner, square = unpack_products([r[tail, :] for r in dirs])
    alpha = inner / (square + 1e-06)
    alpha_ref[...] = jnp.broadcast_to(alpha, alpha_ref.shape)
    dsum = tree([r[rows, :].astype(F32) for r in dirs])
    lsum = tree([r[rows, :].astype(F32) for r in lams])
    centre_ref[...] = ((lsum + alpha * dsum) / count).astype(BF16)


def swap(x, axis, mask):
    n = lax.axis_size(axis)
    return lax.ppermute(x, axis, [(i, i ^ mask) for i in range(n)])


def scatter(keep, send, chunk, wide, extra):
    groups = stage_bits(wide)
    parts = [keep, send]
    shift, chunks = 0, wide
    cols = keep.shape[1]
    for g, bits in enumerate(groups):
        ways = 1 << bits
        got = [parts[0]] + [swap(parts[q], "wide", q << shift) for q in range(1, ways)]
        chunks //= ways
        shift += bits
        nxt = 1 << groups[g + 1] if g + 1 < len(groups) else 1
        shape = sds(((chunks // nxt) * chunk + (EXTRA if extra else 0), cols), BF16)
        parts = call(
            functools.partial(add_kernel, chunk, chunks, ways, nxt, extra),
            [shape] * nxt, ways, 0, chunks * chunk * cols * ways, chunks * chunk * cols * 2 * (ways + 1), vmem=8,
        )(*got)
    return parts[0]


def across(x):
    size = lax.axis_size("eight")
    return [x] + [swap(x, "eight", q) for q in range(1, size)]


def gather(centre, wide):
    groups = stage_bits(wide)
    have = {0: centre}
    shift = wide.bit_length() - 1
    for bits in reversed(groups):
        shift -= bits
        new = dict(have)
        for q in range(1, 1 << bits):
            for k, v in have.items():
                new[k ^ (q << shift)] = swap(v, "wide", q << shift)
        have = new
    return [have[k] for k in range(wide)]


def body(multipliers, gap, flexibility, dirichlet, side, powers, active):
    subs, rows, cols = multipliers.shape
    wide = lax.axis_size("wide")
    eight = lax.axis_size("eight")
    count = wide * eight * subs
    chunk = rows // wide
    info = jnp.stack([lax.axis_index("wide"), lax.axis_index("eight")]).astype(jnp.int32)
    lanes = 128
    floor = jnp.where(
        jnp.broadcast_to(active[..., None], active.shape + (lanes,)) == 1, 0.0, -jnp.inf
    ).astype(F32)

    full = sds((subs, rows, cols), F32)
    half = sds((subs, rows, cols), BF16)
    part = sds(((wide // 2) * chunk, cols), BF16)
    message = sds(((wide // 2) * chunk + EXTRA, cols), BF16)
    mm = 2 * subs * rows * rows * cols
    op_bytes = 2 * subs * rows * rows
    arr = subs * rows * cols

    alphas, centres = [], []
    lam = multipliers
    disp, lkeep, lsend = call(
        functools.partial(first_kernel, chunk, wide),
        [half, part, part], 3, 1, mm, op_bytes + arr * 8,
    )(info, lam, flexibility)
    for step in range(ITERS):
        chip = swap(disp, "wide", 1)
        off = lax.ppermute(
            disp, "wide",
            [(i, (i + 1) % wide if i % 2 else (i - 1) % wide) for i in range(wide)],
        )
        up = lax.ppermute(disp[0], "eight", [(i + 1, i) for i in range(eight - 1)])
        down = lax.ppermute(disp[subs - 1], "eight", [(i, i + 1) for i in range(eight - 1)])
        lam_parts = across(scatter(lkeep, lsend, chunk, wide, False))
        direct, dkeep, dsend = call(
            functools.partial(direct_kernel, chunk, wide),
            [half, message, message], 10, 3, 2 * mm, op_bytes + arr * 16,
            scratch=[pltpu.VMEM((rows, cols), F32), pltpu.VMEM((subs, rows, cols), BF16)],
        )(info, side, powers, gap, disp, chip, off, up, down, dirichlet)
        dir_parts = across(scatter(dkeep, dsend, chunk, wide, True))
        centre, alpha = call(
            functools.partial(centre_kernel, chunk, eight, float(count)),
            [sds((chunk, cols), BF16), sds((8, cols), F32)], 2 * eight, 0,
            chunk * cols * 10, chunk * cols * 20, vmem=8,
        )(*dir_parts, *lam_parts)
        pieces = gather(centre, wide)
        alphas.append(alpha[0])
        last = step == ITERS - 1
        ins = [info, lam, direct, alpha, floor[step], *pieces]
        outs = [full, sds((rows, cols), F32)]
        if last:
            lam, mean = call(
                functools.partial(update_kernel, chunk, wide, True),
                outs, len(ins), 1, arr * 6, arr * 12,
            )(*ins)
        else:
            lam, mean, disp, lkeep, lsend = call(
                functools.partial(update_kernel, chunk, wide, False),
                outs + [half, part, part], len(ins) + 1, 1, mm, op_bytes + arr * 14,
                scratch=[pltpu.VMEM((subs, rows, cols), BF16)],
            )(*ins, flexibility)
        centres.append(mean)
    return (lam, jnp.stack(alphas), jnp.stack(centres))


def solution(mesh):
    return jax.shard_map(
        body,
        mesh=mesh,
        in_specs=(
            P(("wide", "eight"), None, None),
            P(("wide", "eight"), None, None),
            P(("wide", "eight"), None, None),
            P(("wide", "eight"), None, None),
            P(("wide", "eight"), None),
            P(("wide", "eight")),
            P(None, ("wide", "eight"), None),
        ),
        out_specs=(P(("wide", "eight"), None, None), P(), P()),
        check_vma=False,
    )
```

```python
import functools

import jax
import jax.numpy as jnp
from jax import lax
from jax.experimental import pallas as pl
from jax.experimental.pallas import tpu as pltpu
from jax.sharding import PartitionSpec as P

ITERS = 3
PMAX = 3
EXTRA = 16
F32 = jnp.float32
BF16 = jnp.bfloat16
VMEM = pl.BlockSpec(memory_space=pltpu.VMEM)
ANY = pl.BlockSpec(memory_space=pl.ANY)
SMEM = pl.BlockSpec(memory_space=pltpu.SMEM)


def call(kernel, outs, n_smem, ins, flops, nbytes, scratch=(), vmem=16, anys=(), any_outs=(), aliases=None):
    return pl.pallas_call(
        kernel,
        out_shape=outs,
        in_specs=[
            SMEM if i < n_smem else ANY if i in anys else VMEM for i in range(len(ins))
        ],
        out_specs=[ANY if i in any_outs else VMEM for i in range(len(outs))],
        scratch_shapes=list(scratch),
        input_output_aliases=aliases or {},
        compiler_params=pltpu.CompilerParams(vmem_limit_bytes=vmem << 20),
        cost_estimate=pl.CostEstimate(flops=flops, bytes_accessed=nbytes, transcendentals=0),
    )(*ins)


def sds(shape, dtype):
    return jax.ShapeDtypeStruct(shape, dtype)


def stage_bits(size):
    total = size.bit_length() - 1
    groups = [1]
    left = total - 1
    while left > 0:
        take = 2 if left >= 2 else 1
        groups.append(take)
        left -= take
    return groups


def pack_products(inner, square):
    shape = (EXTRA, inner.shape[1])
    row = lax.broadcasted_iota(jnp.int32, shape, 0)
    ih = inner.astype(BF16).astype(F32)
    sh = square.astype(BF16).astype(F32)
    tile = jnp.where(
        row == 0,
        jnp.broadcast_to(ih, shape),
        jnp.where(
            row == 1,
            jnp.broadcast_to(inner - ih, shape),
            jnp.where(
                row == 2,
                jnp.broadcast_to(sh, shape),
                jnp.where(row == 3, jnp.broadcast_to(square - sh, shape), 0.0),
            ),
        ),
    )
    return tile.astype(BF16)


def unpack_products(tiles):
    vals = []
    for tile in tiles:
        t = tile.astype(F32)
        vals.append((t[0:1] + t[1:2], t[2:3] + t[3:4]))
    return tree([v[0] for v in vals]), tree([v[1] for v in vals])


def tree(items):
    items = list(items)
    while len(items) > 1:
        items = [items[i] + items[i + 1] for i in range(0, len(items), 2)]
    return items[0]


def send_partial(chunk, wide, w, part, tile, keep_ref, send_ref):
    for k in range(wide):
        total = part(pl.ds(pl.multiple_of(jnp.bitwise_xor(w, k) * chunk, chunk), chunk))
        out = send_ref if k % 2 else keep_ref
        out[pl.ds((k // 2) * chunk, chunk), :] = total.astype(BF16)
    if tile is not None:
        tail = pl.ds((wide // 2) * chunk, EXTRA)
        keep_ref[tail, :] = tile
        send_ref[tail, :] = tile


def send_halo(info, theirs, disp_ref, za_ref, zb_ref, base_ref, over_ref):
    subs, rows_all, _ = disp_ref.shape
    blocks = theirs.shape[1]
    height = rows_all // blocks
    cap = base_ref.shape[0]
    odd = jnp.bitwise_and(info[0], 1)
    zodd = jnp.bitwise_and(info[1], 1)
    za_ref[...] = disp_ref[(1 - zodd) * (subs - 1)]
    zb_ref[...] = disp_ref[zodd * (subs - 1)]
    count = jnp.int32(0)
    for s in range(subs):

        def block(b, n, s=s):
            need = theirs[s, b] == odd
            rows = pl.ds(pl.multiple_of(b * height, height), height)

            @pl.when(need & (n < cap))
            def _():
                base_ref[n] = disp_ref[s, rows, :]

            @pl.when(need & (n >= cap))
            def _():
                over_ref[n - cap] = disp_ref[s, rows, :]

            return n + need.astype(jnp.int32)

        count = lax.fori_loop(0, blocks, block, count)


def first_kernel(chunk, wide, info, theirs, side, lam_ref, flex_ref, disp_ref, za_ref, zb_ref, base_ref, over_ref, keep_ref, send_ref):
    w = info[0]
    subs, _, cols = lam_ref.shape
    mine = 1 - jnp.bitwise_and(w, 1)
    count = jnp.int32(0)
    for s in range(subs):
        for b in range(side.shape[1]):
            count = count + (side[s, b] == mine).astype(jnp.int32)
    tile = jnp.broadcast_to(count.astype(F32), (EXTRA, cols)).astype(BF16)
    for s in range(subs):
        disp_ref[s] = jnp.dot(
            flex_ref[s], lam_ref[s].astype(BF16), preferred_element_type=F32
        ).astype(BF16)
    send_halo(info, theirs, disp_ref, za_ref, zb_ref, base_ref, over_ref)
    send_partial(
        chunk, wide, w, lambda rows: tree([lam_ref[s, rows, :] for s in range(subs)]),
        tile, keep_ref, send_ref,
    )


def update_kernel(chunk, wide, step, last, *refs):
    if last:
        info, *refs = refs
    else:
        info, theirs, *refs = refs
    lam_ref, dir_ref, alpha_ref, floor_ref = refs[:4]
    centre_refs = refs[4 : 4 + wide]
    refs = refs[4 + wide :]
    if not last:
        flex_ref, *refs = refs
    if step:
        refs = refs[1:]
    if last:
        lam_out, stack_ref, mean, sem = refs
    else:
        lam_out, stack_ref, disp_ref, za_ref, zb_ref, base_ref, over_ref, keep_ref, send_ref, half, mean, sem = refs
    w = info[0]
    subs, rows_all, cols = lam_ref.shape
    alpha = jnp.broadcast_to(alpha_ref[0:1, :], (chunk, cols))
    for k in range(wide):
        rows = pl.ds(pl.multiple_of(jnp.bitwise_xor(w, k) * chunk, chunk), chunk)
        centre = centre_refs[k][...].astype(F32)
        mean[rows, :] = centre
        total = None
        for s in range(subs):
            trial = lam_ref[s, rows, :] + alpha * dir_ref[s, rows, :].astype(F32)
            low = floor_ref[s, rows, :]
            low = jnp.concatenate([low] * (cols // low.shape[1]), axis=1)
            new = jnp.maximum(trial - centre, low)
            lam_out[s, rows, :] = new
            if not last:
                half[s, rows, :] = new.astype(BF16)
                total = new if total is None else total + new
        if not last:
            out = send_ref if k % 2 else keep_ref
            out[pl.ds((k // 2) * chunk, chunk), :] = total.astype(BF16)
    copy = pltpu.make_async_copy(mean, stack_ref.at[step], sem)
    copy.start()
    if not last:
        for s in range(subs):
            disp_ref[s] = jnp.dot(
                flex_ref[s], half[s], preferred_element_type=F32
            ).astype(BF16)
        send_halo(info, theirs, disp_ref, za_ref, zb_ref, base_ref, over_ref)
    copy.wait()


def direct_kernel(chunk, wide, info, side, powers, gap_ref, disp_ref, chip_ref, base_ref, over_ref, za_ref, zb_ref, diri_ref, after_ref, dir_ref, keep_ref, send_ref, jump, work):
    w = info[0]
    odd = jnp.bitwise_and(w, 1)
    zodd = jnp.bitwise_and(info[1], 1)
    subs, rows_all, cols = gap_ref.shape
    blocks = side.shape[1]
    height = rows_all // blocks
    cap = base_ref.shape[0]
    inner = jnp.zeros((8, cols), F32)
    square = jnp.zeros((8, cols), F32)
    count = jnp.int32(0)
    for s in range(subs):

        def block(b, n, s=s):
            face = side[s, b]
            rows = pl.ds(pl.multiple_of(b * height, height), height)

            def put(source):
                value = gap_ref[s, rows, :] - (
                    disp_ref[s, rows, :].astype(F32) - source.astype(F32)
                )
                jump[rows, :] = value
                work[s, rows, :] = value.astype(BF16)

            pl.when(face == odd)(lambda: put(chip_ref[s, rows, :]))
            away = face == 1 - odd
            pl.when(away & (n < cap))(lambda: put(base_ref[n]))
            pl.when(away & (n >= cap))(lambda: put(over_ref[n - cap]))
            if s + 1 < subs:
                pl.when(face == 2)(lambda: put(disp_ref[s + 1, rows, :]))
            else:
                pl.when((face == 2) & (zodd == 0))(lambda: put(za_ref[rows, :]))
                pl.when((face == 2) & (zodd == 1))(lambda: put(zb_ref[rows, :]))
            if s > 0:
                pl.when(face == 3)(lambda: put(disp_ref[s - 1, rows, :]))
            else:
                pl.when((face == 3) & (zodd == 1))(lambda: put(za_ref[rows, :]))
                pl.when((face == 3) & (zodd == 0))(lambda: put(zb_ref[rows, :]))
            return n + away.astype(jnp.int32)

        count = lax.fori_loop(0, blocks, block, count)

        def level(i, carry, s=s):
            work[s] = jnp.dot(
                diri_ref[s], work[s], preferred_element_type=F32
            ).astype(BF16)
            return carry

        lax.fori_loop(0, powers[s], level, 0)
        direct = work[s]
        dir_ref[s] = direct
        dfloat = direct.astype(F32)
        inner = inner + jnp.sum((jump[...] * dfloat).reshape(rows_all // 8, 8, cols), axis=0)
        square = square + jnp.sum((dfloat * dfloat).reshape(rows_all // 8, 8, cols), axis=0)
    tile = pack_products(
        jnp.sum(inner, axis=0, keepdims=True), jnp.sum(square, axis=0, keepdims=True)
    )
    send_partial(
        chunk, wide, w, lambda rows: tree([work[s, rows, :].astype(F32) for s in range(subs)]),
        tile, keep_ref, send_ref,
    )


def add_kernel(chunk, chunks, ways_in, ways_out, extra, *refs):
    ins, outs = refs[:ways_in], refs[ways_in:]
    for c in range(chunks):
        rows = pl.ds(c * chunk, chunk)
        total = tree([r[rows, :].astype(F32) for r in ins]).astype(BF16)
        outs[c % ways_out][pl.ds((c // ways_out) * chunk, chunk), :] = total
    if extra:
        tail = pl.ds(chunks * chunk, EXTRA)
        tiles = [r[tail, :] for r in ins]
        if extra == "max":
            tile = functools.reduce(jnp.maximum, tiles)
        else:
            tile = pack_products(*unpack_products(tiles))
        for o in outs:
            o[pl.ds((chunks // ways_out) * chunk, EXTRA), :] = tile


def total_kernel(chunk, ways, extra, *refs):
    ins = refs[:ways]
    rows = pl.ds(0, chunk)
    refs[ways][...] = tree([r[rows, :].astype(F32) for r in ins])
    if extra:
        tiles = [r[pl.ds(chunk, EXTRA), :].astype(F32) for r in ins]
        refs[ways + 1][...] = functools.reduce(jnp.maximum, tiles)


def centre_kernel(chunk, ways, count, *refs):
    dirs, lam_ref = refs[:ways], refs[ways]
    centre_ref, alpha_ref = refs[ways + 1 :]
    rows = pl.ds(0, chunk)
    tail = pl.ds(chunk, EXTRA)
    inner, square = unpack_products([r[tail, :] for r in dirs])
    alpha = inner / (square + 1e-06)
    alpha_ref[...] = jnp.broadcast_to(alpha, alpha_ref.shape)
    dsum = tree([r[rows, :].astype(F32) for r in dirs])
    centre_ref[...] = ((lam_ref[...] + alpha * dsum) / count).astype(BF16)


def swap(x, axis, mask):
    n = lax.axis_size(axis)
    return lax.ppermute(x, axis, [(i, i ^ mask) for i in range(n)])


def scatter(keep, send, chunk, wide, extra):
    groups = stage_bits(wide)
    parts = [keep, send]
    shift, chunks = 0, wide
    cols = keep.shape[1]
    for g, bits in enumerate(groups):
        ways = 1 << bits
        got = [parts[0]] + [swap(parts[q], "wide", q << shift) for q in range(1, ways)]
        chunks //= ways
        shift += bits
        nxt = 1 << groups[g + 1] if g + 1 < len(groups) else 1
        shape = sds(((chunks // nxt) * chunk + (EXTRA if extra else 0), cols), BF16)
        parts = call(
            functools.partial(add_kernel, chunk, chunks, ways, nxt, extra),
            [shape] * nxt, 0, got, chunks * chunk * cols * ways,
            chunks * chunk * cols * 2 * (ways + 1), vmem=8,
        )
    return parts[0]


def across(x):
    size = lax.axis_size("eight")
    return [x] + [swap(x, "eight", q) for q in range(1, size)]


def gather(centre, wide):
    groups = stage_bits(wide)
    have = {0: centre}
    shift = wide.bit_length() - 1
    for bits in reversed(groups):
        shift -= bits
        new = dict(have)
        for q in range(1, 1 << bits):
            for k, v in have.items():
                new[k ^ (q << shift)] = swap(v, "wide", q << shift)
        have = new
    return [have[k] for k in range(wide)]


def body(multipliers, gap, flexibility, dirichlet, side, powers, active):
    subs, rows, cols = multipliers.shape
    blocks = side.shape[1]
    height = rows // blocks
    wide = lax.axis_size("wide")
    eight = lax.axis_size("eight")
    count = wide * eight * subs
    chunk = rows // wide
    cap = -(-subs * blocks * 9 // 16)
    away = [(i, (i + 1) % wide if i % 2 else (i - 1) % wide) for i in range(wide)]
    pairs_a = [(i, i ^ 1) for i in range(eight) if i ^ 1 < eight]
    pairs_b = [(i, i + 1 if i % 2 else i - 1) for i in range(1, eight - 1)]
    if eight % 2:
        pairs_b = [(i, i + 1 if i % 2 else i - 1) for i in range(1, eight)]
    info = jnp.stack([lax.axis_index("wide"), lax.axis_index("eight")]).astype(jnp.int32)
    theirs = lax.ppermute(side, "wide", away)
    lanes = 128
    floor = jnp.where(
        jnp.broadcast_to(active[..., None], active.shape + (lanes,)) == 1, 0.0, -jnp.inf
    ).astype(F32)

    full = sds((subs, rows, cols), F32)
    half = sds((subs, rows, cols), BF16)
    one = sds((rows, cols), BF16)
    base = sds((cap, height, cols), BF16)
    over = sds((subs * blocks - cap, height, cols), BF16)
    part = sds(((wide // 2) * chunk, cols), BF16)
    message = sds(((wide // 2) * chunk + EXTRA, cols), BF16)
    stack = sds((ITERS, rows, cols), F32)
    halo = [half, one, one, base, over]
    mm = 2 * subs * rows * rows * cols
    op_bytes = 2 * subs * rows * rows
    arr = subs * rows * cols

    alphas = []
    lam = multipliers
    disp, za, zb, blk, rest, lkeep, lsend = call(
        functools.partial(first_kernel, chunk, wide), halo + [message, message],
        3, [info, theirs, side, lam, flexibility], mm, op_bytes + arr * 8,
    )
    centres = None
    many = None
    for step in range(ITERS):
        blk = lax.ppermute(blk, "wide", away)
        za = lax.ppermute(za, "eight", pairs_a)
        zb = lax.ppermute(zb, "eight", pairs_b)
        chip = swap(disp, "wide", 1)
        extra = "max" if step == 0 else None
        lam_parts = across(scatter(lkeep, lsend, chunk, wide, extra))
        outs = [sds((chunk, cols), F32)] + ([sds((EXTRA, cols), F32)] if extra else [])
        lam_total, *most = call(
            functools.partial(total_kernel, chunk, eight, extra), outs, 0, lam_parts,
            chunk * cols * eight, chunk * cols * 12, vmem=8,
        )
        if step == 0:
            many = most[0][0, 0] > cap
        rest = lax.cond(
            many, lambda x: lax.ppermute(x, "wide", away), lambda x: jnp.zeros_like(x), rest
        )
        direct, dkeep, dsend = call(
            functools.partial(direct_kernel, chunk, wide), [half, message, message], 3,
            [info, side, powers, gap, disp, chip, blk, rest, za, zb, dirichlet, lam_total],
            2 * mm, op_bytes + arr * 16,
            scratch=[pltpu.VMEM((rows, cols), F32), pltpu.VMEM((subs, rows, cols), BF16)],
        )
        dir_parts = across(scatter(dkeep, dsend, chunk, wide, "sum"))
        centre, alpha = call(
            functools.partial(centre_kernel, chunk, eight, float(count)),
            [sds((chunk, cols), BF16), sds((8, cols), F32)], 0, dir_parts + [lam_total],
            chunk * cols * 10, chunk * cols * 20, vmem=8,
        )
        pieces = gather(centre, wide)
        alphas.append(alpha[0])
        last = step == ITERS - 1
        ins = [info] + ([] if last else [theirs])
        n_smem = len(ins)
        ins += [lam, direct, alpha, floor[step], *pieces] + ([] if last else [flexibility])
        aliases = {}
        anys = ()
        if step:
            aliases = {len(ins): 1}
            anys = (len(ins),)
            ins.append(centres)
        scratch = [pltpu.VMEM((rows, cols), F32), pltpu.SemaphoreType.DMA]
        kernel = functools.partial(update_kernel, chunk, wide, step, last)
        if last:
            lam, centres = call(
                kernel, [full, stack], n_smem, ins, arr * 6, arr * 12,
                scratch=scratch, anys=anys, any_outs=(1,), aliases=aliases,
            )
        else:
            lam, centres, disp, za, zb, blk, rest, lkeep, lsend = call(
                kernel, [full, stack] + halo + [part, part], n_smem, ins, mm, op_bytes + arr * 14,
                scratch=[pltpu.VMEM((subs, rows, cols), BF16)] + scratch,
                anys=anys, any_outs=(1,), aliases=aliases,
            )
    return (lam, jnp.stack(alphas), centres)


def solution(mesh):
    return jax.shard_map(
        body,
        mesh=mesh,
        in_specs=(
            P(("wide", "eight"), None, None),
            P(("wide", "eight"), None, None),
            P(("wide", "eight"), None, None),
            P(("wide", "eight"), None, None),
            P(("wide", "eight"), None),
            P(("wide", "eight")),
            P(None, ("wide", "eight"), None),
        ),
        out_specs=(P(("wide", "eight"), None, None), P(), P()),
        check_vma=False,
    )
```

```python
import functools

import jax
import jax.numpy as jnp
from jax import lax
from jax.experimental import pallas as pl
from jax.experimental.pallas import tpu as pltpu
from jax.sharding import PartitionSpec as P

ITERS = 3
PMAX = 3
EXTRA = 16
F32 = jnp.float32
BF16 = jnp.bfloat16
VMEM = pl.BlockSpec(memory_space=pltpu.VMEM)
ANY = pl.BlockSpec(memory_space=pl.ANY)
SMEM = pl.BlockSpec(memory_space=pltpu.SMEM)


def call(kernel, outs, n_smem, ins, flops, nbytes, scratch=(), vmem=16, anys=(), any_outs=(), aliases=None):
    return pl.pallas_call(
        kernel,
        out_shape=outs,
        in_specs=[
            SMEM if i < n_smem else ANY if i in anys else VMEM for i in range(len(ins))
        ],
        out_specs=[ANY if i in any_outs else VMEM for i in range(len(outs))],
        scratch_shapes=list(scratch),
        input_output_aliases=aliases or {},
        compiler_params=pltpu.CompilerParams(vmem_limit_bytes=vmem << 20),
        cost_estimate=pl.CostEstimate(flops=flops, bytes_accessed=nbytes, transcendentals=0),
    )(*ins)


def sds(shape, dtype):
    return jax.ShapeDtypeStruct(shape, dtype)


def stage_bits(size):
    total = size.bit_length() - 1
    groups = [1]
    left = total - 1
    while left > 0:
        take = 2 if left >= 2 else 1
        groups.append(take)
        left -= take
    return groups


def pack_products(inner, square):
    shape = (EXTRA, inner.shape[1])
    row = lax.broadcasted_iota(jnp.int32, shape, 0)
    ih = inner.astype(BF16).astype(F32)
    sh = square.astype(BF16).astype(F32)
    tile = jnp.where(
        row == 0,
        jnp.broadcast_to(ih, shape),
        jnp.where(
            row == 1,
            jnp.broadcast_to(inner - ih, shape),
            jnp.where(
                row == 2,
                jnp.broadcast_to(sh, shape),
                jnp.where(row == 3, jnp.broadcast_to(square - sh, shape), 0.0),
            ),
        ),
    )
    return tile.astype(BF16)


def unpack_products(tiles):
    vals = []
    for tile in tiles:
        t = tile.astype(F32)
        vals.append((t[0:1] + t[1:2], t[2:3] + t[3:4]))
    return tree([v[0] for v in vals]), tree([v[1] for v in vals])


def tree(items):
    items = list(items)
    while len(items) > 1:
        items = [items[i] + items[i + 1] for i in range(0, len(items), 2)]
    return items[0]


def send_partial(chunk, wide, w, part, tile, keep_ref, send_ref):
    for k in range(wide):
        total = part(pl.ds(pl.multiple_of(jnp.bitwise_xor(w, k) * chunk, chunk), chunk))
        out = send_ref if k % 2 else keep_ref
        out[pl.ds((k // 2) * chunk, chunk), :] = total.astype(BF16)
    if tile is not None:
        tail = pl.ds((wide // 2) * chunk, EXTRA)
        keep_ref[tail, :] = tile
        send_ref[tail, :] = tile


def send_halo(info, disp_ref, za_ref, zb_ref, theirs=None, base_ref=None):
    subs, rows_all, _ = disp_ref.shape
    zodd = jnp.bitwise_and(info[1], 1)
    za_ref[...] = disp_ref[(1 - zodd) * (subs - 1)]
    zb_ref[...] = disp_ref[zodd * (subs - 1)]
    if theirs is None:
        return
    blocks = theirs.shape[1]
    height = rows_all // blocks
    cap = base_ref.shape[0]
    odd = jnp.bitwise_and(info[0], 1)
    count = jnp.int32(0)
    for s in range(subs):

        def block(b, n, s=s):
            need = theirs[s, b] == odd
            rows = pl.ds(pl.multiple_of(b * height, height), height)

            @pl.when(need & (n < cap))
            def _():
                base_ref[n] = disp_ref[s, rows, :]

            return n + need.astype(jnp.int32)

        count = lax.fori_loop(0, blocks, block, count)


def first_kernel(chunk, wide, info, lam_ref, flex_ref, disp_ref, za_ref, zb_ref, keep_ref, send_ref):
    subs = lam_ref.shape[0]
    send_partial(
        chunk, wide, info[0], lambda rows: tree([lam_ref[s, rows, :] for s in range(subs)]),
        None, keep_ref, send_ref,
    )
    for s in range(subs):
        disp_ref[s] = jnp.dot(
            flex_ref[s], lam_ref[s].astype(BF16), preferred_element_type=F32
        ).astype(BF16)
    send_halo(info, disp_ref, za_ref, zb_ref)


def update_kernel(chunk, wide, step, last, *refs):
    info, *refs = refs
    lam_ref, dir_ref, alpha_ref, floor_ref = refs[:4]
    centre_refs = refs[4 : 4 + wide]
    refs = refs[4 + wide :]
    if not last:
        flex_ref, *refs = refs
    if step:
        refs = refs[1:]
    if last:
        lam_out, stack_ref, mean, sem = refs
    else:
        lam_out, stack_ref, disp_ref, za_ref, zb_ref, keep_ref, send_ref, half, mean, sem = refs
    w = info[0]
    subs, rows_all, cols = lam_ref.shape
    alpha = jnp.broadcast_to(alpha_ref[0:1, :], (chunk, cols))
    for k in range(wide):
        rows = pl.ds(pl.multiple_of(jnp.bitwise_xor(w, k) * chunk, chunk), chunk)
        centre = centre_refs[k][...].astype(F32)
        mean[rows, :] = centre
        total = None
        for s in range(subs):
            trial = lam_ref[s, rows, :] + alpha * dir_ref[s, rows, :].astype(F32)
            low = floor_ref[s, rows, :]
            low = jnp.concatenate([low] * (cols // low.shape[1]), axis=1)
            new = jnp.maximum(trial - centre, low)
            lam_out[s, rows, :] = new
            if not last:
                half[s, rows, :] = new.astype(BF16)
                total = new if total is None else total + new
        if not last:
            out = send_ref if k % 2 else keep_ref
            out[pl.ds((k // 2) * chunk, chunk), :] = total.astype(BF16)
    copy = pltpu.make_async_copy(mean, stack_ref.at[step], sem)
    copy.start()
    if not last:
        for s in range(subs):
            disp_ref[s] = jnp.dot(
                flex_ref[s], half[s], preferred_element_type=F32
            ).astype(BF16)
        send_halo(info, disp_ref, za_ref, zb_ref)
    copy.wait()


def direct_kernel(chunk, wide, info, side, powers, gap_ref, disp_ref, chip_ref, off_ref, za_ref, zb_ref, diri_ref, after_ref, dir_ref, keep_ref, send_ref, jump, work):
    w = info[0]
    odd = jnp.bitwise_and(w, 1)
    zodd = jnp.bitwise_and(info[1], 1)
    subs, rows_all, cols = gap_ref.shape
    blocks = side.shape[1]
    height = rows_all // blocks
    inner = jnp.zeros((8, cols), F32)
    square = jnp.zeros((8, cols), F32)
    count = jnp.int32(0)
    for s in range(subs):

        def block(b, n, s=s):
            face = side[s, b]
            rows = pl.ds(pl.multiple_of(b * height, height), height)

            def put(source):
                value = gap_ref[s, rows, :] - (
                    disp_ref[s, rows, :].astype(F32) - source.astype(F32)
                )
                jump[rows, :] = value
                work[s, rows, :] = value.astype(BF16)

            pl.when(face == odd)(lambda: put(chip_ref[s, rows, :]))
            away = face == 1 - odd
            pl.when(away)(lambda: put(off_ref[s, rows, :]))
            if s + 1 < subs:
                pl.when(face == 2)(lambda: put(disp_ref[s + 1, rows, :]))
            else:
                pl.when((face == 2) & (zodd == 0))(lambda: put(za_ref[rows, :]))
                pl.when((face == 2) & (zodd == 1))(lambda: put(zb_ref[rows, :]))
            if s > 0:
                pl.when(face == 3)(lambda: put(disp_ref[s - 1, rows, :]))
            else:
                pl.when((face == 3) & (zodd == 1))(lambda: put(za_ref[rows, :]))
                pl.when((face == 3) & (zodd == 0))(lambda: put(zb_ref[rows, :]))
            return n + away.astype(jnp.int32)

        count = lax.fori_loop(0, blocks, block, count)

        def level(i, carry, s=s):
            work[s] = jnp.dot(
                diri_ref[s], work[s], preferred_element_type=F32
            ).astype(BF16)
            return carry

        lax.fori_loop(0, powers[s], level, 0)
        direct = work[s]
        dir_ref[s] = direct
        dfloat = direct.astype(F32)
        inner = inner + jnp.sum((jump[...] * dfloat).reshape(rows_all // 8, 8, cols), axis=0)
        square = square + jnp.sum((dfloat * dfloat).reshape(rows_all // 8, 8, cols), axis=0)
    tile = pack_products(
        jnp.sum(inner, axis=0, keepdims=True), jnp.sum(square, axis=0, keepdims=True)
    )
    send_partial(
        chunk, wide, w, lambda rows: tree([work[s, rows, :].astype(F32) for s in range(subs)]),
        tile, keep_ref, send_ref,
    )


def add_kernel(chunk, chunks, ways_in, ways_out, extra, *refs):
    ins, outs = refs[:ways_in], refs[ways_in:]
    for c in range(chunks):
        rows = pl.ds(c * chunk, chunk)
        total = tree([r[rows, :].astype(F32) for r in ins]).astype(BF16)
        outs[c % ways_out][pl.ds((c // ways_out) * chunk, chunk), :] = total
    if extra:
        tail = pl.ds(chunks * chunk, EXTRA)
        tiles = [r[tail, :] for r in ins]
        if extra == "max":
            tile = functools.reduce(jnp.maximum, tiles)
        else:
            tile = pack_products(*unpack_products(tiles))
        for o in outs:
            o[pl.ds((chunks // ways_out) * chunk, EXTRA), :] = tile


def total_kernel(chunk, ways, extra, *refs):
    ins = refs[:ways]
    rows = pl.ds(0, chunk)
    refs[ways][...] = tree([r[rows, :].astype(F32) for r in ins])
    if extra:
        tiles = [r[pl.ds(chunk, EXTRA), :].astype(F32) for r in ins]
        refs[ways + 1][...] = functools.reduce(jnp.maximum, tiles)


def centre_kernel(chunk, ways, count, *refs):
    dirs, lam_ref = refs[:ways], refs[ways]
    centre_ref, alpha_ref = refs[ways + 1 :]
    rows = pl.ds(0, chunk)
    tail = pl.ds(chunk, EXTRA)
    inner, square = unpack_products([r[tail, :] for r in dirs])
    alpha = inner / (square + 1e-06)
    alpha_ref[...] = jnp.broadcast_to(alpha, alpha_ref.shape)
    dsum = tree([r[rows, :].astype(F32) for r in dirs])
    centre_ref[...] = ((lam_ref[...] + alpha * dsum) / count).astype(BF16)


def swap(x, axis, mask):
    n = lax.axis_size(axis)
    return lax.ppermute(x, axis, [(i, i ^ mask) for i in range(n)])


def scatter(keep, send, chunk, wide, extra):
    groups = stage_bits(wide)
    parts = [keep, send]
    shift, chunks = 0, wide
    cols = keep.shape[1]
    for g, bits in enumerate(groups):
        ways = 1 << bits
        got = [parts[0]] + [swap(parts[q], "wide", q << shift) for q in range(1, ways)]
        chunks //= ways
        shift += bits
        nxt = 1 << groups[g + 1] if g + 1 < len(groups) else 1
        shape = sds(((chunks // nxt) * chunk + (EXTRA if extra else 0), cols), BF16)
        parts = call(
            functools.partial(add_kernel, chunk, chunks, ways, nxt, extra),
            [shape] * nxt, 0, got, chunks * chunk * cols * ways,
            chunks * chunk * cols * 2 * (ways + 1), vmem=8,
        )
    return parts[0]


def across(x):
    size = lax.axis_size("eight")
    return [x] + [swap(x, "eight", q) for q in range(1, size)]


def gather(centre, wide):
    groups = stage_bits(wide)
    have = {0: centre}
    shift = wide.bit_length() - 1
    for bits in reversed(groups):
        shift -= bits
        new = dict(have)
        for q in range(1, 1 << bits):
            for k, v in have.items():
                new[k ^ (q << shift)] = swap(v, "wide", q << shift)
        have = new
    return [have[k] for k in range(wide)]


def body(multipliers, gap, flexibility, dirichlet, side, powers, active):
    subs, rows, cols = multipliers.shape
    wide = lax.axis_size("wide")
    eight = lax.axis_size("eight")
    count = wide * eight * subs
    chunk = rows // wide
    away = [(i, (i + 1) % wide if i % 2 else (i - 1) % wide) for i in range(wide)]
    pairs_a = [(i, i ^ 1) for i in range(eight) if i ^ 1 < eight]
    pairs_b = [(i, i + 1 if i % 2 else i - 1) for i in range(1, eight - 1)]
    if eight % 2:
        pairs_b = [(i, i + 1 if i % 2 else i - 1) for i in range(1, eight)]
    info = jnp.stack([lax.axis_index("wide"), lax.axis_index("eight")]).astype(jnp.int32)
    lanes = 128
    floor = jnp.where(
        jnp.broadcast_to(active[..., None], active.shape + (lanes,)) == 1, 0.0, -jnp.inf
    ).astype(F32)

    full = sds((subs, rows, cols), F32)
    half = sds((subs, rows, cols), BF16)
    one = sds((rows, cols), BF16)
    part = sds(((wide // 2) * chunk, cols), BF16)
    message = sds(((wide // 2) * chunk + EXTRA, cols), BF16)
    stack = sds((ITERS, rows, cols), F32)
    halo = [half, one, one]
    mm = 2 * subs * rows * rows * cols
    op_bytes = 2 * subs * rows * rows
    arr = subs * rows * cols

    alphas = []
    lam = multipliers
    disp, za, zb, lkeep, lsend = call(
        functools.partial(first_kernel, chunk, wide), halo + [part, part],
        1, [info, lam, flexibility], mm, op_bytes + arr * 8,
    )
    centres = None
    for step in range(ITERS):
        off = lax.ppermute(disp, "wide", away)
        za = lax.ppermute(za, "eight", pairs_a)
        zb = lax.ppermute(zb, "eight", pairs_b)
        chip = swap(disp, "wide", 1)
        lam_parts = across(scatter(lkeep, lsend, chunk, wide, None))
        (lam_total,) = call(
            functools.partial(total_kernel, chunk, eight, None), [sds((chunk, cols), F32)], 0,
            lam_parts, chunk * cols * eight, chunk * cols * 12, vmem=8,
        )
        direct, dkeep, dsend = call(
            functools.partial(direct_kernel, chunk, wide), [half, message, message], 3,
            [info, side, powers, gap, disp, chip, off, za, zb, dirichlet, lam_total],
            2 * mm, op_bytes + arr * 16,
            scratch=[pltpu.VMEM((rows, cols), F32), pltpu.VMEM((subs, rows, cols), BF16)],
        )
        dir_parts = across(scatter(dkeep, dsend, chunk, wide, "sum"))
        centre, alpha = call(
            functools.partial(centre_kernel, chunk, eight, float(count)),
            [sds((chunk, cols), BF16), sds((8, cols), F32)], 0, dir_parts + [lam_total],
            chunk * cols * 10, chunk * cols * 20, vmem=8,
        )
        pieces = gather(centre, wide)
        alphas.append(alpha[0])
        last = step == ITERS - 1
        n_smem = 1
        ins = [info, lam, direct, alpha, floor[step], *pieces] + ([] if last else [flexibility])
        aliases = {}
        anys = ()
        if step:
            aliases = {len(ins): 1}
            anys = (len(ins),)
            ins.append(centres)
        scratch = [pltpu.VMEM((rows, cols), F32), pltpu.SemaphoreType.DMA]
        kernel = functools.partial(update_kernel, chunk, wide, step, last)
        if last:
            lam, centres = call(
                kernel, [full, stack], n_smem, ins, arr * 6, arr * 12,
                scratch=scratch, anys=anys, any_outs=(1,), aliases=aliases,
            )
        else:
            lam, centres, disp, za, zb, lkeep, lsend = call(
                kernel, [full, stack] + halo + [part, part], n_smem, ins, mm, op_bytes + arr * 14,
                scratch=[pltpu.VMEM((subs, rows, cols), BF16)] + scratch,
                anys=anys, any_outs=(1,), aliases=aliases,
            )
    return (lam, jnp.stack(alphas), centres)


def solution(mesh):
    return jax.shard_map(
        body,
        mesh=mesh,
        in_specs=(
            P(("wide", "eight"), None, None),
            P(("wide", "eight"), None, None),
            P(("wide", "eight"), None, None),
            P(("wide", "eight"), None, None),
            P(("wide", "eight"), None),
            P(("wide", "eight")),
            P(None, ("wide", "eight"), None),
        ),
        out_specs=(P(("wide", "eight"), None, None), P(), P()),
        check_vma=False,
    )
```

```python
import functools

import jax
import jax.numpy as jnp
from jax import lax
from jax.experimental import pallas as pl
from jax.experimental.pallas import tpu as pltpu
from jax.sharding import PartitionSpec as P

ITERS = 3
PMAX = 3
EXTRA = 16
F32 = jnp.float32
BF16 = jnp.bfloat16
VMEM = pl.BlockSpec(memory_space=pltpu.VMEM)
ANY = pl.BlockSpec(memory_space=pl.ANY)
SMEM = pl.BlockSpec(memory_space=pltpu.SMEM)


def call(kernel, outs, n_smem, ins, flops, nbytes, scratch=(), vmem=16, anys=(), any_outs=(), aliases=None):
    return pl.pallas_call(
        kernel,
        out_shape=outs,
        in_specs=[
            SMEM if i < n_smem else ANY if i in anys else VMEM for i in range(len(ins))
        ],
        out_specs=[ANY if i in any_outs else VMEM for i in range(len(outs))],
        scratch_shapes=list(scratch),
        input_output_aliases=aliases or {},
        compiler_params=pltpu.CompilerParams(vmem_limit_bytes=vmem << 20),
        cost_estimate=pl.CostEstimate(flops=flops, bytes_accessed=nbytes, transcendentals=0),
    )(*ins)


def sds(shape, dtype):
    return jax.ShapeDtypeStruct(shape, dtype)


def stage_bits(size):
    total = size.bit_length() - 1
    groups = [1]
    left = total - 1
    while left > 0:
        take = 2 if left >= 2 else 1
        groups.append(take)
        left -= take
    return groups


def pack_products(inner, square, most):
    shape = (EXTRA, inner.shape[1])
    row = lax.broadcasted_iota(jnp.int32, shape, 0)
    ih = inner.astype(BF16).astype(F32)
    sh = square.astype(BF16).astype(F32)
    tile = jnp.zeros(shape, F32)
    for i, value in enumerate((ih, inner - ih, sh, square - sh, most)):
        tile = jnp.where(row == i, jnp.broadcast_to(value, shape), tile)
    return tile.astype(BF16)


def unpack_products(tiles):
    vals = []
    for tile in tiles:
        t = tile.astype(F32)
        vals.append((t[0:1] + t[1:2], t[2:3] + t[3:4], t[4:5]))
    return (
        tree([v[0] for v in vals]),
        tree([v[1] for v in vals]),
        functools.reduce(jnp.maximum, [v[2] for v in vals]),
    )


def tree(items):
    items = list(items)
    while len(items) > 1:
        items = [items[i] + items[i + 1] for i in range(0, len(items), 2)]
    return items[0]


def send_partial(chunk, wide, w, part, tile, keep_ref, send_ref):
    for k in range(wide):
        total = part(pl.ds(pl.multiple_of(jnp.bitwise_xor(w, k) * chunk, chunk), chunk))
        out = send_ref if k % 2 else keep_ref
        out[pl.ds((k // 2) * chunk, chunk), :] = total.astype(BF16)
    if tile is not None:
        tail = pl.ds((wide // 2) * chunk, EXTRA)
        keep_ref[tail, :] = tile
        send_ref[tail, :] = tile


def send_halo(info, disp_ref, za_ref, zb_ref, theirs=None, base_ref=None):
    subs, rows_all, _ = disp_ref.shape
    zodd = jnp.bitwise_and(info[1], 1)
    za_ref[...] = disp_ref[(1 - zodd) * (subs - 1)]
    zb_ref[...] = disp_ref[zodd * (subs - 1)]
    if theirs is None:
        return
    blocks = theirs.shape[1]
    height = rows_all // blocks
    cap = base_ref.shape[0]
    odd = jnp.bitwise_and(info[0], 1)
    count = jnp.int32(0)
    for s in range(subs):

        def block(b, n, s=s):
            need = theirs[s, b] == odd
            rows = pl.ds(pl.multiple_of(b * height, height), height)

            @pl.when(need & (n < cap))
            def _():
                base_ref[n] = disp_ref[s, rows, :]

            return n + need.astype(jnp.int32)

        count = lax.fori_loop(0, blocks, block, count)


def first_kernel(chunk, wide, info, lam_ref, flex_ref, disp_ref, za_ref, zb_ref, keep_ref, send_ref):
    subs = lam_ref.shape[0]
    send_partial(
        chunk, wide, info[0], lambda rows: tree([lam_ref[s, rows, :] for s in range(subs)]),
        None, keep_ref, send_ref,
    )
    for s in range(subs):
        disp_ref[s] = jnp.dot(
            flex_ref[s], lam_ref[s].astype(BF16), preferred_element_type=F32
        ).astype(BF16)
    send_halo(info, disp_ref, za_ref, zb_ref)


def update_kernel(chunk, wide, step, last, packed, *refs):
    info, *refs = refs
    theirs = base_ref = None
    if packed:
        theirs, *refs = refs
    lam_ref, dir_ref, alpha_ref, floor_ref = refs[:4]
    centre_refs = refs[4 : 4 + wide]
    refs = refs[4 + wide :]
    if not last:
        flex_ref, *refs = refs
    if step:
        refs = refs[1:]
    if last:
        lam_out, stack_ref, mean, sem = refs
    else:
        lam_out, stack_ref, disp_ref, za_ref, zb_ref, keep_ref, send_ref, *refs = refs
        if packed:
            base_ref, *refs = refs
        half, mean, sem = refs
    w = info[0]
    subs, rows_all, cols = lam_ref.shape
    alpha = jnp.broadcast_to(alpha_ref[0:1, :], (chunk, cols))
    for k in range(wide):
        rows = pl.ds(pl.multiple_of(jnp.bitwise_xor(w, k) * chunk, chunk), chunk)
        centre = centre_refs[k][...].astype(F32)
        mean[rows, :] = centre
        total = None
        for s in range(subs):
            trial = lam_ref[s, rows, :] + alpha * dir_ref[s, rows, :].astype(F32)
            low = floor_ref[s, rows, :]
            low = jnp.concatenate([low] * (cols // low.shape[1]), axis=1)
            new = jnp.maximum(trial - centre, low)
            lam_out[s, rows, :] = new
            if not last:
                half[s, rows, :] = new.astype(BF16)
                total = new if total is None else total + new
        if not last:
            out = send_ref if k % 2 else keep_ref
            out[pl.ds((k // 2) * chunk, chunk), :] = total.astype(BF16)
    copy = pltpu.make_async_copy(mean, stack_ref.at[step], sem)
    copy.start()
    if not last:
        for s in range(subs):
            disp_ref[s] = jnp.dot(
                flex_ref[s], half[s], preferred_element_type=F32
            ).astype(BF16)
        send_halo(info, disp_ref, za_ref, zb_ref, theirs, base_ref)
    copy.wait()


def direct_kernel(chunk, wide, packed, info, side, powers, gap_ref, disp_ref, chip_ref, off_ref, za_ref, zb_ref, diri_ref, dir_ref, keep_ref, send_ref, jump, work):
    w = info[0]
    odd = jnp.bitwise_and(w, 1)
    zodd = jnp.bitwise_and(info[1], 1)
    subs, rows_all, cols = gap_ref.shape
    blocks = side.shape[1]
    height = rows_all // blocks
    inner = jnp.zeros((8, cols), F32)
    square = jnp.zeros((8, cols), F32)
    count = jnp.int32(0)
    for s in range(subs):

        def block(b, n, s=s):
            face = side[s, b]
            rows = pl.ds(pl.multiple_of(b * height, height), height)

            def put(source):
                value = gap_ref[s, rows, :] - (
                    disp_ref[s, rows, :].astype(F32) - source.astype(F32)
                )
                jump[rows, :] = value
                work[s, rows, :] = value.astype(BF16)

            pl.when(face == odd)(lambda: put(chip_ref[s, rows, :]))
            away = face == 1 - odd
            if packed:
                slot = jnp.minimum(n, off_ref.shape[0] - 1)
                pl.when(away)(lambda: put(off_ref[slot]))
            else:
                pl.when(away)(lambda: put(off_ref[s, rows, :]))
            if s + 1 < subs:
                pl.when(face == 2)(lambda: put(disp_ref[s + 1, rows, :]))
            else:
                pl.when((face == 2) & (zodd == 0))(lambda: put(za_ref[rows, :]))
                pl.when((face == 2) & (zodd == 1))(lambda: put(zb_ref[rows, :]))
            if s > 0:
                pl.when(face == 3)(lambda: put(disp_ref[s - 1, rows, :]))
            else:
                pl.when((face == 3) & (zodd == 1))(lambda: put(za_ref[rows, :]))
                pl.when((face == 3) & (zodd == 0))(lambda: put(zb_ref[rows, :]))
            return n + away.astype(jnp.int32)

        count = lax.fori_loop(0, blocks, block, count)

        def level(i, carry, s=s):
            work[s] = jnp.dot(
                diri_ref[s], work[s], preferred_element_type=F32
            ).astype(BF16)
            return carry

        lax.fori_loop(0, powers[s], level, 0)
        direct = work[s]
        dir_ref[s] = direct
        dfloat = direct.astype(F32)
        inner = inner + jnp.sum((jump[...] * dfloat).reshape(rows_all // 8, 8, cols), axis=0)
        square = square + jnp.sum((dfloat * dfloat).reshape(rows_all // 8, 8, cols), axis=0)
    tile = pack_products(
        jnp.sum(inner, axis=0, keepdims=True),
        jnp.sum(square, axis=0, keepdims=True),
        jnp.broadcast_to(count.astype(F32), (1, cols)),
    )
    send_partial(
        chunk, wide, w, lambda rows: tree([work[s, rows, :].astype(F32) for s in range(subs)]),
        tile, keep_ref, send_ref,
    )


def add_kernel(chunk, chunks, ways_in, ways_out, extra, *refs):
    ins, outs = refs[:ways_in], refs[ways_in:]
    for c in range(chunks):
        rows = pl.ds(c * chunk, chunk)
        total = tree([r[rows, :].astype(F32) for r in ins]).astype(BF16)
        outs[c % ways_out][pl.ds((c // ways_out) * chunk, chunk), :] = total
    if extra:
        tail = pl.ds(chunks * chunk, EXTRA)
        tiles = [r[tail, :] for r in ins]
        tile = pack_products(*unpack_products(tiles))
        for o in outs:
            o[pl.ds((chunks // ways_out) * chunk, EXTRA), :] = tile


def centre_kernel(chunk, ways, count, *refs):
    dirs, lams = refs[:ways], refs[ways : 2 * ways]
    centre_ref, alpha_ref = refs[2 * ways :]
    rows = pl.ds(0, chunk)
    tail = pl.ds(chunk, EXTRA)
    inner, square, most = unpack_products([r[tail, :] for r in dirs])
    alpha = inner / (square + 1e-06)
    row = lax.broadcasted_iota(jnp.int32, alpha_ref.shape, 0)
    alpha_ref[...] = jnp.where(
        row == 0, jnp.broadcast_to(alpha, row.shape), jnp.broadcast_to(most, row.shape)
    )
    dsum = tree([r[rows, :].astype(F32) for r in dirs])
    lsum = tree([r[rows, :].astype(F32) for r in lams])
    centre_ref[...] = ((lsum + alpha * dsum) / count).astype(BF16)


def swap(x, axis, mask):
    n = lax.axis_size(axis)
    return lax.ppermute(x, axis, [(i, i ^ mask) for i in range(n)])


def scatter(keep, send, chunk, wide, extra):
    groups = stage_bits(wide)
    parts = [keep, send]
    shift, chunks = 0, wide
    cols = keep.shape[1]
    for g, bits in enumerate(groups):
        ways = 1 << bits
        got = [parts[0]] + [swap(parts[q], "wide", q << shift) for q in range(1, ways)]
        chunks //= ways
        shift += bits
        nxt = 1 << groups[g + 1] if g + 1 < len(groups) else 1
        shape = sds(((chunks // nxt) * chunk + (EXTRA if extra else 0), cols), BF16)
        parts = call(
            functools.partial(add_kernel, chunk, chunks, ways, nxt, extra),
            [shape] * nxt, 0, got, chunks * chunk * cols * ways,
            chunks * chunk * cols * 2 * (ways + 1), vmem=8,
        )
    return parts[0]


def across(x):
    size = lax.axis_size("eight")
    return [x] + [swap(x, "eight", q) for q in range(1, size)]


def gather(centre, wide):
    groups = stage_bits(wide)
    have = {0: centre}
    shift = wide.bit_length() - 1
    for bits in reversed(groups):
        shift -= bits
        new = dict(have)
        for q in range(1, 1 << bits):
            for k, v in have.items():
                new[k ^ (q << shift)] = swap(v, "wide", q << shift)
        have = new
    return [have[k] for k in range(wide)]


def body(multipliers, gap, flexibility, dirichlet, side, powers, active):
    subs, rows, cols = multipliers.shape
    blocks = side.shape[1]
    wide = lax.axis_size("wide")
    eight = lax.axis_size("eight")
    count = wide * eight * subs
    chunk = rows // wide
    cap = -(-subs * blocks * 9 // 16)
    away = [(i, (i + 1) % wide if i % 2 else (i - 1) % wide) for i in range(wide)]
    pairs_a = [(i, i ^ 1) for i in range(eight) if i ^ 1 < eight]
    pairs_b = [(i, i + 1 if i % 2 else i - 1) for i in range(1, eight - 1 + eight % 2)]
    info = jnp.stack([lax.axis_index("wide"), lax.axis_index("eight")]).astype(jnp.int32)
    theirs = lax.ppermute(side, "wide", away)
    lanes = 128
    floor = jnp.where(
        jnp.broadcast_to(active[..., None], active.shape + (lanes,)) == 1, 0.0, -jnp.inf
    ).astype(F32)

    full = sds((subs, rows, cols), F32)
    half = sds((subs, rows, cols), BF16)
    one = sds((rows, cols), BF16)
    base = sds((cap, rows // blocks, cols), BF16)
    part = sds(((wide // 2) * chunk, cols), BF16)
    message = sds(((wide // 2) * chunk + EXTRA, cols), BF16)
    stack = sds((ITERS, rows, cols), F32)
    halo = [half, one, one, part, part]
    mm = 2 * subs * rows * rows * cols
    op_bytes = 2 * subs * rows * rows
    arr = subs * rows * cols

    def search(disp, za, zb, lkeep, lsend, packed, blk=None):
        off = lax.ppermute(blk if packed else disp, "wide", away)
        za = lax.ppermute(za, "eight", pairs_a)
        zb = lax.ppermute(zb, "eight", pairs_b)
        chip = swap(disp, "wide", 1)
        lam_parts = across(scatter(lkeep, lsend, chunk, wide, False))
        direct, dkeep, dsend = call(
            functools.partial(direct_kernel, chunk, wide, packed), [half, message, message], 3,
            [info, side, powers, gap, disp, chip, off, za, zb, dirichlet],
            2 * mm, op_bytes + arr * 16,
            scratch=[pltpu.VMEM((rows, cols), F32), pltpu.VMEM((subs, rows, cols), BF16)],
        )
        dir_parts = across(scatter(dkeep, dsend, chunk, wide, True))
        centre, alpha = call(
            functools.partial(centre_kernel, chunk, eight, float(count)),
            [sds((chunk, cols), BF16), sds((8, cols), F32)], 0, dir_parts + lam_parts,
            chunk * cols * 10, chunk * cols * 20, vmem=8,
        )
        return direct, alpha, gather(centre, wide)

    def update(step, lam, direct, alpha, pieces, centres, packed):
        last = step == ITERS - 1
        ins = [info] + ([theirs] if packed and not last else [])
        n_smem = len(ins)
        ins += [lam, direct, alpha, floor[step], *pieces] + ([] if last else [flexibility])
        aliases, anys = {}, ()
        if step:
            aliases, anys = {len(ins): 1}, (len(ins),)
            ins.append(centres)
        scratch = [pltpu.VMEM((rows, cols), F32), pltpu.SemaphoreType.DMA]
        outs = [full, stack]
        if not last:
            outs += halo + ([base] if packed else [])
            scratch = [pltpu.VMEM((subs, rows, cols), BF16)] + scratch
        return call(
            functools.partial(update_kernel, chunk, wide, step, last, packed and not last),
            outs, n_smem, ins, arr * 6 if last else mm, arr * 12 + (0 if last else op_bytes),
            scratch=scratch, anys=anys, any_outs=(1,), aliases=aliases,
        )

    first = call(
        functools.partial(first_kernel, chunk, wide), halo, 1, [info, multipliers, flexibility],
        mm, op_bytes + arr * 8,
    )
    direct, alpha, pieces = search(*first, False)

    def rest(packed, direct, alpha, pieces):
        alphas = [alpha[0]]
        lam, centres = multipliers, None
        for step in range(ITERS - 1):
            lam, centres, disp, za, zb, lkeep, lsend, *blk = update(
                step, lam, direct, alpha, pieces, centres, packed
            )
            direct, alpha, pieces = search(disp, za, zb, lkeep, lsend, packed, *blk)
            alphas.append(alpha[0])
        lam, centres = update(ITERS - 1, lam, direct, alpha, pieces, centres, packed)
        return lam, jnp.stack(alphas), centres

    return lax.cond(
        alpha[1, 0] <= cap,
        functools.partial(rest, True),
        functools.partial(rest, False),
        direct, alpha, pieces,
    )


def solution(mesh):
    return jax.shard_map(
        body,
        mesh=mesh,
        in_specs=(
            P(("wide", "eight"), None, None),
            P(("wide", "eight"), None, None),
            P(("wide", "eight"), None, None),
            P(("wide", "eight"), None, None),
            P(("wide", "eight"), None),
            P(("wide", "eight")),
            P(None, ("wide", "eight"), None),
        ),
        out_specs=(P(("wide", "eight"), None, None), P(), P()),
        check_vma=False,
    )
```

```python
import functools

import jax
import jax.numpy as jnp
from jax import lax
from jax.experimental import pallas as pl
from jax.experimental.pallas import tpu as pltpu
from jax.sharding import PartitionSpec as P


ITERS = 3
EXTRA = 16
F32 = jnp.float32
BF16 = jnp.bfloat16
VMEM = pl.BlockSpec(memory_space=pltpu.VMEM)
ANY = pl.BlockSpec(memory_space=pl.ANY)
SMEM = pl.BlockSpec(memory_space=pltpu.SMEM)


def call(kernel, outs, n_smem, ins, flops, nbytes, scratch=(), vmem=16, anys=(), any_outs=(), aliases=None):
    return pl.pallas_call(
        kernel,
        out_shape=outs,
        in_specs=[
            SMEM if i < n_smem else ANY if i in anys else VMEM for i in range(len(ins))
        ],
        out_specs=[ANY if i in any_outs else VMEM for i in range(len(outs))],
        scratch_shapes=list(scratch),
        input_output_aliases=aliases or {},
        compiler_params=pltpu.CompilerParams(vmem_limit_bytes=vmem << 20),
        cost_estimate=pl.CostEstimate(flops=flops, bytes_accessed=nbytes, transcendentals=0),
    )(*ins)


def sds(shape, dtype):
    return jax.ShapeDtypeStruct(shape, dtype)


def stage_bits(size):
    total = size.bit_length() - 1
    groups = [1]
    left = total - 1
    while left > 0:
        take = 2 if left >= 2 else 1
        groups.append(take)
        left -= take
    return groups


def pack_products(inner, square, most):
    shape = (EXTRA, inner.shape[1])
    row = lax.broadcasted_iota(jnp.int32, shape, 0)
    ih = inner.astype(BF16).astype(F32)
    sh = square.astype(BF16).astype(F32)
    tile = jnp.zeros(shape, F32)
    for i, value in enumerate((ih, inner - ih, sh, square - sh, most)):
        tile = jnp.where(row == i, jnp.broadcast_to(value, shape), tile)
    return tile.astype(BF16)


def unpack_products(tiles):
    vals = []
    for tile in tiles:
        t = tile.astype(F32)
        vals.append((t[0:1] + t[1:2], t[2:3] + t[3:4], t[4:5]))
    return (
        tree([v[0] for v in vals]),
        tree([v[1] for v in vals]),
        functools.reduce(jnp.maximum, [v[2] for v in vals]),
    )


def tree(items):
    items = list(items)
    while len(items) > 1:
        items = [items[i] + items[i + 1] for i in range(0, len(items), 2)]
    return items[0]


def send_partial(chunk, wide, w, part, tile, keep_ref, send_ref):
    for k in range(wide):
        total = part(pl.ds(pl.multiple_of(jnp.bitwise_xor(w, k) * chunk, chunk), chunk))
        out = send_ref if k % 2 else keep_ref
        out[pl.ds((k // 2) * chunk, chunk), :] = total.astype(BF16)
    if tile is not None:
        tail = pl.ds((wide // 2) * chunk, EXTRA)
        keep_ref[tail, :] = tile
        send_ref[tail, :] = tile


def send_halo(info, disp_ref, za_ref, zb_ref, theirs=None, base_ref=None):
    subs, rows_all, _ = disp_ref.shape
    zodd = jnp.bitwise_and(info[1], 1)
    za_ref[...] = disp_ref[(1 - zodd) * (subs - 1)]
    zb_ref[...] = disp_ref[zodd * (subs - 1)]
    if theirs is None:
        return
    blocks = theirs.shape[1]
    height = rows_all // blocks
    cap = base_ref.shape[0]
    odd = jnp.bitwise_and(info[0], 1)
    count = jnp.int32(0)
    for s in range(subs):

        def block(b, n, s=s):
            need = theirs[s, b] == odd
            rows = pl.ds(pl.multiple_of(b * height, height), height)

            @pl.when(need & (n < cap))
            def _():
                base_ref[n] = disp_ref[s, rows, :]

            return n + need.astype(jnp.int32)

        count = lax.fori_loop(0, blocks, block, count)


def first_kernel(chunk, wide, info, lam_ref, half_ref, keep_ref, send_ref):
    subs = lam_ref.shape[0]
    half_ref[...] = lam_ref[...].astype(BF16)
    send_partial(
        chunk, wide, info[0], lambda rows: tree([lam_ref[s, rows, :] for s in range(subs)]),
        None, keep_ref, send_ref,
    )


def flex_kernel(packed, info, *refs):
    theirs = base_ref = None
    if packed:
        theirs, half_ref, flex_ref, disp_ref, za_ref, zb_ref, base_ref = refs
    else:
        half_ref, flex_ref, disp_ref, za_ref, zb_ref = refs
    for s in range(half_ref.shape[0]):
        disp_ref[s] = jnp.dot(
            flex_ref[s], half_ref[s], preferred_element_type=F32
        ).astype(BF16)
    send_halo(info, disp_ref, za_ref, zb_ref, theirs, base_ref)


def update_kernel(chunk, wide, step, last, info, lam_ref, dir_ref, alpha_ref, floor_ref, *refs):
    centre_refs = refs[:wide]
    refs = refs[wide:]
    if step:
        refs = refs[1:]
    if last:
        lam_out, stack_ref, mean, sem = refs
    else:
        lam_out, stack_ref, half_ref, keep_ref, send_ref, mean, sem = refs
    w = info[0]
    subs, _, cols = lam_ref.shape
    alpha = jnp.broadcast_to(alpha_ref[0:1, :], (chunk, cols))
    for k in range(wide):
        rows = pl.ds(pl.multiple_of(jnp.bitwise_xor(w, k) * chunk, chunk), chunk)
        centre = centre_refs[k][...].astype(F32)
        mean[rows, :] = centre
        total = None
        for s in range(subs):
            trial = lam_ref[s, rows, :] + alpha * dir_ref[s, rows, :].astype(F32)
            low = floor_ref[s, rows, :]
            low = jnp.concatenate([low] * (cols // low.shape[1]), axis=1)
            new = jnp.maximum(trial - centre, low)
            lam_out[s, rows, :] = new
            if not last:
                half_ref[s, rows, :] = new.astype(BF16)
                total = new if total is None else total + new
        if not last:
            out = send_ref if k % 2 else keep_ref
            out[pl.ds((k // 2) * chunk, chunk), :] = total.astype(BF16)
    copy = pltpu.make_async_copy(mean, stack_ref.at[step], sem)
    copy.start()
    copy.wait()


def direct_kernel(chunk, wide, packed, info, side, powers, gap_ref, disp_ref, chip_ref, off_ref, za_ref, zb_ref, diri_ref, after_ref, dir_ref, keep_ref, send_ref, jump, work):
    w = info[0]
    odd = jnp.bitwise_and(w, 1)
    zodd = jnp.bitwise_and(info[1], 1)
    subs, rows_all, cols = gap_ref.shape
    blocks = side.shape[1]
    height = rows_all // blocks
    inner = jnp.zeros((8, cols), F32)
    square = jnp.zeros((8, cols), F32)
    count = jnp.int32(0)
    for s in range(subs):

        def block(b, n, s=s):
            face = side[s, b]
            rows = pl.ds(pl.multiple_of(b * height, height), height)

            def put(source):
                value = gap_ref[s, rows, :] - (
                    disp_ref[s, rows, :].astype(F32) - source.astype(F32)
                )
                jump[rows, :] = value
                work[s, rows, :] = value.astype(BF16)

            pl.when(face == odd)(lambda: put(chip_ref[s, rows, :]))
            away = face == 1 - odd
            if packed:
                slot = jnp.minimum(n, off_ref.shape[0] - 1)
                pl.when(away)(lambda: put(off_ref[slot]))
            else:
                pl.when(away)(lambda: put(off_ref[s, rows, :]))
            if s + 1 < subs:
                pl.when(face == 2)(lambda: put(disp_ref[s + 1, rows, :]))
            else:
                pl.when((face == 2) & (zodd == 0))(lambda: put(za_ref[rows, :]))
                pl.when((face == 2) & (zodd == 1))(lambda: put(zb_ref[rows, :]))
            if s > 0:
                pl.when(face == 3)(lambda: put(disp_ref[s - 1, rows, :]))
            else:
                pl.when((face == 3) & (zodd == 1))(lambda: put(za_ref[rows, :]))
                pl.when((face == 3) & (zodd == 0))(lambda: put(zb_ref[rows, :]))
            return n + away.astype(jnp.int32)

        count = lax.fori_loop(0, blocks, block, count)

        def level(i, carry, s=s):
            work[s] = jnp.dot(
                diri_ref[s], work[s], preferred_element_type=F32
            ).astype(BF16)
            return carry

        lax.fori_loop(0, powers[s], level, 0)
        direct = work[s]
        dir_ref[s] = direct
        dfloat = direct.astype(F32)
        inner = inner + jnp.sum((jump[...] * dfloat).reshape(rows_all // 8, 8, cols), axis=0)
        square = square + jnp.sum((dfloat * dfloat).reshape(rows_all // 8, 8, cols), axis=0)
    tile = pack_products(
        jnp.sum(inner, axis=0, keepdims=True),
        jnp.sum(square, axis=0, keepdims=True),
        jnp.broadcast_to(count.astype(F32), (1, cols)),
    )
    send_partial(
        chunk, wide, w, lambda rows: tree([work[s, rows, :].astype(F32) for s in range(subs)]),
        tile, keep_ref, send_ref,
    )


def add_kernel(chunk, chunks, ways_in, ways_out, extra, *refs):
    ins, outs = refs[:ways_in], refs[ways_in:]
    for c in range(chunks):
        rows = pl.ds(c * chunk, chunk)
        total = tree([r[rows, :].astype(F32) for r in ins]).astype(BF16)
        outs[c % ways_out][pl.ds((c // ways_out) * chunk, chunk), :] = total
    if extra:
        tail = pl.ds(chunks * chunk, EXTRA)
        tiles = [r[tail, :] for r in ins]
        tile = pack_products(*unpack_products(tiles))
        for o in outs:
            o[pl.ds((chunks // ways_out) * chunk, EXTRA), :] = tile


def centre_kernel(chunk, ways, count, *refs):
    dirs, lams = refs[:ways], refs[ways : 2 * ways]
    centre_ref, alpha_ref = refs[2 * ways :]
    rows = pl.ds(0, chunk)
    tail = pl.ds(chunk, EXTRA)
    inner, square, most = unpack_products([r[tail, :] for r in dirs])
    alpha = inner / (square + 1e-06)
    row = lax.broadcasted_iota(jnp.int32, alpha_ref.shape, 0)
    alpha_ref[...] = jnp.where(
        row == 0, jnp.broadcast_to(alpha, row.shape), jnp.broadcast_to(most, row.shape)
    )
    dsum = tree([r[rows, :].astype(F32) for r in dirs])
    lsum = tree([r[rows, :].astype(F32) for r in lams])
    centre_ref[...] = ((lsum + alpha * dsum) / count).astype(BF16)


def swap(x, axis, mask):
    n = lax.axis_size(axis)
    return lax.ppermute(x, axis, [(i, i ^ mask) for i in range(n)])


def stage(parts, g, chunk, wide, extra):
    groups = stage_bits(wide)
    shift = sum(groups[:g])
    ways = 1 << groups[g]
    chunks = wide >> (shift + groups[g])
    cols = parts[0].shape[1]
    got = [parts[0]] + [swap(parts[q], "wide", q << shift) for q in range(1, ways)]
    nxt = 1 << groups[g + 1] if g + 1 < len(groups) else 1
    shape = sds(((chunks // nxt) * chunk + (EXTRA if extra else 0), cols), BF16)
    return call(
        functools.partial(add_kernel, chunk, chunks, ways, nxt, extra),
        [shape] * nxt, 0, got, chunks * chunk * cols * ways,
        chunks * chunk * cols * 2 * (ways + 1), vmem=8,
    )


def scatter(parts, first, chunk, wide, extra):
    for g in range(first, len(stage_bits(wide))):
        parts = stage(parts, g, chunk, wide, extra)
    return parts[0]


def across(x):
    size = lax.axis_size("eight")
    return [x] + [swap(x, "eight", q) for q in range(1, size)]


def gather(centre, wide):
    groups = stage_bits(wide)
    have = {0: centre}
    shift = wide.bit_length() - 1
    for bits in reversed(groups):
        shift -= bits
        new = dict(have)
        for q in range(1, 1 << bits):
            for k, v in have.items():
                new[k ^ (q << shift)] = swap(v, "wide", q << shift)
        have = new
    return [have[k] for k in range(wide)]


def body(multipliers, gap, flexibility, dirichlet, side, powers, active):
    subs, rows, cols = multipliers.shape
    blocks = side.shape[1]
    wide = lax.axis_size("wide")
    eight = lax.axis_size("eight")
    count = wide * eight * subs
    chunk = rows // wide
    cap = -(-subs * blocks * 9 // 16)
    away = [(i, (i + 1) % wide if i % 2 else (i - 1) % wide) for i in range(wide)]
    pairs_a = [(i, i ^ 1) for i in range(eight) if i ^ 1 < eight]
    pairs_b = [(i, i + 1 if i % 2 else i - 1) for i in range(1, eight - 1 + eight % 2)]
    info = jnp.stack([lax.axis_index("wide"), lax.axis_index("eight")]).astype(jnp.int32)
    theirs = lax.ppermute(side, "wide", away)
    lanes = 128
    floor = jnp.where(
        jnp.broadcast_to(active[..., None], active.shape + (lanes,)) == 1, 0.0, -jnp.inf
    ).astype(F32)

    full = sds((subs, rows, cols), F32)
    half = sds((subs, rows, cols), BF16)
    one = sds((rows, cols), BF16)
    base = sds((cap, rows // blocks, cols), BF16)
    part = sds(((wide // 2) * chunk, cols), BF16)
    message = sds(((wide // 2) * chunk + EXTRA, cols), BF16)
    stack = sds((ITERS, rows, cols), F32)
    mm = 2 * subs * rows * rows * cols
    op_bytes = 2 * subs * rows * rows
    arr = subs * rows * cols

    def search(half_lam, lkeep, lsend, packed):
        ins = [info] + ([theirs] if packed else []) + [half_lam, flexibility]
        sends = call(
            functools.partial(flex_kernel, packed), [half, one, one] + ([base] if packed else []),
            len(ins) - 2, ins, mm, op_bytes + arr * 6,
        )
        lams = stage([lkeep, lsend], 0, chunk, wide, False)
        lams, sends = lax.optimization_barrier((lams, sends))
        own = scatter(lams, 1, chunk, wide, False)
        disp, za, zb = sends[:3]
        off = lax.ppermute(sends[-1] if packed else disp, "wide", away)
        za = lax.ppermute(za, "eight", pairs_a)
        zb = lax.ppermute(zb, "eight", pairs_b)
        chip = swap(disp, "wide", 1)
        lam_parts = across(own)
        direct, dkeep, dsend = call(
            functools.partial(direct_kernel, chunk, wide, packed), [half, message, message], 3,
            [info, side, powers, gap, disp, chip, off, za, zb, dirichlet, own],
            2 * mm, op_bytes + arr * 16,
            scratch=[pltpu.VMEM((rows, cols), F32), pltpu.VMEM((subs, rows, cols), BF16)],
        )
        dirs = stage([dkeep, dsend], 0, chunk, wide, True)
        dir_parts = across(scatter(dirs, 1, chunk, wide, True))
        centre, alpha = call(
            functools.partial(centre_kernel, chunk, eight, float(count)),
            [sds((chunk, cols), BF16), sds((8, cols), F32)], 0, dir_parts + lam_parts,
            chunk * cols * 10, chunk * cols * 20, vmem=8,
        )
        return direct, alpha, gather(centre, wide)

    def update(step, lam, direct, alpha, pieces, centres):
        last = step == ITERS - 1
        ins = [info, lam, direct, alpha, floor[step], *pieces]
        aliases, anys = {}, ()
        if step:
            aliases, anys = {len(ins): 1}, (len(ins),)
            ins.append(centres)
        return call(
            functools.partial(update_kernel, chunk, wide, step, last),
            [full, stack] + ([] if last else [half, part, part]), 1, ins, arr * 6, arr * 16,
            scratch=[pltpu.VMEM((rows, cols), F32), pltpu.SemaphoreType.DMA],
            anys=anys, any_outs=(1,), aliases=aliases,
        )

    first = call(
        functools.partial(first_kernel, chunk, wide), [half, part, part], 1, [info, multipliers],
        arr * 2, arr * 8,
    )
    direct, alpha, pieces = search(*first, False)

    def rest(packed, direct, alpha, pieces):
        alphas = [alpha[0]]
        lam, centres = multipliers, None
        for step in range(ITERS - 1):
            lam, centres, *sums = update(step, lam, direct, alpha, pieces, centres)
            direct, alpha, pieces = search(*sums, packed)
            alphas.append(alpha[0])
        lam, centres = update(ITERS - 1, lam, direct, alpha, pieces, centres)
        return lam, jnp.stack(alphas), centres

    return lax.cond(
        alpha[1, 0] <= cap,
        functools.partial(rest, True),
        functools.partial(rest, False),
        direct, alpha, pieces,
    )


def solution(mesh):
    return jax.shard_map(
        body,
        mesh=mesh,
        in_specs=(
            P(("wide", "eight"), None, None),
            P(("wide", "eight"), None, None),
            P(("wide", "eight"), None, None),
            P(("wide", "eight"), None, None),
            P(("wide", "eight"), None),
            P(("wide", "eight")),
            P(None, ("wide", "eight"), None),
        ),
        out_specs=(P(("wide", "eight"), None, None), P(), P()),
        check_vma=False,
    )
```

```python
import functools

import jax
import jax.numpy as jnp
from jax import lax
from jax.experimental import pallas as pl
from jax.experimental.pallas import tpu as pltpu
from jax.sharding import PartitionSpec as P


ITERS = 3
EXTRA = 16
F32 = jnp.float32
BF16 = jnp.bfloat16
VMEM = pl.BlockSpec(memory_space=pltpu.VMEM)
ANY = pl.BlockSpec(memory_space=pl.ANY)
SMEM = pl.BlockSpec(memory_space=pltpu.SMEM)


def call(kernel, outs, n_smem, ins, flops, nbytes, scratch=(), vmem=16, anys=(), any_outs=(), aliases=None):
    return pl.pallas_call(
        kernel,
        out_shape=outs,
        in_specs=[
            SMEM if i < n_smem else ANY if i in anys else VMEM for i in range(len(ins))
        ],
        out_specs=[ANY if i in any_outs else VMEM for i in range(len(outs))],
        scratch_shapes=list(scratch),
        input_output_aliases=aliases or {},
        compiler_params=pltpu.CompilerParams(vmem_limit_bytes=vmem << 20),
        cost_estimate=pl.CostEstimate(flops=flops, bytes_accessed=nbytes, transcendentals=0),
    )(*ins)


def sds(shape, dtype):
    return jax.ShapeDtypeStruct(shape, dtype)


def stage_bits(size):
    total = size.bit_length() - 1
    groups = [1]
    left = total - 1
    while left > 0:
        take = 2 if left >= 2 else 1
        groups.append(take)
        left -= take
    return groups


def pack_products(inner, square, most):
    shape = (EXTRA, inner.shape[1])
    row = lax.broadcasted_iota(jnp.int32, shape, 0)
    ih = inner.astype(BF16).astype(F32)
    sh = square.astype(BF16).astype(F32)
    tile = jnp.zeros(shape, F32)
    for i, value in enumerate((ih, inner - ih, sh, square - sh, most)):
        tile = jnp.where(row == i, jnp.broadcast_to(value, shape), tile)
    return tile.astype(BF16)


def unpack_products(tiles):
    vals = []
    for tile in tiles:
        t = tile.astype(F32)
        vals.append((t[0:1] + t[1:2], t[2:3] + t[3:4], t[4:5]))
    return (
        tree([v[0] for v in vals]),
        tree([v[1] for v in vals]),
        functools.reduce(jnp.maximum, [v[2] for v in vals]),
    )


def tree(items):
    items = list(items)
    while len(items) > 1:
        items = [items[i] + items[i + 1] for i in range(0, len(items), 2)]
    return items[0]


def send_partial(chunk, wide, w, part, tile, keep_ref, send_ref):
    for k in range(wide):
        total = part(pl.ds(pl.multiple_of(jnp.bitwise_xor(w, k) * chunk, chunk), chunk))
        out = send_ref if k % 2 else keep_ref
        out[pl.ds((k // 2) * chunk, chunk), :] = total.astype(BF16)
    if tile is not None:
        tail = pl.ds((wide // 2) * chunk, EXTRA)
        keep_ref[tail, :] = tile
        send_ref[tail, :] = tile


def pack_blocks(table, row, face, source, disp_ref, out_ref, count):
    blocks = table.shape[1]
    height = disp_ref.shape[1] // blocks
    cap = out_ref.shape[0]

    def block(b, n):
        need = table[row, b] == face
        rows = pl.ds(pl.multiple_of(b * height, height), height)

        @pl.when(need & (n < cap))
        def _():
            out_ref[n] = disp_ref[source, rows, :]

        return n + need.astype(jnp.int32)

    return lax.fori_loop(0, blocks, block, count)


def send_halo(info, disp_ref, outs, tables):
    last = disp_ref.shape[0] - 1
    odd = jnp.bitwise_and(info[0], 1)
    zodd = jnp.bitwise_and(info[1], 1)
    za_ref, zb_ref = outs[:2]
    zero = jnp.int32(0)
    if not tables:
        za_ref[...] = disp_ref[(1 - zodd) * last]
        zb_ref[...] = disp_ref[zodd * last]
        return
    theirs, ta, tb = tables
    count = zero
    for s in range(last + 1):
        count = pack_blocks(theirs, s, odd, s, disp_ref, outs[2], count)
    pack_blocks(ta, zodd * last, 3 - zodd, (1 - zodd) * last, disp_ref, za_ref, zero)
    pack_blocks(tb, (1 - zodd) * last, 2 + zodd, zodd * last, disp_ref, zb_ref, zero)


def first_kernel(chunk, wide, info, lam_ref, half_ref, keep_ref, send_ref):
    subs = lam_ref.shape[0]
    half_ref[...] = lam_ref[...].astype(BF16)
    send_partial(
        chunk, wide, info[0], lambda rows: tree([lam_ref[s, rows, :] for s in range(subs)]),
        None, keep_ref, send_ref,
    )


def flex_kernel(step, packed, info, *refs):
    tables, refs = refs[: 3 * packed], refs[3 * packed :]
    half_ref, flex_ref, *refs = refs
    if step:
        mean_ref, *refs = refs
        if step > 1:
            refs = refs[1:]
        disp_ref, *outs, stack_ref, sem = refs
        copy = pltpu.make_async_copy(mean_ref, stack_ref.at[step - 1], sem)
        copy.start()
    else:
        disp_ref, *outs = refs
    for s in range(half_ref.shape[0]):
        disp_ref[s] = jnp.dot(
            flex_ref[s], half_ref[s], preferred_element_type=F32
        ).astype(BF16)
    send_halo(info, disp_ref, outs, tables)
    if step:
        copy.wait()


def update_kernel(chunk, wide, step, last, info, lam_ref, dir_ref, alpha_ref, floor_ref, *refs):
    centre_refs = refs[:wide]
    refs = refs[wide:]
    if last:
        _, lam_out, stack_ref, new_ref, mean_ref, sems = refs
    else:
        new_ref, mean_ref, half_ref, keep_ref, send_ref = refs
    w = info[0]
    subs, _, cols = lam_ref.shape
    alpha = jnp.broadcast_to(alpha_ref[0:1, :], (chunk, cols))
    copies = []

    def send(src, dst):
        copies.append(pltpu.make_async_copy(src, dst, sems.at[len(copies)]))
        copies[-1].start()

    for k in range(wide):
        rows = pl.ds(pl.multiple_of(jnp.bitwise_xor(w, k) * chunk, chunk), chunk)
        centre = centre_refs[k][...].astype(F32)
        mean_ref[rows, :] = centre
        total = None
        for s in range(subs):
            trial = lam_ref[s, rows, :] + alpha * dir_ref[s, rows, :].astype(F32)
            low = floor_ref[s, rows, :]
            low = jnp.concatenate([low] * (cols // low.shape[1]), axis=1)
            new = jnp.maximum(trial - centre, low)
            new_ref[s, rows, :] = new
            if last:
                send(new_ref.at[s, rows, :], lam_out.at[s, rows, :])
            else:
                half_ref[s, rows, :] = new.astype(BF16)
                total = new if total is None else total + new
        if last:
            send(mean_ref.at[rows, :], stack_ref.at[step, rows, :])
        else:
            out = send_ref if k % 2 else keep_ref
            out[pl.ds((k // 2) * chunk, chunk), :] = total.astype(BF16)
    for copy in copies:
        copy.wait()


def direct_kernel(chunk, wide, eight, caps, packed, info, side, powers, gap_ref, disp_ref, chip_ref, off_ref, za_ref, zb_ref, diri_ref, after_ref, dir_ref, keep_ref, send_ref, jump, work):
    w, z = info[0], info[1]
    odd = jnp.bitwise_and(w, 1)
    zodd = jnp.bitwise_and(z, 1)
    subs, rows_all, cols = gap_ref.shape
    blocks = side.shape[1]
    height = rows_all // blocks
    inner = jnp.zeros((8, cols), F32)
    square = jnp.zeros((8, cols), F32)
    counts = (jnp.int32(0),) * 3
    for s in range(subs):

        def block(b, ns, s=s):
            n, above, below = ns
            face = side[s, b]
            rows = pl.ds(pl.multiple_of(b * height, height), height)

            def put(source):
                value = gap_ref[s, rows, :] - (
                    disp_ref[s, rows, :].astype(F32) - source.astype(F32)
                )
                jump[rows, :] = value
                work[s, rows, :] = value.astype(BF16)

            def take(ref, slot):
                if packed:
                    return ref[jnp.minimum(slot, ref.shape[0] - 1)]
                return ref[s, rows, :] if len(ref.shape) == 3 else ref[rows, :]

            pl.when(face == odd)(lambda: put(chip_ref[s, rows, :]))
            away = face == 1 - odd
            pl.when(away)(lambda: put(take(off_ref, n)))
            n = n + away.astype(jnp.int32)
            if s + 1 < subs:
                pl.when(face == 2)(lambda: put(disp_ref[s + 1, rows, :]))
            else:
                pl.when((face == 2) & (zodd == 0))(lambda: put(take(za_ref, above)))
                pl.when((face == 2) & (zodd == 1))(lambda: put(take(zb_ref, above)))
                above = above + (face == 2).astype(jnp.int32)
            if s > 0:
                pl.when(face == 3)(lambda: put(disp_ref[s - 1, rows, :]))
            else:
                pl.when((face == 3) & (zodd == 1))(lambda: put(take(za_ref, below)))
                pl.when((face == 3) & (zodd == 0))(lambda: put(take(zb_ref, below)))
                below = below + (face == 3).astype(jnp.int32)
            return n, above, below

        counts = lax.fori_loop(0, blocks, block, counts)

        def level(i, carry, s=s):
            work[s] = jnp.dot(
                diri_ref[s], work[s], preferred_element_type=F32
            ).astype(BF16)
            return carry

        lax.fori_loop(0, powers[s], level, 0)
        direct = work[s]
        dir_ref[s] = direct
        dfloat = direct.astype(F32)
        inner = inner + jnp.sum((jump[...] * dfloat).reshape(rows_all // 8, 8, cols), axis=0)
        square = square + jnp.sum((dfloat * dfloat).reshape(rows_all // 8, 8, cols), axis=0)
    n, above, below = counts
    excess = jnp.maximum(
        n - caps[0],
        jnp.maximum(
            jnp.where(z < eight - 1, above, 0) - caps[1], jnp.where(z > 0, below, 0) - caps[1]
        ),
    )
    tile = pack_products(
        jnp.sum(inner, axis=0, keepdims=True),
        jnp.sum(square, axis=0, keepdims=True),
        jnp.broadcast_to(excess.astype(F32), (1, cols)),
    )
    send_partial(
        chunk, wide, w, lambda rows: tree([work[s, rows, :].astype(F32) for s in range(subs)]),
        tile, keep_ref, send_ref,
    )


def add_kernel(chunk, chunks, ways_in, ways_out, extra, *refs):
    ins, outs = refs[:ways_in], refs[ways_in:]
    for c in range(chunks):
        rows = pl.ds(c * chunk, chunk)
        total = tree([r[rows, :].astype(F32) for r in ins]).astype(BF16)
        outs[c % ways_out][pl.ds((c // ways_out) * chunk, chunk), :] = total
    if extra:
        tail = pl.ds(chunks * chunk, EXTRA)
        tiles = [r[tail, :] for r in ins]
        tile = pack_products(*unpack_products(tiles))
        for o in outs:
            o[pl.ds((chunks // ways_out) * chunk, EXTRA), :] = tile


def centre_kernel(chunk, ways, count, *refs):
    dirs, lams = refs[:ways], refs[ways : 2 * ways]
    centre_ref, alpha_ref = refs[2 * ways :]
    rows = pl.ds(0, chunk)
    tail = pl.ds(chunk, EXTRA)
    inner, square, most = unpack_products([r[tail, :] for r in dirs])
    alpha = inner / (square + 1e-06)
    row = lax.broadcasted_iota(jnp.int32, alpha_ref.shape, 0)
    alpha_ref[...] = jnp.where(
        row == 0, jnp.broadcast_to(alpha, row.shape), jnp.broadcast_to(most, row.shape)
    )
    dsum = tree([r[rows, :].astype(F32) for r in dirs])
    lsum = tree([r[rows, :].astype(F32) for r in lams])
    centre_ref[...] = ((lsum + alpha * dsum) / count).astype(BF16)


def swap(x, axis, mask):
    n = lax.axis_size(axis)
    return lax.ppermute(x, axis, [(i, i ^ mask) for i in range(n)])


def stage(parts, g, chunk, wide, extra):
    groups = stage_bits(wide)
    shift = sum(groups[:g])
    ways = 1 << groups[g]
    chunks = wide >> (shift + groups[g])
    cols = parts[0].shape[1]
    got = [parts[0]] + [swap(parts[q], "wide", q << shift) for q in range(1, ways)]
    nxt = 1 << groups[g + 1] if g + 1 < len(groups) else 1
    shape = sds(((chunks // nxt) * chunk + (EXTRA if extra else 0), cols), BF16)
    return call(
        functools.partial(add_kernel, chunk, chunks, ways, nxt, extra),
        [shape] * nxt, 0, got, chunks * chunk * cols * ways,
        chunks * chunk * cols * 2 * (ways + 1), vmem=8,
    )


def scatter(parts, first, chunk, wide, extra):
    for g in range(first, len(stage_bits(wide))):
        parts = stage(parts, g, chunk, wide, extra)
    return parts[0]


def across(x):
    size = lax.axis_size("eight")
    return [x] + [swap(x, "eight", q) for q in range(1, size)]


def gather(centre, wide):
    groups = stage_bits(wide)
    have = {0: centre}
    shift = wide.bit_length() - 1
    for bits in reversed(groups):
        shift -= bits
        new = dict(have)
        for q in range(1, 1 << bits):
            for k, v in have.items():
                new[k ^ (q << shift)] = swap(v, "wide", q << shift)
        have = new
    return [have[k] for k in range(wide)]


def body(multipliers, gap, flexibility, dirichlet, side, powers, active):
    subs, rows, cols = multipliers.shape
    blocks = side.shape[1]
    wide = lax.axis_size("wide")
    eight = lax.axis_size("eight")
    count = wide * eight * subs
    chunk = rows // wide
    caps = (-(-subs * blocks * 9 // 16), -(-blocks * 3 // 4))
    away = [(i, (i + 1) % wide if i % 2 else (i - 1) % wide) for i in range(wide)]
    pairs_a = [(i, i ^ 1) for i in range(eight) if i ^ 1 < eight]
    pairs_b = [(i, i + 1 if i % 2 else i - 1) for i in range(1, eight - 1 + eight % 2)]
    info = jnp.stack([lax.axis_index("wide"), lax.axis_index("eight")]).astype(jnp.int32)
    tables = [
        lax.ppermute(side, "wide", away),
        lax.ppermute(side, "eight", pairs_a),
        lax.ppermute(side, "eight", pairs_b),
    ]
    lanes = 128
    floor = jnp.where(
        jnp.broadcast_to(active[..., None], active.shape + (lanes,)) == 1, 0.0, -jnp.inf
    ).astype(F32)

    full = sds((subs, rows, cols), F32)
    half = sds((subs, rows, cols), BF16)
    one = sds((rows, cols), BF16)
    few = [sds((cap, rows // blocks, cols), BF16) for cap in (caps[1], caps[1], caps[0])]
    part = sds(((wide // 2) * chunk, cols), BF16)
    message = sds(((wide // 2) * chunk + EXTRA, cols), BF16)
    stack = sds((ITERS, rows, cols), F32)
    mm = 2 * subs * rows * rows * cols
    op_bytes = 2 * subs * rows * rows
    arr = subs * rows * cols

    def search(step, sums, centres, packed, tables):
        mean, half_lam, lkeep, lsend = sums
        ins = [info] + (tables if packed else []) + [half_lam, flexibility]
        n_smem = len(ins) - 2
        outs = [half] + (few if packed else [one, one])
        spots = {}
        if step:
            ins.append(mean)
            if step > 1:
                spots = dict(anys=(len(ins),), aliases={len(ins): len(outs)})
                ins.append(centres)
            spots |= dict(any_outs=(len(outs),), scratch=[pltpu.SemaphoreType.DMA])
            outs = outs + [stack]
        sends = call(
            functools.partial(flex_kernel, step, packed), outs, n_smem, ins, mm,
            op_bytes + arr * 6, **spots,
        )
        if step:
            *sends, centres = sends
        lams = stage([lkeep, lsend], 0, chunk, wide, False)
        lams, sends = lax.optimization_barrier((lams, sends))
        own = scatter(lams, 1, chunk, wide, False)
        disp, za, zb = sends[:3]
        off = lax.ppermute(sends[3] if packed else disp, "wide", away)
        za = lax.ppermute(za, "eight", pairs_a)
        zb = lax.ppermute(zb, "eight", pairs_b)
        chip = swap(disp, "wide", 1)
        lam_parts = across(own)
        if not step:
            own, tables = lax.optimization_barrier((own, tables))
        direct, dkeep, dsend = call(
            functools.partial(direct_kernel, chunk, wide, eight, caps, packed), [half, message, message], 3,
            [info, side, powers, gap, disp, chip, off, za, zb, dirichlet, own],
            2 * mm, op_bytes + arr * 16,
            scratch=[pltpu.VMEM((rows, cols), F32), pltpu.VMEM((subs, rows, cols), BF16)],
        )
        dirs = stage([dkeep, dsend], 0, chunk, wide, True)
        dir_parts = across(scatter(dirs, 1, chunk, wide, True))
        centre, alpha = call(
            functools.partial(centre_kernel, chunk, eight, float(count)),
            [sds((chunk, cols), BF16), sds((8, cols), F32)], 0, dir_parts + lam_parts,
            chunk * cols * 10, chunk * cols * 20, vmem=8,
        )
        return (direct, alpha, gather(centre, wide)), centres, tables

    def update(step, lam, found, centres):
        direct, alpha, pieces = found
        ins = [info, lam, direct, alpha, floor[step], *pieces]
        kernel = functools.partial(update_kernel, chunk, wide, step, step == ITERS - 1)
        if step < ITERS - 1:
            outs = [full, sds((rows, cols), F32), half, part, part]
            return call(kernel, outs, 1, ins, arr * 6, arr * 16)
        return call(
            kernel, [full, stack], 1, ins + [centres], arr * 6, arr * 16,
            scratch=[
                pltpu.VMEM((subs, rows, cols), F32),
                pltpu.VMEM((rows, cols), F32),
                pltpu.SemaphoreType.DMA((wide * (subs + 1),)),
            ],
            anys=(len(ins),), any_outs=(0, 1), aliases={len(ins): 1},
        )

    sums = call(
        functools.partial(first_kernel, chunk, wide), [half, part, part], 1, [info, multipliers],
        arr * 2, arr * 8,
    )
    found, _, tables = search(0, [None, *sums], None, False, tables)

    def rest(packed, tables, found):
        alphas = [found[1][0]]
        lam, centres = multipliers, None
        for step in range(1, ITERS):
            lam, *sums = update(step - 1, lam, found, centres)
            found, centres, _ = search(step, sums, centres, packed, tables)
            alphas.append(found[1][0])
        lam, centres = update(ITERS - 1, lam, found, centres)
        return lam, jnp.stack(alphas), centres

    return lax.cond(
        found[1][1, 0] <= 0,
        functools.partial(rest, True),
        functools.partial(rest, False),
        tables, found,
    )


def solution(mesh):
    return jax.shard_map(
        body,
        mesh=mesh,
        in_specs=(
            P(("wide", "eight"), None, None),
            P(("wide", "eight"), None, None),
            P(("wide", "eight"), None, None),
            P(("wide", "eight"), None, None),
            P(("wide", "eight"), None),
            P(("wide", "eight")),
            P(None, ("wide", "eight"), None),
        ),
        out_specs=(P(("wide", "eight"), None, None), P(), P()),
        check_vma=False,
    )
```

```python
import functools

import jax
import jax.numpy as jnp
from jax import lax
from jax.experimental import pallas as pl
from jax.experimental.pallas import tpu as pltpu
from jax.sharding import PartitionSpec as P


ITERS = 3
EXTRA = 16
F32 = jnp.float32
BF16 = jnp.bfloat16
VMEM = pl.BlockSpec(memory_space=pltpu.VMEM)
HBM = pl.BlockSpec(memory_space=pltpu.HBM)
SMEM = pl.BlockSpec(memory_space=pltpu.SMEM)


def call(kernel, outs, n_smem, ins, flops, nbytes, scratch=(), vmem=16, hbm_ins=(), hbm_outs=(), aliases=None):
    return pl.pallas_call(
        kernel,
        out_shape=outs,
        in_specs=[
            SMEM if i < n_smem else HBM if i in hbm_ins else VMEM for i in range(len(ins))
        ],
        out_specs=[HBM if i in hbm_outs else VMEM for i in range(len(outs))],
        scratch_shapes=list(scratch),
        input_output_aliases=aliases or {},
        compiler_params=pltpu.CompilerParams(vmem_limit_bytes=vmem << 20),
        cost_estimate=pl.CostEstimate(flops=flops, bytes_accessed=nbytes, transcendentals=0),
    )(*ins)


def sds(shape, dtype):
    return jax.ShapeDtypeStruct(shape, dtype)


def stage_bits(size):
    total = size.bit_length() - 1
    groups = [1]
    left = total - 1
    while left > 0:
        take = 2 if left >= 2 else 1
        groups.append(take)
        left -= take
    return groups


def pack_products(inner, square, most):
    shape = (EXTRA, inner.shape[1])
    row = lax.broadcasted_iota(jnp.int32, shape, 0)
    ih = inner.astype(BF16).astype(F32)
    sh = square.astype(BF16).astype(F32)
    tile = jnp.zeros(shape, F32)
    for i, value in enumerate((ih, inner - ih, sh, square - sh, most)):
        tile = jnp.where(row == i, jnp.broadcast_to(value, shape), tile)
    return tile.astype(BF16)


def unpack_products(tiles):
    vals = []
    for tile in tiles:
        t = tile.astype(F32)
        vals.append((t[0:1] + t[1:2], t[2:3] + t[3:4], t[4:5]))
    return (
        tree([v[0] for v in vals]),
        tree([v[1] for v in vals]),
        functools.reduce(jnp.maximum, [v[2] for v in vals]),
    )


def tree(items):
    items = list(items)
    while len(items) > 1:
        items = [items[i] + items[i + 1] for i in range(0, len(items), 2)]
    return items[0]


def send_partial(chunk, wide, w, part, tile, keep_ref, send_ref):
    for k in range(wide):
        total = part(pl.ds(pl.multiple_of(jnp.bitwise_xor(w, k) * chunk, chunk), chunk))
        out = send_ref if k % 2 else keep_ref
        out[pl.ds((k // 2) * chunk, chunk), :] = total.astype(BF16)
    if tile is not None:
        tail = pl.ds((wide // 2) * chunk, EXTRA)
        keep_ref[tail, :] = tile
        send_ref[tail, :] = tile


def pack_blocks(table, row, face, source, disp_ref, out_ref, count):
    blocks = table.shape[1]
    height = disp_ref.shape[1] // blocks
    cap = out_ref.shape[0]

    def block(b, n):
        need = table[row, b] == face
        rows = pl.ds(pl.multiple_of(b * height, height), height)

        @pl.when(need & (n < cap))
        def _():
            out_ref[n] = disp_ref[source, rows, :]

        return n + need.astype(jnp.int32)

    return lax.fori_loop(0, blocks, block, count)


def send_halo(info, disp_ref, outs, tables):
    last = disp_ref.shape[0] - 1
    odd = jnp.bitwise_and(info[0], 1)
    zodd = jnp.bitwise_and(info[1], 1)
    za_ref, zb_ref = outs[:2]
    zero = jnp.int32(0)
    if not tables:
        za_ref[...] = disp_ref[(1 - zodd) * last]
        zb_ref[...] = disp_ref[zodd * last]
        return
    theirs, ta, tb = tables
    count = zero
    for s in range(last + 1):
        count = pack_blocks(theirs, s, odd, s, disp_ref, outs[2], count)
    pack_blocks(ta, zodd * last, 3 - zodd, (1 - zodd) * last, disp_ref, za_ref, zero)
    pack_blocks(tb, (1 - zodd) * last, 2 + zodd, zodd * last, disp_ref, zb_ref, zero)


def first_kernel(chunk, wide, info, lam_ref, half_ref, keep_ref, send_ref):
    subs = lam_ref.shape[0]
    half_ref[...] = lam_ref[...].astype(BF16)
    send_partial(
        chunk, wide, info[0], lambda rows: tree([lam_ref[s, rows, :] for s in range(subs)]),
        None, keep_ref, send_ref,
    )


def flex_kernel(step, packed, info, *refs):
    tables, refs = refs[: 3 * packed], refs[3 * packed :]
    half_ref, flex_ref, *refs = refs
    if step:
        mean_ref, *refs = refs
        if step > 1:
            refs = refs[1:]
        disp_ref, *outs, stack_ref, sem = refs
        copy = pltpu.make_async_copy(mean_ref, stack_ref.at[step - 1], sem)
        copy.start()
    else:
        disp_ref, *outs = refs

    def product(s, carry):
        disp_ref[s] = jnp.dot(
            flex_ref[s], half_ref[s], preferred_element_type=F32
        ).astype(BF16)
        return carry

    lax.fori_loop(0, half_ref.shape[0], product, 0)
    send_halo(info, disp_ref, outs, tables)
    if step:
        copy.wait()


def update_kernel(chunk, wide, step, last, info, lam_ref, dir_ref, alpha_ref, floor_ref, *refs):
    centre_refs = refs[:wide]
    refs = refs[wide:]
    if last:
        _, new_ref, stack_ref, mean_ref, sems = refs
    else:
        new_ref, mean_ref, half_ref, keep_ref, send_ref = refs
    w = info[0]
    subs, _, cols = lam_ref.shape
    alpha = jnp.broadcast_to(alpha_ref[0:1, :], (chunk, cols))
    copies = []
    for k in range(wide):
        rows = pl.ds(pl.multiple_of(jnp.bitwise_xor(w, k) * chunk, chunk), chunk)
        centre = centre_refs[k][...].astype(F32)
        mean_ref[rows, :] = centre
        total = None
        for s in range(subs):
            trial = lam_ref[s, rows, :] + alpha * dir_ref[s, rows, :].astype(F32)
            low = floor_ref[s, rows, :]
            low = jnp.concatenate([low] * (cols // low.shape[1]), axis=1)
            new = jnp.maximum(trial - centre, low)
            new_ref[s, rows, :] = new
            if not last:
                half_ref[s, rows, :] = new.astype(BF16)
                total = new if total is None else total + new
        if last:
            copies.append(
                pltpu.make_async_copy(
                    mean_ref.at[rows, :], stack_ref.at[step, rows, :], sems.at[k]
                )
            )
            copies[-1].start()
        else:
            out = send_ref if k % 2 else keep_ref
            out[pl.ds((k // 2) * chunk, chunk), :] = total.astype(BF16)
    for copy in copies:
        copy.wait()


def direct_kernel(chunk, wide, eight, caps, packed, info, side, powers, gap_ref, disp_ref, chip_ref, off_ref, za_ref, zb_ref, diri_ref, after_ref, dir_ref, keep_ref, send_ref, jump, work):
    w, z = info[0], info[1]
    odd = jnp.bitwise_and(w, 1)
    zodd = jnp.bitwise_and(z, 1)
    subs, rows_all, cols = gap_ref.shape
    blocks = side.shape[1]
    height = rows_all // blocks
    counts = (jnp.int32(0),) * 3
    for s in range(subs):

        def block(b, ns, s=s):
            n, above, below = ns
            face = side[s, b]
            rows = pl.ds(pl.multiple_of(b * height, height), height)

            def put(source):
                value = gap_ref[s, rows, :] - (
                    disp_ref[s, rows, :].astype(F32) - source.astype(F32)
                )
                jump[s, rows, :] = value
                work[s, rows, :] = value.astype(BF16)

            def take(ref, slot):
                if packed:
                    return ref[jnp.minimum(slot, ref.shape[0] - 1)]
                return ref[s, rows, :] if len(ref.shape) == 3 else ref[rows, :]

            pl.when(face == odd)(lambda: put(chip_ref[s, rows, :]))
            away = face == 1 - odd
            pl.when(away)(lambda: put(take(off_ref, n)))
            n = n + away.astype(jnp.int32)
            if s + 1 < subs:
                pl.when(face == 2)(lambda: put(disp_ref[s + 1, rows, :]))
            else:
                pl.when((face == 2) & (zodd == 0))(lambda: put(take(za_ref, above)))
                pl.when((face == 2) & (zodd == 1))(lambda: put(take(zb_ref, above)))
                above = above + (face == 2).astype(jnp.int32)
            if s > 0:
                pl.when(face == 3)(lambda: put(disp_ref[s - 1, rows, :]))
            else:
                pl.when((face == 3) & (zodd == 1))(lambda: put(take(za_ref, below)))
                pl.when((face == 3) & (zodd == 0))(lambda: put(take(zb_ref, below)))
                below = below + (face == 3).astype(jnp.int32)
            return n, above, below

        counts = lax.fori_loop(0, blocks, block, counts)

    def apply(s, sums):
        def level(i, carry):
            work[s] = jnp.dot(
                diri_ref[s], work[s], preferred_element_type=F32
            ).astype(BF16)
            return carry

        lax.fori_loop(0, powers[s], level, 0)
        direct = work[s]
        dir_ref[s] = direct
        dfloat = direct.astype(F32)
        split = (rows_all // 8, 8, cols)
        return (
            sums[0] + jnp.sum((jump[s] * dfloat).reshape(split), axis=0),
            sums[1] + jnp.sum((dfloat * dfloat).reshape(split), axis=0),
        )

    zeros = jnp.zeros((8, cols), F32)
    inner, square = lax.fori_loop(0, subs, apply, (zeros, zeros))
    n, above, below = counts
    excess = jnp.maximum(
        n - caps[0],
        jnp.maximum(
            jnp.where(z < eight - 1, above, 0) - caps[1], jnp.where(z > 0, below, 0) - caps[1]
        ),
    )
    tile = pack_products(
        jnp.sum(inner, axis=0, keepdims=True),
        jnp.sum(square, axis=0, keepdims=True),
        jnp.broadcast_to(excess.astype(F32), (1, cols)),
    )
    send_partial(
        chunk, wide, w, lambda rows: tree([work[s, rows, :].astype(F32) for s in range(subs)]),
        tile, keep_ref, send_ref,
    )


def add_kernel(chunk, chunks, ways_in, ways_out, extra, *refs):
    ins, outs = refs[:ways_in], refs[ways_in:]
    for c in range(chunks):
        rows = pl.ds(c * chunk, chunk)
        total = tree([r[rows, :].astype(F32) for r in ins]).astype(BF16)
        outs[c % ways_out][pl.ds((c // ways_out) * chunk, chunk), :] = total
    if extra:
        tail = pl.ds(chunks * chunk, EXTRA)
        tiles = [r[tail, :] for r in ins]
        tile = pack_products(*unpack_products(tiles))
        for o in outs:
            o[pl.ds((chunks // ways_out) * chunk, EXTRA), :] = tile


def centre_kernel(chunk, ways, count, *refs):
    dirs, lams = refs[:ways], refs[ways:-2]
    centre_ref, alpha_ref = refs[-2:]
    rows = pl.ds(0, chunk)
    tail = pl.ds(chunk, EXTRA)
    inner, square, most = unpack_products([r[tail, :] for r in dirs])
    alpha = inner / (square + 1e-06)
    row = lax.broadcasted_iota(jnp.int32, alpha_ref.shape, 0)
    alpha_ref[...] = jnp.where(
        row == 0, jnp.broadcast_to(alpha, row.shape), jnp.broadcast_to(most, row.shape)
    )
    dsum = tree([r[rows, :].astype(F32) for r in dirs])
    lsum = tree([r[rows, :].astype(F32) for r in lams])
    centre_ref[...] = ((lsum + alpha * dsum) / count).astype(BF16)


def swap(x, axis, mask):
    n = lax.axis_size(axis)
    return lax.ppermute(x, axis, [(i, i ^ mask) for i in range(n)])


def stage(parts, g, chunk, wide, extra):
    groups = stage_bits(wide)
    shift = sum(groups[:g])
    ways = 1 << groups[g]
    chunks = wide >> (shift + groups[g])
    cols = parts[0].shape[1]
    got = [parts[0]] + [swap(parts[q], "wide", q << shift) for q in range(1, ways)]
    nxt = 1 << groups[g + 1] if g + 1 < len(groups) else 1
    shape = sds(((chunks // nxt) * chunk + (EXTRA if extra else 0), cols), BF16)
    return call(
        functools.partial(add_kernel, chunk, chunks, ways, nxt, extra),
        [shape] * nxt, 0, got, chunks * chunk * cols * ways,
        chunks * chunk * cols * 2 * (ways + 1), vmem=8,
    )


def scatter(parts, first, chunk, wide, extra):
    for g in range(first, len(stage_bits(wide))):
        parts = stage(parts, g, chunk, wide, extra)
    return parts[0]


def across(x):
    size = lax.axis_size("eight")
    return [x] + [swap(x, "eight", q) for q in range(1, size)]


def across_steps(x, chunk):
    size = lax.axis_size("eight")
    q = 1
    while 2 * q < size:
        (x,) = call(
            functools.partial(add_kernel, chunk, 1, 2, 1, False), [sds(x.shape, BF16)], 0,
            [x, swap(x, "eight", q)], 2 * x.size, 6 * x.size, vmem=8,
        )
        q *= 2
    return [x, swap(x, "eight", q)]


def gather(centre, wide):
    groups = stage_bits(wide)
    have = {0: centre}
    shift = wide.bit_length() - 1
    for bits in reversed(groups):
        shift -= bits
        new = dict(have)
        for q in range(1, 1 << bits):
            for k, v in have.items():
                new[k ^ (q << shift)] = swap(v, "wide", q << shift)
        have = new
    return [have[k] for k in range(wide)]


def body(multipliers, gap, flexibility, dirichlet, side, powers, active):
    subs, rows, cols = multipliers.shape
    blocks = side.shape[1]
    wide = lax.axis_size("wide")
    eight = lax.axis_size("eight")
    count = wide * eight * subs
    chunk = rows // wide
    caps = (-(-subs * blocks * 9 // 16), -(-blocks * 3 // 4))
    away = [(i, (i + 1) % wide if i % 2 else (i - 1) % wide) for i in range(wide)]
    pairs_a = [(i, i ^ 1) for i in range(eight) if i ^ 1 < eight]
    pairs_b = [(i, i + 1 if i % 2 else i - 1) for i in range(1, eight - 1 + eight % 2)]
    info = jnp.stack([lax.axis_index("wide"), lax.axis_index("eight")]).astype(jnp.int32)
    tables = [
        lax.ppermute(side, "wide", away),
        lax.ppermute(side, "eight", pairs_a),
        lax.ppermute(side, "eight", pairs_b),
    ]

    def low_of(flags):
        wide_flags = jnp.broadcast_to(flags[..., None], flags.shape + (128,))
        return jnp.where(wide_flags == 1, 0.0, -jnp.inf).astype(F32)

    full = sds((subs, rows, cols), F32)
    half = sds((subs, rows, cols), BF16)
    one = sds((rows, cols), BF16)
    few = [sds((cap, rows // blocks, cols), BF16) for cap in (caps[1], caps[1], caps[0])]
    part = sds(((wide // 2) * chunk, cols), BF16)
    message = sds(((wide // 2) * chunk + EXTRA, cols), BF16)
    stack = sds((ITERS, rows, cols), F32)
    mm = 2 * subs * rows * rows * cols
    op_bytes = 2 * subs * rows * rows
    arr = subs * rows * cols

    def search(step, sums, centres, packed):
        mean, half_lam, lkeep, lsend = sums
        ins = [info] + (tables if packed else []) + [half_lam, flexibility]
        n_smem = len(ins) - 2
        outs = [half] + (few if packed else [one, one])
        spots = {}
        if step:
            ins.append(mean)
            if step > 1:
                spots = dict(hbm_ins=(len(ins),), aliases={len(ins): len(outs)})
                ins.append(centres)
            spots |= dict(hbm_outs=(len(outs),), scratch=[pltpu.SemaphoreType.DMA])
            outs = outs + [stack]
        sends = call(
            functools.partial(flex_kernel, step, packed), outs, n_smem, ins, mm,
            op_bytes + arr * 6, **spots,
        )
        if step:
            *sends, centres = sends
        lams = stage([lkeep, lsend], 0, chunk, wide, False)
        lams, sends = lax.optimization_barrier((lams, sends))
        own = scatter(lams, 1, chunk, wide, False)
        disp, za, zb = sends[:3]
        off = lax.ppermute(sends[3] if packed else disp, "wide", away)
        za = lax.ppermute(za, "eight", pairs_a)
        zb = lax.ppermute(zb, "eight", pairs_b)
        chip = swap(disp, "wide", 1)
        lam_parts = across_steps(own, chunk)
        direct, dkeep, dsend = call(
            functools.partial(direct_kernel, chunk, wide, eight, caps, packed), [half, message, message], 3,
            [info, side, powers, gap, disp, chip, off, za, zb, dirichlet, own],
            2 * mm, op_bytes + arr * 16,
            scratch=[pltpu.VMEM((subs, rows, cols), F32), pltpu.VMEM((subs, rows, cols), BF16)],
        )
        dirs = stage([dkeep, dsend], 0, chunk, wide, True)
        dir_parts = across(scatter(dirs, 1, chunk, wide, True))
        centre, alpha = call(
            functools.partial(centre_kernel, chunk, eight, float(count)),
            [sds((chunk, cols), BF16), sds((8, cols), F32)], 0, dir_parts + lam_parts,
            chunk * cols * 10, chunk * cols * 20, vmem=8,
        )
        return (direct, alpha, gather(centre, wide)), centres

    def update(step, lam, found, centres, low):
        direct, alpha, pieces = found
        ins = [info, lam, direct, alpha, low, *pieces]
        kernel = functools.partial(update_kernel, chunk, wide, step, step == ITERS - 1)
        if step < ITERS - 1:
            outs = [full, sds((rows, cols), F32), half, part, part]
            return call(kernel, outs, 1, ins, arr * 6, arr * 16)
        return call(
            kernel, [full, stack], 1, ins + [centres], arr * 6, arr * 16,
            scratch=[pltpu.VMEM((rows, cols), F32), pltpu.SemaphoreType.DMA((wide,))],
            hbm_ins=(len(ins),), hbm_outs=(1,), aliases={len(ins): 1},
        )

    def start():
        return call(
            functools.partial(first_kernel, chunk, wide), [half, part, part], 1,
            [info, multipliers], arr * 2, arr * 8,
        )

    first, _ = search(0, [None, *start()], None, True)

    def rest(packed, found):
        alphas = [found[1][0]]
        lam, centres = multipliers, None
        for step in range(1, ITERS):
            lam, *sums = update(step - 1, lam, found, centres, low_of(active[step - 1]))
            found, centres = search(step, sums, centres, packed)
            alphas.append(found[1][0])
        lam, centres = update(ITERS - 1, lam, found, centres, low_of(active[ITERS - 1]))
        return lam, jnp.stack(alphas), centres

    def again(found):
        found, _ = search(0, [None, *start()], None, False)
        return rest(False, found)

    return lax.cond(first[1][1, 0] <= 0, functools.partial(rest, True), again, first)


def solution(mesh):
    return jax.shard_map(
        body,
        mesh=mesh,
        in_specs=(
            P(("wide", "eight"), None, None),
            P(("wide", "eight"), None, None),
            P(("wide", "eight"), None, None),
            P(("wide", "eight"), None, None),
            P(("wide", "eight"), None),
            P(("wide", "eight")),
            P(None, ("wide", "eight"), None),
        ),
        out_specs=(P(("wide", "eight"), None, None), P(), P()),
        check_vma=False,
    )
```

```python
import functools

import jax
import jax.numpy as jnp
from jax import lax
from jax.experimental import pallas as pl
from jax.experimental.pallas import tpu as pltpu
from jax.sharding import PartitionSpec as P


ITERS = 3
EXTRA = 16
F32 = jnp.float32
BF16 = jnp.bfloat16
VMEM = pl.BlockSpec(memory_space=pltpu.VMEM)
HBM = pl.BlockSpec(memory_space=pltpu.HBM)
SMEM = pl.BlockSpec(memory_space=pltpu.SMEM)


def call(kernel, outs, n_smem, ins, flops, nbytes, scratch=(), vmem=16, hbm_ins=(), hbm_outs=(), aliases=None):
    return pl.pallas_call(
        kernel,
        out_shape=outs,
        in_specs=[
            SMEM if i < n_smem else HBM if i in hbm_ins else VMEM for i in range(len(ins))
        ],
        out_specs=[HBM if i in hbm_outs else VMEM for i in range(len(outs))],
        scratch_shapes=list(scratch),
        input_output_aliases=aliases or {},
        compiler_params=pltpu.CompilerParams(vmem_limit_bytes=vmem << 20),
        cost_estimate=pl.CostEstimate(flops=flops, bytes_accessed=nbytes, transcendentals=0),
    )(*ins)


def sds(shape, dtype):
    return jax.ShapeDtypeStruct(shape, dtype)


def stage_bits(size):
    total = size.bit_length() - 1
    groups = [1]
    left = total - 1
    while left > 0:
        take = 2 if left >= 2 else 1
        groups.append(take)
        left -= take
    return groups


def pack_products(inner, square, most):
    shape = (EXTRA, inner.shape[1])
    row = lax.broadcasted_iota(jnp.int32, shape, 0)
    ih = inner.astype(BF16).astype(F32)
    sh = square.astype(BF16).astype(F32)
    tile = jnp.zeros(shape, F32)
    for i, value in enumerate((ih, inner - ih, sh, square - sh, most)):
        tile = jnp.where(row == i, jnp.broadcast_to(value, shape), tile)
    return tile.astype(BF16)


def unpack_products(tiles):
    vals = []
    for tile in tiles:
        t = tile.astype(F32)
        vals.append((t[0:1] + t[1:2], t[2:3] + t[3:4], t[4:5]))
    return (
        tree([v[0] for v in vals]),
        tree([v[1] for v in vals]),
        functools.reduce(jnp.maximum, [v[2] for v in vals]),
    )


def tree(items):
    items = list(items)
    while len(items) > 1:
        items = [items[i] + items[i + 1] for i in range(0, len(items), 2)]
    return items[0]


def send_partial(chunk, wide, w, part, tile, keep_ref, send_ref):
    for k in range(wide):
        total = part(pl.ds(pl.multiple_of(jnp.bitwise_xor(w, k) * chunk, chunk), chunk))
        out = send_ref if k % 2 else keep_ref
        out[pl.ds((k // 2) * chunk, chunk), :] = total.astype(BF16)
    if tile is not None:
        tail = pl.ds((wide // 2) * chunk, EXTRA)
        keep_ref[tail, :] = tile
        send_ref[tail, :] = tile


def pack_blocks(table, row, face, source, disp_ref, outs, count):
    blocks = table.shape[1]
    height = disp_ref.shape[1] // blocks

    def block(b, n):
        need = table[row, b] == face
        rows = pl.ds(pl.multiple_of(b * height, height), height)
        low = 0
        for out_ref in outs:
            high = low + out_ref.shape[0]

            @pl.when(need & (n >= low) & (n < high))
            def _(out_ref=out_ref, low=low):
                out_ref[n - low] = disp_ref[source, rows, :]

            low = high
        return n + need.astype(jnp.int32)

    return lax.fori_loop(0, blocks, block, count)


def send_halo(info, disp_ref, outs, tables):
    last = disp_ref.shape[0] - 1
    odd = jnp.bitwise_and(info[0], 1)
    zodd = jnp.bitwise_and(info[1], 1)
    za_ref, zb_ref = outs[:2]
    zero = jnp.int32(0)
    if not tables:
        za_ref[...] = disp_ref[(1 - zodd) * last]
        zb_ref[...] = disp_ref[zodd * last]
        return
    theirs, ta, tb = tables
    count = zero
    for s in range(last + 1):
        count = pack_blocks(theirs, s, odd, s, disp_ref, outs[2:], count)
    pack_blocks(ta, zodd * last, 3 - zodd, (1 - zodd) * last, disp_ref, [za_ref], zero)
    pack_blocks(tb, (1 - zodd) * last, 2 + zodd, zodd * last, disp_ref, [zb_ref], zero)


def open_kernel(chunk, wide, info, lam_ref, flex_ref, keep_ref, send_ref, disp_ref, flex, half, sems):
    subs = lam_ref.shape[0]

    def fetch(s):
        return pltpu.make_async_copy(flex_ref.at[s], flex.at[s], sems.at[s])

    for s in range(subs):
        fetch(s).start()
    half[...] = lam_ref[...].astype(BF16)
    send_partial(
        chunk, wide, info[0], lambda rows: tree([lam_ref[s, rows, :] for s in range(subs)]),
        None, keep_ref, send_ref,
    )

    def product(s, carry):
        fetch(s).wait()
        disp_ref[s] = jnp.dot(flex[s], half[s], preferred_element_type=F32).astype(BF16)
        return carry

    lax.fori_loop(0, subs, product, 0)


def halo_kernel(packed, info, *refs):
    tables, (disp_ref, *outs) = refs[: 3 * packed], refs[3 * packed :]
    send_halo(info, disp_ref, outs, tables)


def flex_kernel(step, packed, info, *refs):
    tables, refs = refs[: 3 * packed], refs[3 * packed :]
    half_ref, flex_ref, mean_ref, *refs = refs
    if step > 1:
        refs = refs[1:]
    disp_ref, *outs, stack_ref, sem = refs
    copy = pltpu.make_async_copy(mean_ref, stack_ref.at[step - 1], sem)
    copy.start()

    def product(s, carry):
        disp_ref[s] = jnp.dot(
            flex_ref[s], half_ref[s], preferred_element_type=F32
        ).astype(BF16)
        return carry

    lax.fori_loop(0, half_ref.shape[0], product, 0)
    send_halo(info, disp_ref, outs, tables)
    copy.wait()


def update_kernel(chunk, wide, step, last, info, lam_ref, dir_ref, alpha_ref, floor_ref, *refs):
    centre_refs = refs[:wide]
    refs = refs[wide:]
    if last:
        _, lam_out, stack_ref, new_ref, mean_ref, sems = refs
    else:
        new_ref, mean_ref, half_ref, keep_ref, send_ref = refs
    w = info[0]
    subs, _, cols = lam_ref.shape
    alpha = jnp.broadcast_to(alpha_ref[0:1, :], (chunk, cols))
    copies = []

    def send(src, dst):
        copies.append(pltpu.make_async_copy(src, dst, sems.at[len(copies)]))
        copies[-1].start()

    for k in range(wide):
        rows = pl.ds(pl.multiple_of(jnp.bitwise_xor(w, k) * chunk, chunk), chunk)
        centre = centre_refs[k][...].astype(F32)
        mean_ref[rows, :] = centre
        total = None
        for s in range(subs):
            trial = lam_ref[s, rows, :] + alpha * dir_ref[s, rows, :].astype(F32)
            low = floor_ref[s, rows, :]
            low = jnp.concatenate([low] * (cols // low.shape[1]), axis=1)
            new = jnp.maximum(trial - centre, low)
            new_ref[s, rows, :] = new
            if last:
                send(new_ref.at[s, rows, :], lam_out.at[s, rows, :])
            else:
                half_ref[s, rows, :] = new.astype(BF16)
                total = new if total is None else total + new
        if last:
            send(mean_ref.at[rows, :], stack_ref.at[step, rows, :])
        else:
            out = send_ref if k % 2 else keep_ref
            out[pl.ds((k // 2) * chunk, chunk), :] = total.astype(BF16)
    for copy in copies:
        copy.wait()


def direct_kernel(chunk, wide, eight, caps, packed, info, side, powers, gap_ref, disp_ref, chip_ref, za_ref, zb_ref, *refs):
    offs, refs = refs[: 1 + packed], refs[1 + packed :]
    diri_ref, _, dir_ref, keep_ref, send_ref, jump, work = refs
    w, z = info[0], info[1]
    odd = jnp.bitwise_and(w, 1)
    zodd = jnp.bitwise_and(z, 1)
    subs, rows_all, cols = gap_ref.shape
    blocks = side.shape[1]
    height = rows_all // blocks
    counts = (jnp.int32(0),) * 3
    for s in range(subs):

        def block(b, ns, s=s):
            n, above, below = ns
            face = side[s, b]
            rows = pl.ds(pl.multiple_of(b * height, height), height)

            def put(source):
                value = gap_ref[s, rows, :] - (
                    disp_ref[s, rows, :].astype(F32) - source.astype(F32)
                )
                jump[s, rows, :] = value
                work[s, rows, :] = value.astype(BF16)

            def take(ref, slot):
                if packed:
                    return ref[jnp.minimum(slot, ref.shape[0] - 1)]
                return ref[s, rows, :] if len(ref.shape) == 3 else ref[rows, :]

            pl.when(face == odd)(lambda: put(chip_ref[s, rows, :]))
            away = face == 1 - odd
            half = offs[0].shape[0] if packed else subs * blocks
            pl.when(away & (n < half))(lambda: put(take(offs[0], n)))
            if packed:
                pl.when(away & (n >= half))(lambda: put(take(offs[1], n - half)))
            n = n + away.astype(jnp.int32)
            if s + 1 < subs:
                pl.when(face == 2)(lambda: put(disp_ref[s + 1, rows, :]))
            else:
                pl.when((face == 2) & (zodd == 0))(lambda: put(take(za_ref, above)))
                pl.when((face == 2) & (zodd == 1))(lambda: put(take(zb_ref, above)))
                above = above + (face == 2).astype(jnp.int32)
            if s > 0:
                pl.when(face == 3)(lambda: put(disp_ref[s - 1, rows, :]))
            else:
                pl.when((face == 3) & (zodd == 1))(lambda: put(take(za_ref, below)))
                pl.when((face == 3) & (zodd == 0))(lambda: put(take(zb_ref, below)))
                below = below + (face == 3).astype(jnp.int32)
            return n, above, below

        counts = lax.fori_loop(0, blocks, block, counts)

    def apply(s, sums):
        def level(i, carry):
            work[s] = jnp.dot(
                diri_ref[s], work[s], preferred_element_type=F32
            ).astype(BF16)
            return carry

        lax.fori_loop(0, powers[s], level, 0)
        direct = work[s]
        dir_ref[s] = direct
        dfloat = direct.astype(F32)
        split = (rows_all // 8, 8, cols)
        return (
            sums[0] + jnp.sum((jump[s] * dfloat).reshape(split), axis=0),
            sums[1] + jnp.sum((dfloat * dfloat).reshape(split), axis=0),
        )

    zeros = jnp.zeros((8, cols), F32)
    inner, square = lax.fori_loop(0, subs, apply, (zeros, zeros))
    n, above, below = counts
    excess = jnp.maximum(
        n - caps[0],
        jnp.maximum(
            jnp.where(z < eight - 1, above, 0) - caps[1], jnp.where(z > 0, below, 0) - caps[1]
        ),
    )
    tile = pack_products(
        jnp.sum(inner, axis=0, keepdims=True),
        jnp.sum(square, axis=0, keepdims=True),
        jnp.broadcast_to(excess.astype(F32), (1, cols)),
    )
    send_partial(
        chunk, wide, w, lambda rows: tree([work[s, rows, :].astype(F32) for s in range(subs)]),
        tile, keep_ref, send_ref,
    )


def add_kernel(chunk, chunks, ways_in, ways_out, extra, *refs):
    ins, outs = refs[:ways_in], refs[ways_in:]
    for c in range(chunks):
        rows = pl.ds(c * chunk, chunk)
        total = tree([r[rows, :].astype(F32) for r in ins]).astype(BF16)
        outs[c % ways_out][pl.ds((c // ways_out) * chunk, chunk), :] = total
    if extra:
        tail = pl.ds(chunks * chunk, EXTRA)
        tiles = [r[tail, :] for r in ins]
        tile = pack_products(*unpack_products(tiles))
        for o in outs:
            o[pl.ds((chunks // ways_out) * chunk, EXTRA), :] = tile


def centre_kernel(chunk, ways, count, *refs):
    dirs, lams = refs[:ways], refs[ways:-2]
    centre_ref, alpha_ref = refs[-2:]
    rows = pl.ds(0, chunk)
    tail = pl.ds(chunk, EXTRA)
    inner, square, most = unpack_products([r[tail, :] for r in dirs])
    alpha = inner / (square + 1e-06)
    row = lax.broadcasted_iota(jnp.int32, alpha_ref.shape, 0)
    alpha_ref[...] = jnp.where(
        row == 0, jnp.broadcast_to(alpha, row.shape), jnp.broadcast_to(most, row.shape)
    )
    dsum = tree([r[rows, :].astype(F32) for r in dirs])
    lsum = tree([r[rows, :].astype(F32) for r in lams])
    centre_ref[...] = ((lsum + alpha * dsum) / count).astype(BF16)


def swap(x, axis, mask):
    n = lax.axis_size(axis)
    return lax.ppermute(x, axis, [(i, i ^ mask) for i in range(n)])


def stage(parts, g, chunk, wide, extra):
    groups = stage_bits(wide)
    shift = sum(groups[:g])
    ways = 1 << groups[g]
    chunks = wide >> (shift + groups[g])
    cols = parts[0].shape[1]
    got = [parts[0]] + [swap(parts[q], "wide", q << shift) for q in range(1, ways)]
    nxt = 1 << groups[g + 1] if g + 1 < len(groups) else 1
    shape = sds(((chunks // nxt) * chunk + (EXTRA if extra else 0), cols), BF16)
    return call(
        functools.partial(add_kernel, chunk, chunks, ways, nxt, extra),
        [shape] * nxt, 0, got, chunks * chunk * cols * ways,
        chunks * chunk * cols * 2 * (ways + 1), vmem=8,
    )


def scatter(parts, first, chunk, wide, extra):
    for g in range(first, len(stage_bits(wide))):
        parts = stage(parts, g, chunk, wide, extra)
    return parts[0]


def across(x):
    size = lax.axis_size("eight")
    return [x] + [swap(x, "eight", q) for q in range(1, size)]


def across_steps(x, chunk):
    size = lax.axis_size("eight")
    q = 1
    while 2 * q < size:
        (x,) = call(
            functools.partial(add_kernel, chunk, 1, 2, 1, False), [sds(x.shape, BF16)], 0,
            [x, swap(x, "eight", q)], 2 * x.size, 6 * x.size, vmem=8,
        )
        q *= 2
    return [x, swap(x, "eight", q)]


def gather(centre, wide):
    groups = stage_bits(wide)
    have = {0: centre}
    shift = wide.bit_length() - 1
    for bits in reversed(groups):
        shift -= bits
        new = dict(have)
        for q in range(1, 1 << bits):
            for k, v in have.items():
                new[k ^ (q << shift)] = swap(v, "wide", q << shift)
        have = new
    return [have[k] for k in range(wide)]


def body(multipliers, gap, flexibility, dirichlet, side, powers, active):
    subs, rows, cols = multipliers.shape
    blocks = side.shape[1]
    wide = lax.axis_size("wide")
    eight = lax.axis_size("eight")
    count = wide * eight * subs
    chunk = rows // wide
    caps = (-(-subs * blocks * 9 // 16), -(-blocks * 3 // 4))
    away = [(i, (i + 1) % wide if i % 2 else (i - 1) % wide) for i in range(wide)]
    pairs_a = [(i, i ^ 1) for i in range(eight) if i ^ 1 < eight]
    pairs_b = [(i, i + 1 if i % 2 else i - 1) for i in range(1, eight - 1 + eight % 2)]
    info = jnp.stack([lax.axis_index("wide"), lax.axis_index("eight")]).astype(jnp.int32)
    tables = [
        lax.ppermute(side, "wide", away),
        lax.ppermute(side, "eight", pairs_a),
        lax.ppermute(side, "eight", pairs_b),
    ]

    def low_of(flags):
        wide_flags = jnp.broadcast_to(flags[..., None], flags.shape + (128,))
        return jnp.where(wide_flags == 1, 0.0, -jnp.inf).astype(F32)

    full = sds((subs, rows, cols), F32)
    half = sds((subs, rows, cols), BF16)
    one = sds((rows, cols), BF16)
    few = [sds((cap, rows // blocks, cols), BF16) for cap in (caps[1], caps[1], -(-caps[0] // 2), caps[0] // 2)]
    part = sds(((wide // 2) * chunk, cols), BF16)
    message = sds(((wide // 2) * chunk + EXTRA, cols), BF16)
    stack = sds((ITERS, rows, cols), F32)
    mm = 2 * subs * rows * rows * cols
    op_bytes = 2 * subs * rows * rows
    arr = subs * rows * cols

    def search(step, sums, centres, packed):
        head = [info] + (tables if packed else [])
        outs = few if packed else [one, one]
        if step:
            mean, half_lam, lkeep, lsend = sums
            ins = head + [half_lam, flexibility, mean] + ([centres] if step > 1 else [])
            *sends, centres = call(
                functools.partial(flex_kernel, step, packed), [half, *outs, stack], len(head), ins,
                mm, op_bytes + arr * 6, scratch=[pltpu.SemaphoreType.DMA],
                hbm_ins=(len(head) + 3,), hbm_outs=(len(outs) + 1,),
                aliases={len(head) + 3: len(outs) + 1} if step > 1 else None,
            )
        else:
            lkeep, lsend, disp = call(
                functools.partial(open_kernel, chunk, wide), [part, part, half], 1,
                [info, multipliers, flexibility], mm, op_bytes + arr * 6,
                scratch=[
                    pltpu.VMEM((subs, rows, rows), BF16),
                    pltpu.VMEM((subs, rows, cols), BF16),
                    pltpu.SemaphoreType.DMA((subs,)),
                ],
                hbm_ins=(2,),
            )
            sends = [disp, *call(
                functools.partial(halo_kernel, packed), outs, len(head), head + [disp],
                arr, arr * 4, vmem=8,
            )]
        lams = stage([lkeep, lsend], 0, chunk, wide, False)
        lams, sends = lax.optimization_barrier((lams, sends))
        disp, za, zb = sends[:3]
        offs = sends[3:] if packed else [disp]
        if packed:
            offs[0] = lax.ppermute(offs[0], "wide", away)
        own = scatter(lams, 1, chunk, wide, False)
        offs[-1] = lax.ppermute(offs[-1], "wide", away)
        za = lax.ppermute(za, "eight", pairs_a)
        zb = lax.ppermute(zb, "eight", pairs_b)
        chip = swap(disp, "wide", 1)
        lam_parts = across_steps(own, chunk)
        direct, dkeep, dsend = call(
            functools.partial(direct_kernel, chunk, wide, eight, caps, packed), [half, message, message], 3,
            [info, side, powers, gap, disp, chip, za, zb, *offs, dirichlet, own],
            2 * mm, op_bytes + arr * 16,
            scratch=[pltpu.VMEM((subs, rows, cols), F32), pltpu.VMEM((subs, rows, cols), BF16)],
        )
        dirs = stage([dkeep, dsend], 0, chunk, wide, True)
        dir_parts = across(scatter(dirs, 1, chunk, wide, True))
        centre, alpha = call(
            functools.partial(centre_kernel, chunk, eight, float(count)),
            [sds((chunk, cols), BF16), sds((8, cols), F32)], 0, dir_parts + lam_parts,
            chunk * cols * 10, chunk * cols * 20, vmem=8,
        )
        return (direct, alpha, gather(centre, wide)), centres

    def update(step, lam, found, centres, low):
        direct, alpha, pieces = found
        ins = [info, lam, direct, alpha, low, *pieces]
        kernel = functools.partial(update_kernel, chunk, wide, step, step == ITERS - 1)
        if step < ITERS - 1:
            outs = [full, sds((rows, cols), F32), half, part, part]
            return call(kernel, outs, 1, ins, arr * 6, arr * 16)
        return call(
            kernel, [full, stack], 1, ins + [centres], arr * 6, arr * 16,
            scratch=[
                pltpu.VMEM((subs, rows, cols), F32),
                pltpu.VMEM((rows, cols), F32),
                pltpu.SemaphoreType.DMA((wide * (subs + 1),)),
            ],
            hbm_ins=(len(ins),), hbm_outs=(0, 1), aliases={len(ins): 1},
        )

    first, _ = search(0, None, None, True)

    def rest(packed, found):
        alphas = [found[1][0]]
        lam, centres = multipliers, None
        for step in range(1, ITERS):
            lam, *sums = update(step - 1, lam, found, centres, low_of(active[step - 1]))
            found, centres = search(step, sums, centres, packed)
            alphas.append(found[1][0])
        lam, centres = update(ITERS - 1, lam, found, centres, low_of(active[ITERS - 1]))
        return lam, jnp.stack(alphas), centres

    def again(found):
        found, _ = search(0, None, None, False)
        return rest(False, found)

    return lax.cond(first[1][1, 0] <= 0, functools.partial(rest, True), again, first)


def solution(mesh):
    return jax.shard_map(
        body,
        mesh=mesh,
        in_specs=(
            P(("wide", "eight"), None, None),
            P(("wide", "eight"), None, None),
            P(("wide", "eight"), None, None),
            P(("wide", "eight"), None, None),
            P(("wide", "eight"), None),
            P(("wide", "eight")),
            P(None, ("wide", "eight"), None),
        ),
        out_specs=(P(("wide", "eight"), None, None), P(), P()),
        check_vma=False,
    )
```

```python
import functools

import jax
import jax.numpy as jnp
from jax import lax
from jax.experimental import pallas as pl
from jax.experimental.pallas import tpu as pltpu
from jax.sharding import PartitionSpec as P


ITERS = 3
EXTRA = 16
F32 = jnp.float32
BF16 = jnp.bfloat16
VMEM = pl.BlockSpec(memory_space=pltpu.VMEM)
HBM = pl.BlockSpec(memory_space=pltpu.HBM)
SMEM = pl.BlockSpec(memory_space=pltpu.SMEM)


def call(kernel, outs, n_smem, ins, flops, nbytes, scratch=(), vmem=16, hbm_ins=(), hbm_outs=(), aliases=None):
    return pl.pallas_call(
        kernel,
        out_shape=outs,
        in_specs=[
            SMEM if i < n_smem else HBM if i in hbm_ins else VMEM for i in range(len(ins))
        ],
        out_specs=[HBM if i in hbm_outs else VMEM for i in range(len(outs))],
        scratch_shapes=list(scratch),
        input_output_aliases=aliases or {},
        compiler_params=pltpu.CompilerParams(vmem_limit_bytes=vmem << 20),
        cost_estimate=pl.CostEstimate(flops=flops, bytes_accessed=nbytes, transcendentals=0),
    )(*ins)


def sds(shape, dtype):
    return jax.ShapeDtypeStruct(shape, dtype)


def stage_bits(size):
    total = size.bit_length() - 1
    groups = [1]
    left = total - 1
    while left > 0:
        take = 2 if left >= 2 else 1
        groups.append(take)
        left -= take
    return groups


def pack_products(inner, square, most):
    shape = (EXTRA, inner.shape[1])
    row = lax.broadcasted_iota(jnp.int32, shape, 0)
    ih = inner.astype(BF16).astype(F32)
    sh = square.astype(BF16).astype(F32)
    tile = jnp.zeros(shape, F32)
    for i, value in enumerate((ih, inner - ih, sh, square - sh, most)):
        tile = jnp.where(row == i, jnp.broadcast_to(value, shape), tile)
    return tile.astype(BF16)


def unpack_products(tiles):
    vals = []
    for tile in tiles:
        t = tile.astype(F32)
        vals.append((t[0:1] + t[1:2], t[2:3] + t[3:4], t[4:5]))
    return (
        tree([v[0] for v in vals]),
        tree([v[1] for v in vals]),
        functools.reduce(jnp.maximum, [v[2] for v in vals]),
    )


def tree(items):
    items = list(items)
    while len(items) > 1:
        items = [items[i] + items[i + 1] for i in range(0, len(items), 2)]
    return items[0]


def send_partial(chunk, wide, w, part, tile, keep_ref, send_ref):
    for k in range(wide):
        total = part(pl.ds(pl.multiple_of(jnp.bitwise_xor(w, k) * chunk, chunk), chunk))
        out = send_ref if k % 2 else keep_ref
        out[pl.ds((k // 2) * chunk, chunk), :] = total.astype(BF16)
    if tile is not None:
        tail = pl.ds((wide // 2) * chunk, EXTRA)
        keep_ref[tail, :] = tile
        send_ref[tail, :] = tile


def pack_blocks(table, row, face, source, disp_ref, outs, count):
    blocks = table.shape[1]
    height = disp_ref.shape[1] // blocks

    def block(b, n):
        need = table[row, b] == face
        rows = pl.ds(pl.multiple_of(b * height, height), height)
        low = 0
        for out_ref in outs:
            high = low + out_ref.shape[0]

            @pl.when(need & (n >= low) & (n < high))
            def _(out_ref=out_ref, low=low):
                out_ref[n - low] = disp_ref[source, rows, :]

            low = high
        return n + need.astype(jnp.int32)

    return lax.fori_loop(0, blocks, block, count, unroll=True)


def send_halo(info, disp_ref, outs, tables):
    last = disp_ref.shape[0] - 1
    odd = jnp.bitwise_and(info[0], 1)
    zodd = jnp.bitwise_and(info[1], 1)
    za_ref, zb_ref = outs[:2]
    zero = jnp.int32(0)
    if not tables:
        za_ref[...] = disp_ref[(1 - zodd) * last]
        zb_ref[...] = disp_ref[zodd * last]
        return
    theirs, ta, tb = tables
    count = zero
    for s in range(last + 1):
        count = pack_blocks(theirs, s, odd, s, disp_ref, outs[2:], count)
    pack_blocks(ta, zodd * last, 3 - zodd, (1 - zodd) * last, disp_ref, [za_ref], zero)
    pack_blocks(tb, (1 - zodd) * last, 2 + zodd, zodd * last, disp_ref, [zb_ref], zero)


def open_kernel(chunk, wide, info, lam_ref, flex_ref, keep_ref, send_ref, disp_ref, flex, half, sems):
    subs = lam_ref.shape[0]

    def fetch(s):
        return pltpu.make_async_copy(flex_ref.at[s], flex.at[s], sems.at[s])

    for s in range(subs):
        fetch(s).start()
    half[...] = lam_ref[...].astype(BF16)
    send_partial(
        chunk, wide, info[0], lambda rows: tree([lam_ref[s, rows, :] for s in range(subs)]),
        None, keep_ref, send_ref,
    )

    def product(s, carry):
        fetch(s).wait()
        disp_ref[s] = jnp.dot(flex[s], half[s], preferred_element_type=F32).astype(BF16)
        return carry

    lax.fori_loop(0, subs, product, 0)


def halo_kernel(packed, info, *refs):
    tables, (disp_ref, *outs) = refs[: 3 * packed], refs[3 * packed :]
    send_halo(info, disp_ref, outs, tables)


def flex_kernel(step, packed, info, *refs):
    tables, refs = refs[: 3 * packed], refs[3 * packed :]
    half_ref, flex_ref, mean_ref, *refs = refs
    if step > 1:
        refs = refs[1:]
    disp_ref, *outs, stack_ref, sem = refs
    copy = pltpu.make_async_copy(mean_ref, stack_ref.at[step - 1], sem)
    copy.start()

    def product(s, carry):
        disp_ref[s] = jnp.dot(
            flex_ref[s], half_ref[s], preferred_element_type=F32
        ).astype(BF16)
        return carry

    lax.fori_loop(0, half_ref.shape[0], product, 0)
    send_halo(info, disp_ref, outs, tables)
    copy.wait()


def update_kernel(chunk, wide, step, last, info, lam_ref, dir_ref, alpha_ref, floor_ref, *refs):
    centre_refs = refs[:wide]
    refs = refs[wide:]
    if last:
        _, lam_out, stack_ref, new_ref, mean_ref, sems = refs
    else:
        new_ref, mean_ref, half_ref, keep_ref, send_ref = refs
    w = info[0]
    subs, _, cols = lam_ref.shape
    alpha = jnp.broadcast_to(alpha_ref[0:1, :], (chunk, cols))
    copies = []

    def send(src, dst):
        copies.append(pltpu.make_async_copy(src, dst, sems.at[len(copies)]))
        copies[-1].start()

    for k in range(wide):
        rows = pl.ds(pl.multiple_of(jnp.bitwise_xor(w, k) * chunk, chunk), chunk)
        centre = centre_refs[k][...].astype(F32)
        mean_ref[rows, :] = centre
        total = None
        for s in range(subs):
            trial = lam_ref[s, rows, :] + alpha * dir_ref[s, rows, :].astype(F32)
            low = floor_ref[s, rows, :]
            low = jnp.concatenate([low] * (cols // low.shape[1]), axis=1)
            new = jnp.maximum(trial - centre, low)
            new_ref[s, rows, :] = new
            if last:
                send(new_ref.at[s, rows, :], lam_out.at[s, rows, :])
            else:
                half_ref[s, rows, :] = new.astype(BF16)
                total = new if total is None else total + new
        if last:
            send(mean_ref.at[rows, :], stack_ref.at[step, rows, :])
        else:
            out = send_ref if k % 2 else keep_ref
            out[pl.ds((k // 2) * chunk, chunk), :] = total.astype(BF16)
    for copy in copies:
        copy.wait()


def direct_kernel(chunk, wide, eight, caps, packed, info, side, powers, gap_ref, disp_ref, chip_ref, za_ref, zb_ref, *refs):
    offs, refs = refs[: 1 + packed], refs[1 + packed :]
    diri_ref, _, dir_ref, keep_ref, send_ref, jump, work = refs
    w, z = info[0], info[1]
    odd = jnp.bitwise_and(w, 1)
    zodd = jnp.bitwise_and(z, 1)
    subs, rows_all, cols = gap_ref.shape
    blocks = side.shape[1]
    height = rows_all // blocks
    counts = (jnp.int32(0),) * 3
    for s in range(subs):

        def block(b, ns, s=s):
            n, above, below = ns
            face = side[s, b]
            rows = pl.ds(pl.multiple_of(b * height, height), height)

            def put(source):
                value = gap_ref[s, rows, :] - (
                    disp_ref[s, rows, :].astype(F32) - source.astype(F32)
                )
                jump[s, rows, :] = value
                work[s, rows, :] = value.astype(BF16)

            def take(ref, slot):
                if packed:
                    return ref[jnp.minimum(slot, ref.shape[0] - 1)]
                return ref[s, rows, :] if len(ref.shape) == 3 else ref[rows, :]

            away = face == 1 - odd
            size = offs[0].shape[0] if packed else subs * blocks
            up = (face == 2).astype(jnp.int32)
            down = (face == 3).astype(jnp.int32)

            @pl.when(face < 2)
            def _():
                pl.when(face == odd)(lambda: put(chip_ref[s, rows, :]))
                pl.when(away & (n < size))(lambda: put(take(offs[0], n)))
                if packed:
                    pl.when(away & (n >= size))(lambda: put(take(offs[1], n - size)))

            @pl.when(face == 2)
            def _():
                if s + 1 < subs:
                    put(disp_ref[s + 1, rows, :])
                else:
                    pl.when(zodd == 0)(lambda: put(take(za_ref, above)))
                    pl.when(zodd == 1)(lambda: put(take(zb_ref, above)))

            @pl.when(face == 3)
            def _():
                if s > 0:
                    put(disp_ref[s - 1, rows, :])
                else:
                    pl.when(zodd == 1)(lambda: put(take(za_ref, below)))
                    pl.when(zodd == 0)(lambda: put(take(zb_ref, below)))

            n = n + away.astype(jnp.int32)
            if s + 1 == subs:
                above = above + up
            if s == 0:
                below = below + down
            return n, above, below

        counts = lax.fori_loop(0, blocks, block, counts)

    def apply(s, sums):
        def level(i, carry):
            work[s] = jnp.dot(
                diri_ref[s], work[s], preferred_element_type=F32
            ).astype(BF16)
            return carry

        lax.fori_loop(0, powers[s], level, 0)
        direct = work[s]
        dir_ref[s] = direct
        dfloat = direct.astype(F32)
        split = (rows_all // 8, 8, cols)
        return (
            sums[0] + jnp.sum((jump[s] * dfloat).reshape(split), axis=0),
            sums[1] + jnp.sum((dfloat * dfloat).reshape(split), axis=0),
        )

    zeros = jnp.zeros((8, cols), F32)
    inner, square = lax.fori_loop(0, subs, apply, (zeros, zeros))
    n, above, below = counts
    excess = jnp.maximum(
        n - caps[0],
        jnp.maximum(
            jnp.where(z < eight - 1, above, 0) - caps[1], jnp.where(z > 0, below, 0) - caps[1]
        ),
    )
    tile = pack_products(
        jnp.sum(inner, axis=0, keepdims=True),
        jnp.sum(square, axis=0, keepdims=True),
        jnp.broadcast_to(excess.astype(F32), (1, cols)),
    )
    send_partial(
        chunk, wide, w, lambda rows: tree([work[s, rows, :].astype(F32) for s in range(subs)]),
        tile, keep_ref, send_ref,
    )


def add_kernel(chunk, chunks, ways_in, ways_out, extra, *refs):
    ins, outs = refs[:ways_in], refs[-ways_out:]
    for c in range(chunks):
        rows = pl.ds(c * chunk, chunk)
        total = tree([r[rows, :].astype(F32) for r in ins]).astype(BF16)
        outs[c % ways_out][pl.ds((c // ways_out) * chunk, chunk), :] = total
    if extra:
        tail = pl.ds(chunks * chunk, EXTRA)
        tiles = [r[tail, :] for r in ins]
        tile = pack_products(*unpack_products(tiles))
        for o in outs:
            o[pl.ds((chunks // ways_out) * chunk, EXTRA), :] = tile


def centre_kernel(chunk, ways, count, *refs):
    dirs, lams = refs[:ways], refs[ways:-2]
    centre_ref, alpha_ref = refs[-2:]
    rows = pl.ds(0, chunk)
    tail = pl.ds(chunk, EXTRA)
    inner, square, most = unpack_products([r[tail, :] for r in dirs])
    alpha = inner / (square + 1e-06)
    row = lax.broadcasted_iota(jnp.int32, alpha_ref.shape, 0)
    alpha_ref[...] = jnp.where(
        row == 0, jnp.broadcast_to(alpha, row.shape), jnp.broadcast_to(most, row.shape)
    )
    dsum = tree([r[rows, :].astype(F32) for r in dirs])
    lsum = tree([r[rows, :].astype(F32) for r in lams])
    centre_ref[...] = ((lsum + alpha * dsum) / count).astype(BF16)


def swap(x, axis, mask):
    n = lax.axis_size(axis)
    return lax.ppermute(x, axis, [(i, i ^ mask) for i in range(n)])


def stage(parts, g, chunk, wide, extra):
    groups = stage_bits(wide)
    shift = sum(groups[:g])
    ways = 1 << groups[g]
    chunks = wide >> (shift + groups[g])
    cols = parts[0].shape[1]
    got = [parts[0]] + [swap(parts[q], "wide", q << shift) for q in range(1, ways)]
    nxt = 1 << groups[g + 1] if g + 1 < len(groups) else 1
    shape = sds(((chunks // nxt) * chunk + (EXTRA if extra else 0), cols), BF16)
    return call(
        functools.partial(add_kernel, chunk, chunks, ways, nxt, extra),
        [shape] * nxt, 0, got, chunks * chunk * cols * ways,
        chunks * chunk * cols * 2 * (ways + 1), vmem=8,
    )


def scatter(parts, first, chunk, wide, extra):
    for g in range(first, len(stage_bits(wide))):
        parts = stage(parts, g, chunk, wide, extra)
    return parts[0]


def across(x):
    size = lax.axis_size("eight")
    return [x] + [swap(x, "eight", q) for q in range(1, size)]


def gather(centre, wide):
    groups = stage_bits(wide)
    have = {0: centre}
    shift = wide.bit_length() - 1
    for bits in reversed(groups):
        shift -= bits
        new = dict(have)
        for q in range(1, 1 << bits):
            for k, v in have.items():
                new[k ^ (q << shift)] = swap(v, "wide", q << shift)
        have = new
    return [have[k] for k in range(wide)]


def body(multipliers, gap, flexibility, dirichlet, side, powers, active):
    subs, rows, cols = multipliers.shape
    blocks = side.shape[1]
    wide = lax.axis_size("wide")
    eight = lax.axis_size("eight")
    count = wide * eight * subs
    chunk = rows // wide
    caps = (-(-subs * blocks * 5 // 8), -(-blocks * 3 // 4))
    away = [(i, (i + 1) % wide if i % 2 else (i - 1) % wide) for i in range(wide)]
    pairs_a = [(i, i ^ 1) for i in range(eight) if i ^ 1 < eight]
    pairs_b = [(i, i + 1 if i % 2 else i - 1) for i in range(1, eight - 1 + eight % 2)]
    info = jnp.stack([lax.axis_index("wide"), lax.axis_index("eight")]).astype(jnp.int32)
    tables = [
        lax.ppermute(side, "wide", away),
        lax.ppermute(side, "eight", pairs_a),
        lax.ppermute(side, "eight", pairs_b),
    ]

    def low_of(flags):
        wide_flags = jnp.broadcast_to(flags[..., None], flags.shape + (128,))
        return jnp.where(wide_flags == 1, 0.0, -jnp.inf).astype(F32)

    full = sds((subs, rows, cols), F32)
    half = sds((subs, rows, cols), BF16)
    one = sds((rows, cols), BF16)
    few = [sds((cap, rows // blocks, cols), BF16) for cap in (caps[1], caps[1], -(-caps[0] // 2), caps[0] // 2)]
    part = sds(((wide // 2) * chunk, cols), BF16)
    message = sds(((wide // 2) * chunk + EXTRA, cols), BF16)
    stack = sds((ITERS, rows, cols), F32)
    mm = 2 * subs * rows * rows * cols
    op_bytes = 2 * subs * rows * rows
    arr = subs * rows * cols

    def search(step, sums, centres, packed):
        head = [info] + (tables if packed else [])
        outs = few if packed else [one, one]
        if step:
            mean, half_lam, lkeep, lsend = sums
            ins = head + [half_lam, flexibility, mean] + ([centres] if step > 1 else [])
            *sends, centres = call(
                functools.partial(flex_kernel, step, packed), [half, *outs, stack], len(head), ins,
                mm, op_bytes + arr * 6, scratch=[pltpu.SemaphoreType.DMA],
                hbm_ins=(len(head) + 3,), hbm_outs=(len(outs) + 1,),
                aliases={len(head) + 3: len(outs) + 1} if step > 1 else None,
            )
        else:
            lkeep, lsend, disp = call(
                functools.partial(open_kernel, chunk, wide), [part, part, half], 1,
                [info, multipliers, flexibility], mm, op_bytes + arr * 6,
                scratch=[
                    pltpu.VMEM((subs, rows, rows), BF16),
                    pltpu.VMEM((subs, rows, cols), BF16),
                    pltpu.SemaphoreType.DMA((subs,)),
                ],
                hbm_ins=(2,),
            )
            sends = [disp, *call(
                functools.partial(halo_kernel, packed), outs, len(head), head + [disp],
                arr, arr * 4, vmem=8,
            )]
        lams = stage([lkeep, lsend], 0, chunk, wide, False)
        lams, sends = lax.optimization_barrier((lams, sends))
        disp, za, zb = sends[:3]
        offs = sends[3:] if packed else [disp]
        if packed:
            offs[0] = lax.ppermute(offs[0], "wide", away)
        own = scatter(lams, 1, chunk, wide, False)
        offs[-1] = lax.ppermute(offs[-1], "wide", away)
        za = lax.ppermute(za, "eight", pairs_a)
        zb = lax.ppermute(zb, "eight", pairs_b)
        chip = swap(disp, "wide", 1)
        lam_parts = [own] + ([swap(own, "eight", 1)] if eight > 1 else [])
        direct, dkeep, dsend = call(
            functools.partial(direct_kernel, chunk, wide, eight, caps, packed),
            [half, message, message], 3,
            [info, side, powers, gap, disp, chip, za, zb, *offs, dirichlet, own],
            2 * mm, op_bytes + arr * 16,
            scratch=[
                pltpu.VMEM((subs, rows, cols), F32),
                pltpu.VMEM((subs, rows, cols), BF16),
            ],
        )
        dirs = stage([dkeep, dsend], 0, chunk, wide, True)
        for q in range(1, eight.bit_length() - 1):
            (own,) = call(
                functools.partial(add_kernel, chunk, 1, 2, 1, False), [sds(own.shape, BF16)], 0,
                [*lam_parts, dkeep], 2 * own.size, 6 * own.size, vmem=8,
            )
            lam_parts = [own, swap(own, "eight", 1 << q)]
        dirs = scatter(dirs, 1, chunk, wide, True)
        dir_parts = across(dirs)
        centre, alpha = call(
            functools.partial(centre_kernel, chunk, eight, float(count)),
            [sds((chunk, cols), BF16), sds((8, cols), F32)], 0, dir_parts + lam_parts,
            chunk * cols * 10, chunk * cols * 20, vmem=8,
        )
        return (direct, alpha, gather(centre, wide)), centres

    def update(step, lam, found, centres, low):
        direct, alpha, pieces = found
        ins = [info, lam, direct, alpha, low, *pieces]
        kernel = functools.partial(update_kernel, chunk, wide, step, step == ITERS - 1)
        if step < ITERS - 1:
            outs = [full, sds((rows, cols), F32), half, part, part]
            return call(kernel, outs, 1, ins, arr * 6, arr * 16)
        return call(
            kernel, [full, stack], 1, ins + [centres], arr * 6, arr * 16,
            scratch=[
                pltpu.VMEM((subs, rows, cols), F32),
                pltpu.VMEM((rows, cols), F32),
                pltpu.SemaphoreType.DMA((wide * (subs + 1),)),
            ],
            hbm_ins=(len(ins),), hbm_outs=(0, 1), aliases={len(ins): 1},
        )

    first, _ = search(0, None, None, True)

    def rest(packed, found):
        alphas = [found[1][0]]
        lam, centres = multipliers, None
        for step in range(1, ITERS):
            lam, *sums = update(step - 1, lam, found, centres, low_of(active[step - 1]))
            found, centres = search(step, sums, centres, packed)
            alphas.append(found[1][0])
        lam, centres = update(ITERS - 1, lam, found, centres, low_of(active[ITERS - 1]))
        return lam, jnp.stack(alphas), centres

    def again(found):
        found, _ = search(0, None, None, False)
        return rest(False, found)

    return lax.cond(first[1][1, 0] <= 0, functools.partial(rest, True), again, first)


def solution(mesh):
    return jax.shard_map(
        body,
        mesh=mesh,
        in_specs=(
            P(("wide", "eight"), None, None),
            P(("wide", "eight"), None, None),
            P(("wide", "eight"), None, None),
            P(("wide", "eight"), None, None),
            P(("wide", "eight"), None),
            P(("wide", "eight")),
            P(None, ("wide", "eight"), None),
        ),
        out_specs=(P(("wide", "eight"), None, None), P(), P()),
        check_vma=False,
    )
```

```python
import functools

import jax
import jax.numpy as jnp
from jax import lax
from jax.experimental import pallas as pl
from jax.experimental.pallas import tpu as pltpu
from jax.sharding import PartitionSpec as P


ITERS = 3
EXTRA = 16
F32 = jnp.float32
BF16 = jnp.bfloat16
VMEM = pl.BlockSpec(memory_space=pltpu.VMEM)
HBM = pl.BlockSpec(memory_space=pltpu.HBM)
SMEM = pl.BlockSpec(memory_space=pltpu.SMEM)


def call(kernel, outs, n_smem, ins, flops, nbytes, scratch=(), vmem=16, hbm_ins=(), hbm_outs=(), aliases=None):
    return pl.pallas_call(
        kernel,
        out_shape=outs,
        in_specs=[
            SMEM if i < n_smem else HBM if i in hbm_ins else VMEM for i in range(len(ins))
        ],
        out_specs=[HBM if i in hbm_outs else VMEM for i in range(len(outs))],
        scratch_shapes=list(scratch),
        input_output_aliases=aliases or {},
        compiler_params=pltpu.CompilerParams(vmem_limit_bytes=vmem << 20),
        cost_estimate=pl.CostEstimate(flops=flops, bytes_accessed=nbytes, transcendentals=0),
    )(*ins)


def sds(shape, dtype):
    return jax.ShapeDtypeStruct(shape, dtype)


def paired_stages(size):
    total = size.bit_length() - 1
    stages, shift = [(0, 1)], 1
    while shift < total:
        stages.append((shift, min(2, total - shift)))
        shift += stages[-1][1]
    return stages


def single_stages(size):
    return [(0, 1)] + [(shift, 1) for shift in range(size.bit_length() - 2, 0, -1)]


def pack_products(inner, square, most):
    shape = (EXTRA, inner.shape[1])
    row = lax.broadcasted_iota(jnp.int32, shape, 0)
    ih = inner.astype(BF16).astype(F32)
    sh = square.astype(BF16).astype(F32)
    tile = jnp.zeros(shape, F32)
    for i, value in enumerate((ih, inner - ih, sh, square - sh, most)):
        tile = jnp.where(row == i, jnp.broadcast_to(value, shape), tile)
    return tile.astype(BF16)


def unpack_products(tiles):
    vals = []
    for tile in tiles:
        t = tile.astype(F32)
        vals.append((t[0:1] + t[1:2], t[2:3] + t[3:4], t[4:5]))
    return (
        tree([v[0] for v in vals]),
        tree([v[1] for v in vals]),
        functools.reduce(jnp.maximum, [v[2] for v in vals]),
    )


def tree(items):
    items = list(items)
    while len(items) > 1:
        items = [items[i] + items[i + 1] for i in range(0, len(items), 2)]
    return items[0]


def send_partial(chunk, wide, w, part, tile, keep_ref, send_ref):
    for k in range(wide):
        total = part(pl.ds(pl.multiple_of(jnp.bitwise_xor(w, k) * chunk, chunk), chunk))
        out = send_ref if k % 2 else keep_ref
        out[pl.ds((k // 2) * chunk, chunk), :] = total.astype(BF16)
    if tile is not None:
        tail = pl.ds((wide // 2) * chunk, EXTRA)
        keep_ref[tail, :] = tile
        send_ref[tail, :] = tile


def pack_blocks(table, row, face, source, disp_ref, outs, count):
    blocks = table.shape[1]
    height = disp_ref.shape[1] // blocks

    def block(b, n):
        need = table[row, b] == face
        rows = pl.ds(pl.multiple_of(b * height, height), height)
        low = 0
        for out_ref in outs:
            high = low + out_ref.shape[0]

            @pl.when(need & (n >= low) & (n < high))
            def _(out_ref=out_ref, low=low):
                out_ref[n - low] = disp_ref[source, rows, :]

            low = high
        return n + need.astype(jnp.int32)

    return lax.fori_loop(0, blocks, block, count, unroll=True)


def send_halo(info, disp_ref, outs, tables):
    last = disp_ref.shape[0] - 1
    odd = jnp.bitwise_and(info[0], 1)
    zodd = jnp.bitwise_and(info[1], 1)
    za_ref, zb_ref = outs[:2]
    zero = jnp.int32(0)
    if not tables:
        za_ref[...] = disp_ref[(1 - zodd) * last]
        zb_ref[...] = disp_ref[zodd * last]
        return
    theirs, ta, tb = tables
    count = zero
    for s in range(last + 1):
        count = pack_blocks(theirs, s, odd, s, disp_ref, outs[2:], count)
    pack_blocks(ta, zodd * last, 3 - zodd, (1 - zodd) * last, disp_ref, [za_ref], zero)
    pack_blocks(tb, (1 - zodd) * last, 2 + zodd, zodd * last, disp_ref, [zb_ref], zero)


def open_kernel(chunk, wide, info, lam_ref, flex_ref, keep_ref, send_ref, disp_ref, flex, half, sems):
    subs = lam_ref.shape[0]

    def fetch(s):
        return pltpu.make_async_copy(flex_ref.at[s], flex.at[s], sems.at[s])

    for s in range(subs):
        fetch(s).start()
    half[...] = lam_ref[...].astype(BF16)
    send_partial(
        chunk, wide, info[0], lambda rows: tree([lam_ref[s, rows, :] for s in range(subs)]),
        None, keep_ref, send_ref,
    )

    def product(s, carry):
        fetch(s).wait()
        disp_ref[s] = jnp.dot(flex[s], half[s], preferred_element_type=F32).astype(BF16)
        return carry

    lax.fori_loop(0, subs, product, 0)


def halo_kernel(packed, info, *refs):
    tables, (disp_ref, *outs) = refs[: 3 * packed], refs[3 * packed :]
    send_halo(info, disp_ref, outs, tables)


def flex_kernel(step, packed, info, *refs):
    tables, refs = refs[: 3 * packed], refs[3 * packed :]
    half_ref, flex_ref, mean_ref, *refs = refs
    if step > 1:
        refs = refs[1:]
    disp_ref, *outs, stack_ref, sem = refs
    copy = pltpu.make_async_copy(mean_ref, stack_ref.at[step - 1], sem)
    copy.start()

    def product(s, carry):
        disp_ref[s] = jnp.dot(
            flex_ref[s], half_ref[s], preferred_element_type=F32
        ).astype(BF16)
        return carry

    lax.fori_loop(0, half_ref.shape[0], product, 0)
    send_halo(info, disp_ref, outs, tables)
    copy.wait()


def update_kernel(chunk, wide, step, last, info, lam_ref, dir_ref, alpha_ref, floor_ref, *refs):
    centre_refs = refs[:wide]
    refs = refs[wide:]
    if last:
        _, lam_out, stack_ref, new_ref, mean_ref, sems = refs
    else:
        new_ref, mean_ref, half_ref, keep_ref, send_ref = refs
    w = info[0]
    subs, _, cols = lam_ref.shape
    alpha = jnp.broadcast_to(alpha_ref[0:1, :], (chunk, cols))
    copies = []

    def send(src, dst):
        copies.append(pltpu.make_async_copy(src, dst, sems.at[len(copies)]))
        copies[-1].start()

    for k in range(wide):
        rows = pl.ds(pl.multiple_of(jnp.bitwise_xor(w, k) * chunk, chunk), chunk)
        centre = centre_refs[k][...].astype(F32)
        mean_ref[rows, :] = centre
        total = None
        for s in range(subs):
            trial = lam_ref[s, rows, :] + alpha * dir_ref[s, rows, :].astype(F32)
            low = floor_ref[s, rows, :]
            low = jnp.concatenate([low] * (cols // low.shape[1]), axis=1)
            new = jnp.maximum(trial - centre, low)
            new_ref[s, rows, :] = new
            if last:
                send(new_ref.at[s, rows, :], lam_out.at[s, rows, :])
            else:
                half_ref[s, rows, :] = new.astype(BF16)
                total = new if total is None else total + new
        if last:
            send(mean_ref.at[rows, :], stack_ref.at[step, rows, :])
        else:
            out = send_ref if k % 2 else keep_ref
            out[pl.ds((k // 2) * chunk, chunk), :] = total.astype(BF16)
    for copy in copies:
        copy.wait()


def direct_kernel(chunk, wide, eight, caps, packed, info, side, powers, gap_ref, disp_ref, chip_ref, za_ref, zb_ref, *refs):
    offs, refs = refs[: 1 + packed], refs[1 + packed :]
    diri_ref, _, dir_ref, keep_ref, send_ref, jump, work = refs
    w, z = info[0], info[1]
    odd = jnp.bitwise_and(w, 1)
    zodd = jnp.bitwise_and(z, 1)
    subs, rows_all, cols = gap_ref.shape
    blocks = side.shape[1]
    height = rows_all // blocks
    counts = (jnp.int32(0),) * 3
    for s in range(subs):

        def block(b, ns, s=s):
            n, above, below = ns
            face = side[s, b]
            rows = pl.ds(pl.multiple_of(b * height, height), height)

            def put(source):
                value = gap_ref[s, rows, :] - (
                    disp_ref[s, rows, :].astype(F32) - source.astype(F32)
                )
                jump[s, rows, :] = value
                work[s, rows, :] = value.astype(BF16)

            def take(ref, slot):
                if packed:
                    return ref[jnp.minimum(slot, ref.shape[0] - 1)]
                return ref[s, rows, :] if len(ref.shape) == 3 else ref[rows, :]

            away = face == 1 - odd
            size = offs[0].shape[0] if packed else subs * blocks
            up = (face == 2).astype(jnp.int32)
            down = (face == 3).astype(jnp.int32)

            pl.when(face == odd)(lambda: put(chip_ref[s, rows, :]))
            pl.when(away & (n < size))(lambda: put(take(offs[0], n)))
            if packed:
                pl.when(away & (n >= size))(lambda: put(take(offs[1], n - size)))
            if s + 1 < subs:
                pl.when(face == 2)(lambda: put(disp_ref[s + 1, rows, :]))
            else:
                pl.when((face == 2) & (zodd == 0))(lambda: put(take(za_ref, above)))
                pl.when((face == 2) & (zodd == 1))(lambda: put(take(zb_ref, above)))
            if s > 0:
                pl.when(face == 3)(lambda: put(disp_ref[s - 1, rows, :]))
            else:
                pl.when((face == 3) & (zodd == 1))(lambda: put(take(za_ref, below)))
                pl.when((face == 3) & (zodd == 0))(lambda: put(take(zb_ref, below)))
            n = n + away.astype(jnp.int32)
            if s + 1 == subs:
                above = above + up
            if s == 0:
                below = below + down
            return n, above, below

        counts = lax.fori_loop(0, blocks, block, counts)

    def apply(s, sums):
        def level(i, carry):
            work[s] = jnp.dot(
                diri_ref[s], work[s], preferred_element_type=F32
            ).astype(BF16)
            return carry

        lax.fori_loop(0, powers[s], level, 0)
        direct = work[s]
        dir_ref[s] = direct
        dfloat = direct.astype(F32)
        split = (rows_all // 8, 8, cols)
        return (
            sums[0] + jnp.sum((jump[s] * dfloat).reshape(split), axis=0),
            sums[1] + jnp.sum((dfloat * dfloat).reshape(split), axis=0),
        )

    zeros = jnp.zeros((8, cols), F32)
    inner, square = lax.fori_loop(0, subs, apply, (zeros, zeros))
    n, above, below = counts
    excess = jnp.maximum(
        n - caps[0],
        jnp.maximum(
            jnp.where(z < eight - 1, above, 0) - caps[1], jnp.where(z > 0, below, 0) - caps[1]
        ),
    )
    tile = pack_products(
        jnp.sum(inner, axis=0, keepdims=True),
        jnp.sum(square, axis=0, keepdims=True),
        jnp.broadcast_to(excess.astype(F32), (1, cols)),
    )
    send_partial(
        chunk, wide, w, lambda rows: tree([work[s, rows, :].astype(F32) for s in range(subs)]),
        tile, keep_ref, send_ref,
    )


def add_kernel(chunk, chunks, ways_in, ways_out, high, extra, *refs):
    ins, outs = refs[:ways_in], refs[-ways_out:]
    for c in range(chunks):
        rows = pl.ds(c * chunk, chunk)
        total = tree([r[rows, :].astype(F32) for r in ins]).astype(BF16)
        way, spot = divmod(c, chunks // ways_out) if high else (c % ways_out, c // ways_out)
        outs[way][pl.ds(spot * chunk, chunk), :] = total
    if extra:
        tail = pl.ds(chunks * chunk, EXTRA)
        tiles = [r[tail, :] for r in ins]
        tile = pack_products(*unpack_products(tiles))
        for o in outs:
            o[pl.ds((chunks // ways_out) * chunk, EXTRA), :] = tile


def centre_kernel(chunk, ways, count, *refs):
    dirs, lams = refs[:ways], refs[ways:-2]
    centre_ref, alpha_ref = refs[-2:]
    rows = pl.ds(0, chunk)
    tail = pl.ds(chunk, EXTRA)
    inner, square, most = unpack_products([r[tail, :] for r in dirs])
    alpha = inner / (square + 1e-06)
    row = lax.broadcasted_iota(jnp.int32, alpha_ref.shape, 0)
    alpha_ref[...] = jnp.where(
        row == 0, jnp.broadcast_to(alpha, row.shape), jnp.broadcast_to(most, row.shape)
    )
    dsum = tree([r[rows, :].astype(F32) for r in dirs])
    lsum = tree([r[rows, :].astype(F32) for r in lams])
    centre_ref[...] = ((lsum + alpha * dsum) / count).astype(BF16)


def swap(x, axis, mask):
    n = lax.axis_size(axis)
    return lax.ppermute(x, axis, [(i, i ^ mask) for i in range(n)])


def stage(parts, stages, g, chunk, wide, extra):
    shift, bits = stages[g]
    ways = 1 << bits
    chunks = wide >> sum(b for _, b in stages[: g + 1])
    cols = parts[0].shape[1]
    got = [parts[0]] + [swap(parts[q], "wide", q << shift) for q in range(1, ways)]
    nxt = 1 << stages[g + 1][1] if g + 1 < len(stages) else 1
    high = g + 1 < len(stages) and 1 << stages[g + 1][0] != wide // chunks
    shape = sds(((chunks // nxt) * chunk + (EXTRA if extra else 0), cols), BF16)
    return call(
        functools.partial(add_kernel, chunk, chunks, ways, nxt, high, extra),
        [shape] * nxt, 0, got, chunks * chunk * cols * ways,
        chunks * chunk * cols * 2 * (ways + 1), vmem=8,
    )


def scatter(parts, stages, first, chunk, wide, extra):
    for g in range(first, len(stages)):
        parts = stage(parts, stages, g, chunk, wide, extra)
    return parts[0]


def across(x):
    size = lax.axis_size("eight")
    return [x] + [swap(x, "eight", q) for q in range(1, size)]


def gather(centre, wide):
    have = {0: centre}
    for shift, bits in reversed(paired_stages(wide)):
        new = dict(have)
        for q in range(1, 1 << bits):
            for k, v in have.items():
                new[k ^ (q << shift)] = swap(v, "wide", q << shift)
        have = new
    return [have[k] for k in range(wide)]


def body(multipliers, gap, flexibility, dirichlet, side, powers, active):
    subs, rows, cols = multipliers.shape
    blocks = side.shape[1]
    wide = lax.axis_size("wide")
    eight = lax.axis_size("eight")
    count = wide * eight * subs
    chunk = rows // wide
    caps = (-(-subs * blocks * 5 // 8), -(-blocks * 3 // 4))
    away = [(i, (i + 1) % wide if i % 2 else (i - 1) % wide) for i in range(wide)]
    pairs_a = [(i, i ^ 1) for i in range(eight) if i ^ 1 < eight]
    pairs_b = [(i, i + 1 if i % 2 else i - 1) for i in range(1, eight - 1 + eight % 2)]
    info = jnp.stack([lax.axis_index("wide"), lax.axis_index("eight")]).astype(jnp.int32)
    tables = [
        lax.ppermute(side, "wide", away),
        lax.ppermute(side, "eight", pairs_a),
        lax.ppermute(side, "eight", pairs_b),
    ]

    def low_of(flags):
        wide_flags = jnp.broadcast_to(flags[..., None], flags.shape + (128,))
        return jnp.where(wide_flags == 1, 0.0, -jnp.inf).astype(F32)

    full = sds((subs, rows, cols), F32)
    half = sds((subs, rows, cols), BF16)
    one = sds((rows, cols), BF16)
    few = [sds((cap, rows // blocks, cols), BF16) for cap in (caps[1], caps[1], -(-caps[0] * 3 // 5), caps[0] * 2 // 5)]
    part = sds(((wide // 2) * chunk, cols), BF16)
    message = sds(((wide // 2) * chunk + EXTRA, cols), BF16)
    stack = sds((ITERS, rows, cols), F32)
    mm = 2 * subs * rows * rows * cols
    op_bytes = 2 * subs * rows * rows
    arr = subs * rows * cols

    def search(step, sums, centres, packed):
        head = [info] + (tables if packed else [])
        outs = few if packed else [one, one]
        if step:
            mean, half_lam, lkeep, lsend = sums
            ins = head + [half_lam, flexibility, mean] + ([centres] if step > 1 else [])
            *sends, centres = call(
                functools.partial(flex_kernel, step, packed), [half, *outs, stack], len(head), ins,
                mm, op_bytes + arr * 6, scratch=[pltpu.SemaphoreType.DMA],
                hbm_ins=(len(head) + 3,), hbm_outs=(len(outs) + 1,),
                aliases={len(head) + 3: len(outs) + 1} if step > 1 else None,
            )
        else:
            lkeep, lsend, disp = call(
                functools.partial(open_kernel, chunk, wide), [part, part, half], 1,
                [info, multipliers, flexibility], mm, op_bytes + arr * 6,
                scratch=[
                    pltpu.VMEM((subs, rows, rows), BF16),
                    pltpu.VMEM((subs, rows, cols), BF16),
                    pltpu.SemaphoreType.DMA((subs,)),
                ],
                hbm_ins=(2,),
            )
            sends = [disp, *call(
                functools.partial(halo_kernel, packed), outs, len(head), head + [disp],
                arr, arr * 4, vmem=8,
            )]
        lams = stage([lkeep, lsend], single_stages(wide), 0, chunk, wide, False)
        lams, sends = lax.optimization_barrier((lams, sends))
        disp, za, zb = sends[:3]
        offs = sends[3:] if packed else [disp]
        if packed:
            offs[0] = lax.ppermute(offs[0], "wide", away)
        own = scatter(lams, single_stages(wide), 1, chunk, wide, False)
        offs[-1] = lax.ppermute(offs[-1], "wide", away)
        za = lax.ppermute(za, "eight", pairs_a)
        zb = lax.ppermute(zb, "eight", pairs_b)
        chip = swap(disp, "wide", 1)
        lam_parts = [own] + ([swap(own, "eight", 1)] if eight > 1 else [])
        direct, dkeep, dsend = call(
            functools.partial(direct_kernel, chunk, wide, eight, caps, packed),
            [half, message, message], 3,
            [info, side, powers, gap, disp, chip, za, zb, *offs, dirichlet, own],
            2 * mm, op_bytes + arr * 16,
            scratch=[
                pltpu.VMEM((subs, rows, cols), F32),
                pltpu.VMEM((subs, rows, cols), BF16),
            ],
        )
        dirs = stage([dkeep, dsend], paired_stages(wide), 0, chunk, wide, True)
        for q in range(1, eight.bit_length() - 1):
            (own,) = call(
                functools.partial(add_kernel, chunk, 1, 2, 1, False, False), [sds(own.shape, BF16)], 0,
                [*lam_parts, dkeep], 2 * own.size, 6 * own.size, vmem=8,
            )
            lam_parts = [own, swap(own, "eight", 1 << q)]
        dirs = scatter(dirs, paired_stages(wide), 1, chunk, wide, True)
        dir_parts = across(dirs)
        centre, alpha = call(
            functools.partial(centre_kernel, chunk, eight, float(count)),
            [sds((chunk, cols), BF16), sds((8, cols), F32)], 0, dir_parts + lam_parts,
            chunk * cols * 10, chunk * cols * 20, vmem=8,
        )
        return (direct, alpha, gather(centre, wide)), centres

    def update(step, lam, found, centres, low):
        direct, alpha, pieces = found
        ins = [info, lam, direct, alpha, low, *pieces]
        kernel = functools.partial(update_kernel, chunk, wide, step, step == ITERS - 1)
        if step < ITERS - 1:
            outs = [full, sds((rows, cols), F32), half, part, part]
            return call(kernel, outs, 1, ins, arr * 6, arr * 16)
        return call(
            kernel, [full, stack], 1, ins + [centres], arr * 6, arr * 16,
            scratch=[
                pltpu.VMEM((subs, rows, cols), F32),
                pltpu.VMEM((rows, cols), F32),
                pltpu.SemaphoreType.DMA((wide * (subs + 1),)),
            ],
            hbm_ins=(len(ins),), hbm_outs=(0, 1), aliases={len(ins): 1},
        )

    first, _ = search(0, None, None, True)

    def rest(packed, found):
        alphas = [found[1][0]]
        lam, centres = multipliers, None
        for step in range(1, ITERS):
            lam, *sums = update(step - 1, lam, found, centres, low_of(active[step - 1]))
            found, centres = search(step, sums, centres, packed)
            alphas.append(found[1][0])
        lam, centres = update(ITERS - 1, lam, found, centres, low_of(active[ITERS - 1]))
        return lam, jnp.stack(alphas), centres

    def again(found):
        found, _ = search(0, None, None, False)
        return rest(False, found)

    return lax.cond(first[1][1, 0] <= 0, functools.partial(rest, True), again, first)


def solution(mesh):
    return jax.shard_map(
        body,
        mesh=mesh,
        in_specs=(
            P(("wide", "eight"), None, None),
            P(("wide", "eight"), None, None),
            P(("wide", "eight"), None, None),
            P(("wide", "eight"), None, None),
            P(("wide", "eight"), None),
            P(("wide", "eight")),
            P(None, ("wide", "eight"), None),
        ),
        out_specs=(P(("wide", "eight"), None, None), P(), P()),
        check_vma=False,
    )
```

```python
import functools

import jax
import jax.numpy as jnp
from jax import lax
from jax.experimental import pallas as pl
from jax.experimental.pallas import tpu as pltpu
from jax.sharding import PartitionSpec as P


ITERS = 3
EXTRA = 16
F32 = jnp.float32
BF16 = jnp.bfloat16
VMEM = pl.BlockSpec(memory_space=pltpu.VMEM)
HBM = pl.BlockSpec(memory_space=pltpu.HBM)
SMEM = pl.BlockSpec(memory_space=pltpu.SMEM)


def call(kernel, outs, n_smem, ins, flops, nbytes, scratch=(), vmem=16, hbm_ins=(), hbm_outs=(), aliases=None):
    return pl.pallas_call(
        kernel,
        out_shape=outs,
        in_specs=[
            SMEM if i < n_smem else HBM if i in hbm_ins else VMEM for i in range(len(ins))
        ],
        out_specs=[HBM if i in hbm_outs else VMEM for i in range(len(outs))],
        scratch_shapes=list(scratch),
        input_output_aliases=aliases or {},
        compiler_params=pltpu.CompilerParams(vmem_limit_bytes=vmem << 20),
        cost_estimate=pl.CostEstimate(flops=flops, bytes_accessed=nbytes, transcendentals=0),
    )(*ins)


def sds(shape, dtype):
    return jax.ShapeDtypeStruct(shape, dtype)


def stage_bits(size):
    total = size.bit_length() - 1
    groups = [1]
    left = total - 1
    while left > 0:
        take = 2 if left >= 2 else 1
        groups.append(take)
        left -= take
    return groups


def pack_products(inner, square, most):
    shape = (EXTRA, inner.shape[1])
    row = lax.broadcasted_iota(jnp.int32, shape, 0)
    ih = inner.astype(BF16).astype(F32)
    sh = square.astype(BF16).astype(F32)
    tile = jnp.zeros(shape, F32)
    for i, value in enumerate((ih, inner - ih, sh, square - sh, most)):
        tile = jnp.where(row == i, jnp.broadcast_to(value, shape), tile)
    return tile.astype(BF16)


def unpack_products(tiles):
    vals = []
    for tile in tiles:
        t = tile.astype(F32)
        vals.append((t[0:1] + t[1:2], t[2:3] + t[3:4], t[4:5]))
    return (
        tree([v[0] for v in vals]),
        tree([v[1] for v in vals]),
        functools.reduce(jnp.maximum, [v[2] for v in vals]),
    )


def tree(items):
    items = list(items)
    while len(items) > 1:
        items = [items[i] + items[i + 1] for i in range(0, len(items), 2)]
    return items[0]


def send_partial(chunk, wide, w, part, tile, keep_ref, send_ref):
    for k in range(wide):
        total = part(pl.ds(pl.multiple_of(jnp.bitwise_xor(w, k) * chunk, chunk), chunk))
        out = send_ref if k % 2 else keep_ref
        out[pl.ds((k // 2) * chunk, chunk), :] = total.astype(BF16)
    if tile is not None:
        tail = pl.ds((wide // 2) * chunk, EXTRA)
        keep_ref[tail, :] = tile
        send_ref[tail, :] = tile


def pack_blocks(table, row, face, source, disp_ref, outs, count):
    blocks = table.shape[1]
    height = disp_ref.shape[1] // blocks

    def block(b, n):
        need = table[row, b] == face
        rows = pl.ds(pl.multiple_of(b * height, height), height)
        low = 0
        for out_ref in outs:
            high = low + out_ref.shape[0]

            @pl.when(need & (n >= low) & (n < high))
            def _(out_ref=out_ref, low=low):
                out_ref[n - low] = disp_ref[source, rows, :]

            low = high
        return n + need.astype(jnp.int32)

    return lax.fori_loop(0, blocks, block, count, unroll=True)


def send_halo(info, disp_ref, outs, tables):
    last = disp_ref.shape[0] - 1
    odd = jnp.bitwise_and(info[0], 1)
    zodd = jnp.bitwise_and(info[1], 1)
    za_ref, zb_ref = outs[:2]
    zero = jnp.int32(0)
    if not tables:
        za_ref[...] = disp_ref[(1 - zodd) * last]
        zb_ref[...] = disp_ref[zodd * last]
        return
    theirs, ta, tb = tables
    count = zero
    for s in range(last + 1):
        count = pack_blocks(theirs, s, odd, s, disp_ref, outs[2:], count)
    pack_blocks(ta, zodd * last, 3 - zodd, (1 - zodd) * last, disp_ref, [za_ref], zero)
    pack_blocks(tb, (1 - zodd) * last, 2 + zodd, zodd * last, disp_ref, [zb_ref], zero)


def open_kernel(chunk, wide, info, lam_ref, flex_ref, keep_ref, send_ref, disp_ref, flex, half, sems):
    subs = lam_ref.shape[0]

    def fetch(s):
        return pltpu.make_async_copy(flex_ref.at[s], flex.at[s], sems.at[s])

    for s in range(subs):
        fetch(s).start()
    half[...] = lam_ref[...].astype(BF16)
    send_partial(
        chunk, wide, info[0], lambda rows: tree([lam_ref[s, rows, :] for s in range(subs)]),
        None, keep_ref, send_ref,
    )

    def product(s, carry):
        fetch(s).wait()
        disp_ref[s] = jnp.dot(flex[s], half[s], preferred_element_type=F32).astype(BF16)
        return carry

    lax.fori_loop(0, subs, product, 0)


def halo_kernel(packed, info, *refs):
    tables, (disp_ref, *outs) = refs[: 3 * packed], refs[3 * packed :]
    send_halo(info, disp_ref, outs, tables)


def flex_kernel(step, packed, info, *refs):
    tables, refs = refs[: 3 * packed], refs[3 * packed :]
    half_ref, flex_ref, mean_ref, *refs = refs
    if step > 1:
        refs = refs[1:]
    disp_ref, *outs, stack_ref, sem = refs
    copy = pltpu.make_async_copy(mean_ref, stack_ref.at[step - 1], sem)
    copy.start()

    def product(s, carry):
        disp_ref[s] = jnp.dot(
            flex_ref[s], half_ref[s], preferred_element_type=F32
        ).astype(BF16)
        return carry

    lax.fori_loop(0, half_ref.shape[0], product, 0)
    send_halo(info, disp_ref, outs, tables)
    copy.wait()


def update_kernel(chunk, wide, step, last, info, lam_ref, dir_ref, alpha_ref, floor_ref, *refs):
    centre_refs = refs[:wide]
    refs = refs[wide:]
    if last:
        _, lam_out, stack_ref, new_ref, mean_ref, sems = refs
    else:
        new_ref, mean_ref, half_ref, keep_ref, send_ref = refs
    w = info[0]
    subs, _, cols = lam_ref.shape
    alpha = jnp.broadcast_to(alpha_ref[0:1, :], (chunk, cols))
    copies = []

    def send(src, dst):
        copies.append(pltpu.make_async_copy(src, dst, sems.at[len(copies)]))
        copies[-1].start()

    for k in range(wide):
        rows = pl.ds(pl.multiple_of(jnp.bitwise_xor(w, k) * chunk, chunk), chunk)
        centre = centre_refs[k][...].astype(F32)
        mean_ref[rows, :] = centre
        total = None
        for s in range(subs):
            trial = lam_ref[s, rows, :] + alpha * dir_ref[s, rows, :].astype(F32)
            low = floor_ref[s, rows, :]
            low = jnp.concatenate([low] * (cols // low.shape[1]), axis=1)
            new = jnp.maximum(trial - centre, low)
            new_ref[s, rows, :] = new
            if last:
                send(new_ref.at[s, rows, :], lam_out.at[s, rows, :])
            else:
                half_ref[s, rows, :] = new.astype(BF16)
                total = new if total is None else total + new
        if last:
            send(mean_ref.at[rows, :], stack_ref.at[step, rows, :])
        else:
            out = send_ref if k % 2 else keep_ref
            out[pl.ds((k // 2) * chunk, chunk), :] = total.astype(BF16)
    for copy in copies:
        copy.wait()


def direct_kernel(chunk, wide, eight, caps, packed, info, side, powers, gap_ref, disp_ref, chip_ref, za_ref, zb_ref, *refs):
    offs, refs = refs[: 1 + packed], refs[1 + packed :]
    diri_ref, _, dir_ref, keep_ref, send_ref, jump, work = refs
    w, z = info[0], info[1]
    odd = jnp.bitwise_and(w, 1)
    zodd = jnp.bitwise_and(z, 1)
    subs, rows_all, cols = gap_ref.shape
    blocks = side.shape[1]
    height = rows_all // blocks
    counts = (jnp.int32(0),) * 3
    for s in range(subs):

        def block(b, ns, s=s):
            n, above, below = ns
            face = side[s, b]
            rows = pl.ds(pl.multiple_of(b * height, height), height)

            def put(source):
                value = gap_ref[s, rows, :] - (
                    disp_ref[s, rows, :].astype(F32) - source.astype(F32)
                )
                jump[s, rows, :] = value
                work[s, rows, :] = value.astype(BF16)

            def take(ref, slot):
                if packed:
                    return ref[jnp.minimum(slot, ref.shape[0] - 1)]
                return ref[s, rows, :] if len(ref.shape) == 3 else ref[rows, :]

            away = face == 1 - odd
            size = offs[0].shape[0] if packed else subs * blocks
            up = (face == 2).astype(jnp.int32)
            down = (face == 3).astype(jnp.int32)

            pl.when(face == odd)(lambda: put(chip_ref[s, rows, :]))
            pl.when(away & (n < size))(lambda: put(take(offs[0], n)))
            if packed:
                pl.when(away & (n >= size))(lambda: put(take(offs[1], n - size)))
            if s + 1 < subs:
                pl.when(face == 2)(lambda: put(disp_ref[s + 1, rows, :]))
            else:
                pl.when((face == 2) & (zodd == 0))(lambda: put(take(za_ref, above)))
                pl.when((face == 2) & (zodd == 1))(lambda: put(take(zb_ref, above)))
            if s > 0:
                pl.when(face == 3)(lambda: put(disp_ref[s - 1, rows, :]))
            else:
                pl.when((face == 3) & (zodd == 1))(lambda: put(take(za_ref, below)))
                pl.when((face == 3) & (zodd == 0))(lambda: put(take(zb_ref, below)))
            n = n + away.astype(jnp.int32)
            if s + 1 == subs:
                above = above + up
            if s == 0:
                below = below + down
            return n, above, below

        counts = lax.fori_loop(0, blocks, block, counts)

    def apply(s, sums):
        def level(i, carry):
            work[s] = jnp.dot(
                diri_ref[s], work[s], preferred_element_type=F32
            ).astype(BF16)
            return carry

        lax.fori_loop(0, powers[s], level, 0)
        direct = work[s]
        dir_ref[s] = direct
        dfloat = direct.astype(F32)
        split = (rows_all // 8, 8, cols)
        return (
            sums[0] + jnp.sum((jump[s] * dfloat).reshape(split), axis=0),
            sums[1] + jnp.sum((dfloat * dfloat).reshape(split), axis=0),
        )

    zeros = jnp.zeros((8, cols), F32)
    inner, square = lax.fori_loop(0, subs, apply, (zeros, zeros))
    n, above, below = counts
    excess = jnp.maximum(
        n - caps[0],
        jnp.maximum(
            jnp.where(z < eight - 1, above, 0) - caps[1], jnp.where(z > 0, below, 0) - caps[1]
        ),
    )
    tile = pack_products(
        jnp.sum(inner, axis=0, keepdims=True),
        jnp.sum(square, axis=0, keepdims=True),
        jnp.broadcast_to(excess.astype(F32), (1, cols)),
    )
    send_partial(
        chunk, wide, w, lambda rows: tree([work[s, rows, :].astype(F32) for s in range(subs)]),
        tile, keep_ref, send_ref,
    )


def add_kernel(chunk, chunks, ways_in, ways_out, extra, *refs):
    ins, outs = refs[:ways_in], refs[-ways_out:]
    for c in range(chunks):
        rows = pl.ds(c * chunk, chunk)
        total = tree([r[rows, :].astype(F32) for r in ins]).astype(BF16)
        outs[c % ways_out][pl.ds((c // ways_out) * chunk, chunk), :] = total
    if extra:
        tail = pl.ds(chunks * chunk, EXTRA)
        tiles = [r[tail, :] for r in ins]
        tile = pack_products(*unpack_products(tiles))
        for o in outs:
            o[pl.ds((chunks // ways_out) * chunk, EXTRA), :] = tile


def centre_kernel(chunk, ways, count, *refs):
    dirs, lams = refs[:ways], refs[ways:-2]
    centre_ref, alpha_ref = refs[-2:]
    rows = pl.ds(0, chunk)
    tail = pl.ds(chunk, EXTRA)
    inner, square, most = unpack_products([r[tail, :] for r in dirs])
    alpha = inner / (square + 1e-06)
    row = lax.broadcasted_iota(jnp.int32, alpha_ref.shape, 0)
    alpha_ref[...] = jnp.where(
        row == 0, jnp.broadcast_to(alpha, row.shape), jnp.broadcast_to(most, row.shape)
    )
    dsum = tree([r[rows, :].astype(F32) for r in dirs])
    lsum = tree([r[rows, :].astype(F32) for r in lams])
    centre_ref[...] = ((lsum + alpha * dsum) / count).astype(BF16)


def swap(x, axis, mask):
    n = lax.axis_size(axis)
    return lax.ppermute(x, axis, [(i, i ^ mask) for i in range(n)])


def stage(parts, g, chunk, wide, extra):
    groups = stage_bits(wide)
    shift = sum(groups[:g])
    ways = 1 << groups[g]
    chunks = wide >> (shift + groups[g])
    cols = parts[0].shape[1]
    got = [parts[0]] + [swap(parts[q], "wide", q << shift) for q in range(1, ways)]
    nxt = 1 << groups[g + 1] if g + 1 < len(groups) else 1
    shape = sds(((chunks // nxt) * chunk + (EXTRA if extra else 0), cols), BF16)
    return call(
        functools.partial(add_kernel, chunk, chunks, ways, nxt, extra),
        [shape] * nxt, 0, got, chunks * chunk * cols * ways,
        chunks * chunk * cols * 2 * (ways + 1), vmem=8,
    )


def scatter(parts, first, chunk, wide, extra):
    for g in range(first, len(stage_bits(wide))):
        parts = stage(parts, g, chunk, wide, extra)
    return parts[0]


def across(x):
    size = lax.axis_size("eight")
    return [x] + [swap(x, "eight", q) for q in range(1, size)]


def gather(centre, wide):
    groups = stage_bits(wide)
    have = {0: centre}
    shift = wide.bit_length() - 1
    for bits in reversed(groups):
        shift -= bits
        new = dict(have)
        for q in range(1, 1 << bits):
            for k, v in have.items():
                new[k ^ (q << shift)] = swap(v, "wide", q << shift)
        have = new
    return [have[k] for k in range(wide)]


def body(multipliers, gap, flexibility, dirichlet, side, powers, active):
    subs, rows, cols = multipliers.shape
    blocks = side.shape[1]
    wide = lax.axis_size("wide")
    eight = lax.axis_size("eight")
    count = wide * eight * subs
    chunk = rows // wide
    caps = (-(-subs * blocks * 5 // 8), -(-blocks * 3 // 4))
    away = [(i, (i + 1) % wide if i % 2 else (i - 1) % wide) for i in range(wide)]
    pairs_a = [(i, i ^ 1) for i in range(eight) if i ^ 1 < eight]
    pairs_b = [(i, i + 1 if i % 2 else i - 1) for i in range(1, eight - 1 + eight % 2)]
    info = jnp.stack([lax.axis_index("wide"), lax.axis_index("eight")]).astype(jnp.int32)
    tables = [
        lax.ppermute(side, "wide", away),
        lax.ppermute(side, "eight", pairs_a),
        lax.ppermute(side, "eight", pairs_b),
    ]

    def low_of(flags):
        wide_flags = jnp.broadcast_to(flags[..., None], flags.shape + (128,))
        return jnp.where(wide_flags == 1, 0.0, -jnp.inf).astype(F32)

    full = sds((subs, rows, cols), F32)
    half = sds((subs, rows, cols), BF16)
    one = sds((rows, cols), BF16)
    few = [sds((cap, rows // blocks, cols), BF16) for cap in (caps[1], caps[1], -(-caps[0] // 2), caps[0] // 2)]
    part = sds(((wide // 2) * chunk, cols), BF16)
    message = sds(((wide // 2) * chunk + EXTRA, cols), BF16)
    stack = sds((ITERS, rows, cols), F32)
    mm = 2 * subs * rows * rows * cols
    op_bytes = 2 * subs * rows * rows
    arr = subs * rows * cols

    def search(step, sums, centres, packed):
        head = [info] + (tables if packed else [])
        outs = few if packed else [one, one]
        if step:
            mean, half_lam, lkeep, lsend = sums
            ins = head + [half_lam, flexibility, mean] + ([centres] if step > 1 else [])
            *sends, centres = call(
                functools.partial(flex_kernel, step, packed), [half, *outs, stack], len(head), ins,
                mm, op_bytes + arr * 6, scratch=[pltpu.SemaphoreType.DMA],
                hbm_ins=(len(head) + 3,), hbm_outs=(len(outs) + 1,),
                aliases={len(head) + 3: len(outs) + 1} if step > 1 else None,
            )
        else:
            lkeep, lsend, disp = call(
                functools.partial(open_kernel, chunk, wide), [part, part, half], 1,
                [info, multipliers, flexibility], mm, op_bytes + arr * 6,
                scratch=[
                    pltpu.VMEM((subs, rows, rows), BF16),
                    pltpu.VMEM((subs, rows, cols), BF16),
                    pltpu.SemaphoreType.DMA((subs,)),
                ],
                hbm_ins=(2,),
            )
            sends = [disp, *call(
                functools.partial(halo_kernel, packed), outs, len(head), head + [disp],
                arr, arr * 4, vmem=8,
            )]
        lams = stage([lkeep, lsend], 0, chunk, wide, False)
        lams, sends = lax.optimization_barrier((lams, sends))
        disp, za, zb = sends[:3]
        offs = sends[3:] if packed else [disp]
        if packed:
            offs[0] = lax.ppermute(offs[0], "wide", away)
        own = scatter(lams, 1, chunk, wide, False)
        offs[-1] = lax.ppermute(offs[-1], "wide", away)
        za = lax.ppermute(za, "eight", pairs_a)
        zb = lax.ppermute(zb, "eight", pairs_b)
        chip = swap(disp, "wide", 1)
        lam_parts = [own] + ([swap(own, "eight", 1)] if eight > 1 else [])
        direct, dkeep, dsend = call(
            functools.partial(direct_kernel, chunk, wide, eight, caps, packed),
            [half, message, message], 3,
            [info, side, powers, gap, disp, chip, za, zb, *offs, dirichlet, own],
            2 * mm, op_bytes + arr * 16,
            scratch=[
                pltpu.VMEM((subs, rows, cols), F32),
                pltpu.VMEM((subs, rows, cols), BF16),
            ],
        )
        dirs = stage([dkeep, dsend], 0, chunk, wide, True)
        for q in range(1, eight.bit_length() - 1):
            (own,) = call(
                functools.partial(add_kernel, chunk, 1, 2, 1, False), [sds(own.shape, BF16)], 0,
                [*lam_parts, dkeep], 2 * own.size, 6 * own.size, vmem=8,
            )
            lam_parts = [own, swap(own, "eight", 1 << q)]
        dirs = scatter(dirs, 1, chunk, wide, True)
        dir_parts = across(dirs)
        centre, alpha = call(
            functools.partial(centre_kernel, chunk, eight, float(count)),
            [sds((chunk, cols), BF16), sds((8, cols), F32)], 0, dir_parts + lam_parts,
            chunk * cols * 10, chunk * cols * 20, vmem=8,
        )
        return (direct, alpha, gather(centre, wide)), centres

    def update(step, lam, found, centres, low):
        direct, alpha, pieces = found
        ins = [info, lam, direct, alpha, low, *pieces]
        kernel = functools.partial(update_kernel, chunk, wide, step, step == ITERS - 1)
        if step < ITERS - 1:
            outs = [full, sds((rows, cols), F32), half, part, part]
            return call(kernel, outs, 1, ins, arr * 6, arr * 16)
        return call(
            kernel, [full, stack], 1, ins + [centres], arr * 6, arr * 16,
            scratch=[
                pltpu.VMEM((subs, rows, cols), F32),
                pltpu.VMEM((rows, cols), F32),
                pltpu.SemaphoreType.DMA((wide * (subs + 1),)),
            ],
            hbm_ins=(len(ins),), hbm_outs=(0, 1), aliases={len(ins): 1},
        )

    first, _ = search(0, None, None, True)

    def rest(packed, found):
        alphas = [found[1][0]]
        lam, centres = multipliers, None
        for step in range(1, ITERS):
            lam, *sums = update(step - 1, lam, found, centres, low_of(active[step - 1]))
            found, centres = search(step, sums, centres, packed)
            alphas.append(found[1][0])
        lam, centres = update(ITERS - 1, lam, found, centres, low_of(active[ITERS - 1]))
        return lam, jnp.stack(alphas), centres

    def again(found):
        found, _ = search(0, None, None, False)
        return rest(False, found)

    return lax.cond(first[1][1, 0] <= 0, functools.partial(rest, True), again, first)


def solution(mesh):
    return jax.shard_map(
        body,
        mesh=mesh,
        in_specs=(
            P(("wide", "eight"), None, None),
            P(("wide", "eight"), None, None),
            P(("wide", "eight"), None, None),
            P(("wide", "eight"), None, None),
            P(("wide", "eight"), None),
            P(("wide", "eight")),
            P(None, ("wide", "eight"), None),
        ),
        out_specs=(P(("wide", "eight"), None, None), P(), P()),
        check_vma=False,
    )
```
